512 devices in a mesh: clip: 4 (over x), frame: 4 (over z_hi), tile: 32 (over y, z_lo, core).
Axes of the slice: x: 4, y: 8, z: 8 (z_hi: 4, z_lo: 2; z = z_hi * 2 + z_lo), core: 2. Of those that a mesh axis runs over, the one named last changes fastest.
Arguments:
- clip_feats: bfloat16 [128, 128, 16, 256], P(('clip', 'frame'), 'tile'), parts along dimension 0, may hold values from -6 to 6
- out_grad: bfloat16 [128, 128, 16, 256], P(('clip', 'frame'), 'tile'), parts along dimension 0, may hold values from -6 to 6
- spatial_weight: bfloat16 [2304, 256], replicated, may hold values from -0.125 to 0.125
- temporal_weight: bfloat16 [2304, 256], replicated, may hold values from -0.125 to 0.125
Outputs:
- block_out: bfloat16 [128, 128, 16, 256], P(('clip', 'frame'), 'tile'), parts along dimension 0
- input_grad: bfloat16 [128, 128, 16, 256], P(('clip', 'frame'), 'tile'), parts along dimension 0
- weight_grad: float32 [9216, 256], P(('clip', 'frame', 'tile')), parts along dimension 0
The draws below stay inside these ranges and needn't reach their ends.
There are 4 independent parts, one for each index of `clip`. The reference program is written for one: setup_inputs(seed, part) draws one part's arguments, and reference() takes and returns one part's arrays. A program takes and returns all parts, laid end to end along the dimension named above; an argument that names none is the same for every part. Nothing has to cross between parts.
All inputs are finite; a program needn't handle non-finite values.
Results may differ from the reference program's by a relative error of at most 0.009.
Values may be sent and summed in bfloat16 or wider, within the bound.
A program may use at most 64 MiB of HBM per device.

```python
import math
import jax
import jax.numpy as jnp
from jax import lax

C = 256
TAP_DILATION = 2
W = 16
FRAMES = 32
HEIGHT = 128


def raised(values, stream_key, source, target, parts, factor):
    def block_of(dim):
        return (jnp.arange(values.shape[dim]) // (values.shape[dim] // parts)).reshape((-1,) + (1,) * (values.ndim - 1 - dim))

    near = jax.random.permutation(stream_key, parts)[block_of(target)]
    far = (block_of(target) + parts // 2) % parts
    return jnp.where((block_of(source) == near) | (block_of(source) == far), factor * values, values)


def shard_levels(stream_key, extent, cuts, least, top_value):
    gain = 1.0
    for axis_at, blocks in cuts:
        heights = jax.random.uniform(jax.random.fold_in(jax.random.fold_in(stream_key, 6), axis_at), (blocks,), jnp.float32, least / len(cuts), top_value / len(cuts))
        gain = gain * jnp.repeat(jnp.exp(heights), extent[axis_at] // blocks).reshape((-1,) + (1,) * (len(extent) - 1 - axis_at))
    return gain


def centred(key, shape, scale, bound, cuts=(), kind=jnp.bfloat16):
    gain = shard_levels(key, shape, cuts, -0.22, 0.18) if cuts else 1.0
    drawn = jax.random.normal(key, shape, jnp.float32) * scale * gain
    return jnp.minimum(jnp.maximum(drawn, -bound), bound).astype(kind)


def noise_with(stream_key, shape, width, limit, shards, heavy, held_as=jnp.bfloat16):
    result = width * jax.random.normal(stream_key, shape, jnp.float32)
    if shards:
        result = result * shard_levels(stream_key, shape, shards, -0.22, 0.18)
    return jnp.clip(raised(result, jax.random.fold_in(stream_key, 3), *heavy), -limit, limit).astype(held_as)


def setup_inputs(seed: int = 0, part: int = 0) -> dict:
    key_of = jax.random.split(jax.random.key(seed), 5)
    part_splits = jax.random.split(jax.random.fold_in(key_of[4], part), 5)
    return {
        "clip_feats": noise_with(part_splits[0], (FRAMES, HEIGHT, W, C), 1.0, 6.0, ((0, 4), (1, 32)), (1, 3, 32, 2.75)),
        "out_grad": centred(part_splits[1], (FRAMES, HEIGHT, W, C), 1.0, 6.0, ((0, 4), (1, 32))),
        "spatial_weight": centred(key_of[2], (9 * C, C), (9 * C) ** -0.5, 0.125),
        "temporal_weight": centred(key_of[3], (9 * C, C), (9 * C) ** -0.5, 0.125),
    }


def frame_columns(frame_feats, backward_pass):
    padded = jnp.pad(frame_feats, ((1, 1), (1, 1), (0, 0)))
    pieces = []
    for row_shift in range(3):
        for col_shift in range(3):
            row_start = 2 - row_shift if backward_pass else row_shift
            col_start = 2 - col_shift if backward_pass else col_shift
            pieces.append(padded[row_start:row_start + HEIGHT, col_start:col_start + W, :])
    return jnp.concatenate(pieces, axis=-1).reshape(HEIGHT * W, 9 * C)

def reference(clip_feats, out_grad, spatial_weight, temporal_weight):
    positions = HEIGHT * W
    spatial_back = spatial_weight.reshape(9, C, C).transpose(0, 2, 1).reshape(9 * C, C)

    def forward_frame(frame_feats):
        return jnp.dot(frame_columns(frame_feats, False), spatial_weight, preferred_element_type=jnp.float32)
    pre = lax.map(forward_frame, clip_feats)
    act = jax.nn.silu(pre).astype(jnp.bfloat16)
    temporal_reach = 4 * TAP_DILATION
    act_pad = jnp.pad(act, ((temporal_reach, temporal_reach), (0, 0), (0, 0)))
    grad_pad = jnp.pad(out_grad.reshape(FRAMES, positions, C), ((temporal_reach, temporal_reach), (0, 0), (0, 0)))
    temporal_out = jnp.zeros((FRAMES * positions, C), jnp.float32)
    act_grad = jnp.zeros((FRAMES * positions, C), jnp.float32)
    for temporal_tap_index in range(9):
        block = temporal_weight[temporal_tap_index * C:(temporal_tap_index + 1) * C]
        forward_first_frame = temporal_tap_index * TAP_DILATION
        backward_first_frame = (8 - temporal_tap_index) * TAP_DILATION
        temporal_out = temporal_out + jnp.dot(act_pad[forward_first_frame:forward_first_frame + FRAMES].reshape(-1, C), block, preferred_element_type=jnp.float32)
        act_grad = act_grad + jnp.dot(grad_pad[backward_first_frame:backward_first_frame + FRAMES].reshape(-1, C), block.T, preferred_element_type=jnp.float32)
    block_out = (clip_feats.reshape(-1, C).astype(jnp.float32) + temporal_out).astype(jnp.bfloat16).reshape(FRAMES, HEIGHT, W, C)
    act_grad = act_grad.astype(jnp.bfloat16)
    sig = jax.nn.sigmoid(pre.reshape(-1, C))
    pre_grad = (act_grad.astype(jnp.float32) * (sig * (1.0 + pre.reshape(-1, C) * (1.0 - sig)))).astype(jnp.bfloat16)
    pre_grad = pre_grad.reshape(FRAMES, HEIGHT, W, C)

    def grad_step(total, pair):
        columns = frame_columns(pair[0], False)
        term = lax.dot_general(columns, pair[1].reshape(positions, C), (((0,), (0,)), ((), ())), preferred_element_type=jnp.float32)
        return (total + term, None)
    total, _ = lax.scan(grad_step, jnp.zeros((9 * C, C), jnp.float32), (clip_feats, pre_grad))
    weight_grad = total * jnp.float32(1.0 / math.sqrt(FRAMES * HEIGHT * W))

    def back_frame(pair):
        columns = frame_columns(pair[0], True)
        local = jnp.dot(columns, spatial_back, preferred_element_type=jnp.float32)
        return (pair[1].reshape(positions, C).astype(jnp.float32) + local).astype(jnp.bfloat16).reshape(HEIGHT, W, C)
    input_grad = lax.map(back_frame, (pre_grad, out_grad))
    return (block_out, input_grad, weight_grad)
```

```python
import math

import jax
import jax.numpy as jnp
from jax import lax
from jax.sharding import PartitionSpec as P

TAP_DILATION = 2


def padded_2(block, sides, width):
    for axis, dim in sides:
        count = lax.axis_size(axis)
        forward = [(i, i + 1) for i in range(count - 1)]
        backward = [(target, source) for source, target in forward]
        low = lax.ppermute(
            lax.slice_in_dim(block, block.shape[dim] - width, None, axis=dim), axis, forward
        )
        high = lax.ppermute(lax.slice_in_dim(block, 0, width, axis=dim), axis, backward)
        block = jnp.concatenate([low, block, high], axis=dim)
    return block


def tile_columns(extended, tile_rows, width_cells, backward_pass):
    padded = jnp.pad(extended, ((0, 0), (0, 0), (1, 1), (0, 0)))
    pieces = []
    for row_shift in range(3):
        for col_shift in range(3):
            row_start = 2 - row_shift if backward_pass else row_shift
            col_start = 2 - col_shift if backward_pass else col_shift
            pieces.append(
                padded[:, row_start : row_start + tile_rows, col_start : col_start + width_cells, :]
            )
    channels = extended.shape[3]
    return jnp.concatenate(pieces, axis=-1).reshape(-1, 9 * channels)


def temporal_taps(padded_seq, weight, frame_count, backward_pass):
    pieces = []
    for temporal_tap_index in range(9):
        first_frame_index = (
            (8 - temporal_tap_index) * TAP_DILATION
            if backward_pass
            else temporal_tap_index * TAP_DILATION
        )
        pieces.append(padded_seq[first_frame_index : first_frame_index + frame_count])
    channels = padded_seq.shape[2]
    columns = jnp.concatenate(pieces, axis=-1).reshape(-1, 9 * channels)
    return jnp.dot(columns, weight, preferred_element_type=jnp.float32)


def per_device(clip_feats, out_grad, spatial_weight, temporal_weight):
    slab_frames, tile_rows, width_cells, channels = clip_feats.shape
    row_count = slab_frames * tile_rows * width_cells
    frame_devs = lax.axis_size("frame")
    tile_devs = lax.axis_size("tile")
    grad_scale = jnp.float32(
        1.0 / math.sqrt(slab_frames * frame_devs * tile_rows * tile_devs * width_cells)
    )
    spatial_back = (
        spatial_weight.reshape(9, channels, channels)
        .transpose(0, 2, 1)
        .reshape(9 * channels, channels)
    )
    temporal_back = (
        temporal_weight.reshape(9, channels, channels)
        .transpose(0, 2, 1)
        .reshape(9 * channels, channels)
    )
    feat_ext = padded_2(clip_feats, (("tile", 1),), 1)
    feat_columns = tile_columns(feat_ext, tile_rows, width_cells, False)
    pre = jnp.dot(feat_columns, spatial_weight, preferred_element_type=jnp.float32)
    act = jax.nn.silu(pre).astype(jnp.bfloat16)
    temporal_reach = 4 * TAP_DILATION
    per_group = tile_rows * width_cells // frame_devs
    grouped = (slab_frames, frame_devs, per_group, channels)
    act_part = lax.all_to_all(
        act.reshape(grouped), "frame", split_axis=1, concat_axis=0, tiled=True
    )
    grad_part = lax.all_to_all(out_grad, "frame", split_axis=1, concat_axis=0, tiled=True)
    feat_part = lax.all_to_all(clip_feats, "frame", split_axis=1, concat_axis=0, tiled=True)
    frame_count = act_part.shape[0]
    item_count = act_part.shape[2]
    act_pad = jnp.pad(
        act_part.reshape(frame_count, item_count, channels),
        ((temporal_reach, temporal_reach), (0, 0), (0, 0)),
    )
    grad_pad = jnp.pad(
        grad_part.reshape(frame_count, item_count, channels),
        ((temporal_reach, temporal_reach), (0, 0), (0, 0)),
    )
    mixed = temporal_taps(act_pad, temporal_weight, frame_count, False)
    out_part = (feat_part.reshape(-1, channels).astype(jnp.float32) + mixed).astype(jnp.bfloat16)
    back_part = temporal_taps(grad_pad, temporal_back, frame_count, True).astype(jnp.bfloat16)
    out_part = out_part.reshape(frame_count, 1, item_count, channels)
    back_part = back_part.reshape(frame_count, 1, item_count, channels)
    out_slab = lax.all_to_all(out_part, "frame", split_axis=0, concat_axis=1, tiled=True)
    grad_slab = lax.all_to_all(back_part, "frame", split_axis=0, concat_axis=1, tiled=True)
    act_grad = grad_slab.reshape(row_count, channels)
    sig = jax.nn.sigmoid(pre)
    pre_grad = (act_grad.astype(jnp.float32) * (sig * (1.0 + pre * (1.0 - sig)))).astype(
        jnp.bfloat16
    )
    full_term = lax.dot_general(
        feat_columns, pre_grad, (((0,), (0,)), ((), ())), preferred_element_type=jnp.float32
    )
    blk = full_term.shape[0] // (frame_devs * tile_devs)
    swapped = full_term.reshape(frame_devs, tile_devs, blk, channels).transpose(1, 0, 2, 3)
    stage = lax.psum_scatter(swapped, "tile", scatter_dimension=0, tiled=True)
    summed = lax.psum_scatter(stage.reshape(frame_devs, blk, channels), "frame", scatter_dimension=0, tiled=True).reshape(blk, channels)
    weight_grad = summed * grad_scale
    grad_ext = padded_2(
        pre_grad.reshape(slab_frames, tile_rows, width_cells, channels), (("tile", 1),), 1
    )
    grad_columns = tile_columns(grad_ext, tile_rows, width_cells, True)
    local_back = jnp.dot(grad_columns, spatial_back, preferred_element_type=jnp.float32)
    input_grad = (out_grad.reshape(row_count, channels).astype(jnp.float32) + local_back).astype(
        jnp.bfloat16
    )
    input_grad = input_grad.reshape(slab_frames, tile_rows, width_cells, channels)
    return (out_slab, input_grad, weight_grad)


def solution(mesh):
    return jax.shard_map(
        per_device,
        mesh=mesh,
        in_specs=(
            P(("clip", "frame"), "tile", None, None),
            P(("clip", "frame"), "tile", None, None),
            P(),
            P(),
        ),
        out_specs=(
            P(("clip", "frame"), "tile", None, None),
            P(("clip", "frame"), "tile", None, None),
            P(("clip", "frame", "tile"), None),
        ),
        check_vma=False,
    )
```

```python
import math

import jax
import jax.numpy as jnp
from jax import lax
from jax.sharding import PartitionSpec as P

TAP_DILATION = 2


def padded_2(block, sides, width):
    for axis, dim in sides:
        count = lax.axis_size(axis)
        forward = [(i, i + 1) for i in range(count - 1)]
        backward = [(target, source) for source, target in forward]
        low = lax.ppermute(
            lax.slice_in_dim(block, block.shape[dim] - width, None, axis=dim), axis, forward
        )
        high = lax.ppermute(lax.slice_in_dim(block, 0, width, axis=dim), axis, backward)
        block = jnp.concatenate([low, block, high], axis=dim)
    return block


def halving_scatter(term, axes):
    sizes = [size for _, size in axes]
    if any(size & (size - 1) for size in sizes):
        return lax.psum_scatter(term, tuple(name for name, _ in axes), scatter_dimension=0, tiled=True)
    bits = []
    for name, size in axes:
        bits += [(name, size, b) for b in reversed(range(size.bit_length() - 1))]
    groups = 1
    for size in sizes:
        groups *= size
    block = term.shape[0] // groups
    x = term.reshape((2,) * len(bits) + (block,) + term.shape[1:])
    for pos in reversed(range(len(bits))):
        name, size, b = bits[pos]
        mine = (lax.axis_index(name) >> b) & 1
        keep = lax.dynamic_index_in_dim(x, mine, axis=pos, keepdims=False)
        send = lax.dynamic_index_in_dim(x, 1 - mine, axis=pos, keepdims=False)
        pairs = [(i, i ^ (1 << b)) for i in range(size)]
        x = keep + lax.ppermute(send, name, pairs)
    return x


def tile_columns(extended, tile_rows, width_cells, backward_pass):
    padded = jnp.pad(extended, ((0, 0), (0, 0), (1, 1), (0, 0)))
    pieces = []
    for row_shift in range(3):
        for col_shift in range(3):
            row_start = 2 - row_shift if backward_pass else row_shift
            col_start = 2 - col_shift if backward_pass else col_shift
            pieces.append(
                padded[:, row_start : row_start + tile_rows, col_start : col_start + width_cells, :]
            )
    channels = extended.shape[3]
    return jnp.concatenate(pieces, axis=-1).reshape(-1, 9 * channels)


def temporal_taps(padded_seq, weight, frame_count, backward_pass):
    pieces = []
    for temporal_tap_index in range(9):
        first_frame_index = (
            (8 - temporal_tap_index) * TAP_DILATION
            if backward_pass
            else temporal_tap_index * TAP_DILATION
        )
        pieces.append(padded_seq[first_frame_index : first_frame_index + frame_count])
    channels = padded_seq.shape[2]
    columns = jnp.concatenate(pieces, axis=-1).reshape(-1, 9 * channels)
    return jnp.dot(columns, weight, preferred_element_type=jnp.float32)


def per_device(clip_feats, out_grad, spatial_weight, temporal_weight):
    slab_frames, tile_rows, width_cells, channels = clip_feats.shape
    row_count = slab_frames * tile_rows * width_cells
    frame_devs = lax.axis_size("frame")
    tile_devs = lax.axis_size("tile")
    grad_scale = jnp.float32(
        1.0 / math.sqrt(slab_frames * frame_devs * tile_rows * tile_devs * width_cells)
    )
    spatial_back = (
        spatial_weight.reshape(9, channels, channels)
        .transpose(0, 2, 1)
        .reshape(9 * channels, channels)
    )
    temporal_back = (
        temporal_weight.reshape(9, channels, channels)
        .transpose(0, 2, 1)
        .reshape(9 * channels, channels)
    )
    feat_ext = padded_2(clip_feats, (("tile", 1),), 1)
    feat_columns = tile_columns(feat_ext, tile_rows, width_cells, False)
    pre = jnp.dot(feat_columns, spatial_weight, preferred_element_type=jnp.float32)
    act = jax.nn.silu(pre).astype(jnp.bfloat16)
    temporal_reach = 4 * TAP_DILATION
    per_group = tile_rows * width_cells // frame_devs
    grouped = (slab_frames, frame_devs, per_group, channels)
    act_part = lax.all_to_all(
        act.reshape(grouped), "frame", split_axis=1, concat_axis=0, tiled=True
    )
    grad_part = lax.all_to_all(out_grad, "frame", split_axis=1, concat_axis=0, tiled=True)
    feat_part = lax.all_to_all(clip_feats, "frame", split_axis=1, concat_axis=0, tiled=True)
    frame_count = act_part.shape[0]
    item_count = act_part.shape[2]
    act_pad = jnp.pad(
        act_part.reshape(frame_count, item_count, channels),
        ((temporal_reach, temporal_reach), (0, 0), (0, 0)),
    )
    grad_pad = jnp.pad(
        grad_part.reshape(frame_count, item_count, channels),
        ((temporal_reach, temporal_reach), (0, 0), (0, 0)),
    )
    mixed = temporal_taps(act_pad, temporal_weight, frame_count, False)
    out_part = (feat_part.reshape(-1, channels).astype(jnp.float32) + mixed).astype(jnp.bfloat16)
    back_part = temporal_taps(grad_pad, temporal_back, frame_count, True).astype(jnp.bfloat16)
    out_part = out_part.reshape(frame_count, 1, item_count, channels)
    back_part = back_part.reshape(frame_count, 1, item_count, channels)
    out_slab = lax.all_to_all(out_part, "frame", split_axis=0, concat_axis=1, tiled=True)
    grad_slab = lax.all_to_all(back_part, "frame", split_axis=0, concat_axis=1, tiled=True)
    act_grad = grad_slab.reshape(row_count, channels)
    sig = jax.nn.sigmoid(pre)
    pre_grad = (act_grad.astype(jnp.float32) * (sig * (1.0 + pre * (1.0 - sig)))).astype(
        jnp.bfloat16
    )
    full_term = lax.dot_general(
        feat_columns, pre_grad, (((0,), (0,)), ((), ())), preferred_element_type=jnp.float32
    )
    summed = halving_scatter(full_term, (("frame", frame_devs), ("tile", tile_devs)))
    weight_grad = summed * grad_scale
    grad_ext = padded_2(
        pre_grad.reshape(slab_frames, tile_rows, width_cells, channels), (("tile", 1),), 1
    )
    grad_columns = tile_columns(grad_ext, tile_rows, width_cells, True)
    local_back = jnp.dot(grad_columns, spatial_back, preferred_element_type=jnp.float32)
    input_grad = (out_grad.reshape(row_count, channels).astype(jnp.float32) + local_back).astype(
        jnp.bfloat16
    )
    input_grad = input_grad.reshape(slab_frames, tile_rows, width_cells, channels)
    return (out_slab, input_grad, weight_grad)


def solution(mesh):
    return jax.shard_map(
        per_device,
        mesh=mesh,
        in_specs=(
            P(("clip", "frame"), "tile", None, None),
            P(("clip", "frame"), "tile", None, None),
            P(),
            P(),
        ),
        out_specs=(
            P(("clip", "frame"), "tile", None, None),
            P(("clip", "frame"), "tile", None, None),
            P(("clip", "frame", "tile"), None),
        ),
        check_vma=False,
    )
```

```python
import math

import jax
import jax.numpy as jnp
from jax import lax
from jax.sharding import PartitionSpec as P

TAP_DILATION = 2


def padded_2(block, sides, width):
    for axis, dim in sides:
        count = lax.axis_size(axis)
        forward = [(i, i + 1) for i in range(count - 1)]
        backward = [(target, source) for source, target in forward]
        low = lax.ppermute(
            lax.slice_in_dim(block, block.shape[dim] - width, None, axis=dim), axis, forward
        )
        high = lax.ppermute(lax.slice_in_dim(block, 0, width, axis=dim), axis, backward)
        block = jnp.concatenate([low, block, high], axis=dim)
    return block


def halving_scatter(term, axes):
    sizes = [size for _, size in axes]
    if any(size & (size - 1) for size in sizes):
        return lax.psum_scatter(term, tuple(name for name, _ in axes), scatter_dimension=0, tiled=True)
    bits = []
    for name, size in axes:
        bits += [(name, size, b) for b in reversed(range(size.bit_length() - 1))]
    groups = 1
    for size in sizes:
        groups *= size
    block = term.shape[0] // groups
    x = term.reshape((2,) * len(bits) + (block,) + term.shape[1:])
    for pos in reversed(range(len(bits))):
        name, size, b = bits[pos]
        mine = (lax.axis_index(name) >> b) & 1
        keep = lax.dynamic_index_in_dim(x, mine, axis=pos, keepdims=False)
        send = lax.dynamic_index_in_dim(x, 1 - mine, axis=pos, keepdims=False)
        pairs = [(i, i ^ (1 << b)) for i in range(size)]
        x = keep + lax.ppermute(send, name, pairs)
    return x


def tile_columns(extended, tile_rows, width_cells, backward_pass):
    padded = jnp.pad(extended, ((0, 0), (0, 0), (1, 1), (0, 0)))
    pieces = []
    for row_shift in range(3):
        for col_shift in range(3):
            row_start = 2 - row_shift if backward_pass else row_shift
            col_start = 2 - col_shift if backward_pass else col_shift
            pieces.append(
                padded[:, row_start : row_start + tile_rows, col_start : col_start + width_cells, :]
            )
    channels = extended.shape[3]
    return jnp.concatenate(pieces, axis=-1).reshape(-1, 9 * channels)


def temporal_taps(padded_seq, weight, frame_count, backward_pass):
    pieces = []
    for temporal_tap_index in range(9):
        first_frame_index = (
            (8 - temporal_tap_index) * TAP_DILATION
            if backward_pass
            else temporal_tap_index * TAP_DILATION
        )
        pieces.append(padded_seq[first_frame_index : first_frame_index + frame_count])
    channels = padded_seq.shape[2]
    columns = jnp.concatenate(pieces, axis=-1).reshape(-1, 9 * channels)
    return jnp.dot(columns, weight, preferred_element_type=jnp.float32)


def frame_exchange(clip_feats, out_grad, act, temporal_weight, temporal_back, temporal_reach):
    slab_frames, tile_rows, width_cells, channels = clip_feats.shape
    row_count = slab_frames * tile_rows * width_cells
    frame_devs = lax.axis_size("frame")
    per_group = tile_rows * width_cells // frame_devs
    grouped = (slab_frames, frame_devs, per_group, channels)
    act_part = lax.all_to_all(
        act.reshape(grouped), "frame", split_axis=1, concat_axis=0, tiled=True
    )
    grad_part = lax.all_to_all(out_grad, "frame", split_axis=1, concat_axis=0, tiled=True)
    feat_part = lax.all_to_all(clip_feats, "frame", split_axis=1, concat_axis=0, tiled=True)
    frame_count = act_part.shape[0]
    item_count = act_part.shape[2]
    act_pad = jnp.pad(
        act_part.reshape(frame_count, item_count, channels),
        ((temporal_reach, temporal_reach), (0, 0), (0, 0)),
    )
    grad_pad = jnp.pad(
        grad_part.reshape(frame_count, item_count, channels),
        ((temporal_reach, temporal_reach), (0, 0), (0, 0)),
    )
    mixed = temporal_taps(act_pad, temporal_weight, frame_count, False)
    out_part = (feat_part.reshape(-1, channels).astype(jnp.float32) + mixed).astype(jnp.bfloat16)
    back_part = temporal_taps(grad_pad, temporal_back, frame_count, True).astype(jnp.bfloat16)
    out_part = out_part.reshape(frame_count, 1, item_count, channels)
    back_part = back_part.reshape(frame_count, 1, item_count, channels)
    out_slab = lax.all_to_all(out_part, "frame", split_axis=0, concat_axis=1, tiled=True)
    grad_slab = lax.all_to_all(back_part, "frame", split_axis=0, concat_axis=1, tiled=True)
    act_grad = grad_slab.reshape(row_count, channels)
    return out_slab, act_grad


def per_device(clip_feats, out_grad, spatial_weight, temporal_weight):
    slab_frames, tile_rows, width_cells, channels = clip_feats.shape
    row_count = slab_frames * tile_rows * width_cells
    frame_devs = lax.axis_size("frame")
    tile_devs = lax.axis_size("tile")
    grad_scale = jnp.float32(
        1.0 / math.sqrt(slab_frames * frame_devs * tile_rows * tile_devs * width_cells)
    )
    spatial_back = (
        spatial_weight.reshape(9, channels, channels)
        .transpose(0, 2, 1)
        .reshape(9 * channels, channels)
    )
    temporal_back = (
        temporal_weight.reshape(9, channels, channels)
        .transpose(0, 2, 1)
        .reshape(9 * channels, channels)
    )
    feat_ext = padded_2(clip_feats, (("tile", 1),), 1)
    feat_columns = tile_columns(feat_ext, tile_rows, width_cells, False)
    pre = jnp.dot(feat_columns, spatial_weight, preferred_element_type=jnp.float32)
    act = jax.nn.silu(pre).astype(jnp.bfloat16)
    temporal_reach = 4 * TAP_DILATION
    if temporal_reach <= slab_frames:
        seq_shape = (slab_frames, tile_rows * width_cells, channels)
        act_ext = padded_2(act.reshape(seq_shape), (("frame", 0),), temporal_reach)
        grad_ext = padded_2(out_grad.reshape(seq_shape), (("frame", 0),), temporal_reach)
        act_grad = temporal_taps(grad_ext, temporal_back, slab_frames, True).astype(jnp.bfloat16)
        mixed = temporal_taps(act_ext, temporal_weight, slab_frames, False)
        out_slab = (clip_feats.reshape(-1, channels).astype(jnp.float32) + mixed).astype(
            jnp.bfloat16
        )
        out_slab = out_slab.reshape(clip_feats.shape)
    else:
        out_slab, act_grad = frame_exchange(
            clip_feats, out_grad, act, temporal_weight, temporal_back, temporal_reach
        )
    sig = jax.nn.sigmoid(pre)
    pre_grad = (act_grad.astype(jnp.float32) * (sig * (1.0 + pre * (1.0 - sig)))).astype(
        jnp.bfloat16
    )
    full_term = lax.dot_general(
        feat_columns, pre_grad, (((0,), (0,)), ((), ())), preferred_element_type=jnp.float32
    )
    summed = halving_scatter(full_term, (("frame", frame_devs), ("tile", tile_devs)))
    weight_grad = summed * grad_scale
    grad_ext = padded_2(
        pre_grad.reshape(slab_frames, tile_rows, width_cells, channels), (("tile", 1),), 1
    )
    grad_columns = tile_columns(grad_ext, tile_rows, width_cells, True)
    local_back = jnp.dot(grad_columns, spatial_back, preferred_element_type=jnp.float32)
    input_grad = (out_grad.reshape(row_count, channels).astype(jnp.float32) + local_back).astype(
        jnp.bfloat16
    )
    input_grad = input_grad.reshape(slab_frames, tile_rows, width_cells, channels)
    return (out_slab, input_grad, weight_grad)


def solution(mesh):
    return jax.shard_map(
        per_device,
        mesh=mesh,
        in_specs=(
            P(("clip", "frame"), "tile", None, None),
            P(("clip", "frame"), "tile", None, None),
            P(),
            P(),
        ),
        out_specs=(
            P(("clip", "frame"), "tile", None, None),
            P(("clip", "frame"), "tile", None, None),
            P(("clip", "frame", "tile"), None),
        ),
        check_vma=False,
    )
```

```python
import functools
import math

import jax
import jax.numpy as jnp
from jax import lax
from jax.experimental import pallas as pl
from jax.experimental.pallas import tpu as pltpu
from jax.sharding import PartitionSpec as P

TAP_DILATION = 2


def padded_2(block, sides, width):
    for axis, dim in sides:
        count = lax.axis_size(axis)
        forward = [(i, i + 1) for i in range(count - 1)]
        backward = [(target, source) for source, target in forward]
        low = lax.ppermute(
            lax.slice_in_dim(block, block.shape[dim] - width, None, axis=dim), axis, forward
        )
        high = lax.ppermute(lax.slice_in_dim(block, 0, width, axis=dim), axis, backward)
        block = jnp.concatenate([low, block, high], axis=dim)
    return block


def halving_scatter(term, axes):
    sizes = [size for _, size in axes]
    if any(size & (size - 1) for size in sizes):
        return lax.psum_scatter(term, tuple(name for name, _ in axes), scatter_dimension=0, tiled=True)
    bits = []
    for name, size in axes:
        bits += [(name, size, b) for b in reversed(range(size.bit_length() - 1))]
    groups = 1
    for size in sizes:
        groups *= size
    block = term.shape[0] // groups
    x = term.reshape((2,) * len(bits) + (block,) + term.shape[1:])
    for pos in reversed(range(len(bits))):
        name, size, b = bits[pos]
        mine = (lax.axis_index(name) >> b) & 1
        keep = lax.dynamic_index_in_dim(x, mine, axis=pos, keepdims=False)
        send = lax.dynamic_index_in_dim(x, 1 - mine, axis=pos, keepdims=False)
        pairs = [(i, i ^ (1 << b)) for i in range(size)]
        x = keep + lax.ppermute(send, name, pairs)
    return x


def halving_kernel(steps, x_ref, o_ref, acc, recv, send_sems, recv_sems):
    mesh_ids = pl.DeviceIdType.MESH
    plan = []
    for name, b in steps:
        me = lax.axis_index(name)
        mine = (me // (1 << b)) % 2
        plan.append((name, me + (1 - 2 * mine) * (1 << b), mine))
    barrier = pltpu.get_barrier_semaphore()
    for name, partner, _ in plan:
        pl.semaphore_signal(barrier, inc=1, device_id={name: partner}, device_id_type=mesh_ids)
    pl.semaphore_wait(barrier, len(plan))
    source = x_ref
    count = x_ref.shape[0]
    offset = 0
    for k, (name, partner, mine) in enumerate(plan):
        half = count // 2
        landing = recv.at[pl.ds(offset, half)]
        copy = pltpu.make_async_remote_copy(
            src_ref=source.at[pl.ds((1 - mine) * half, half)],
            dst_ref=landing,
            send_sem=send_sems.at[k],
            recv_sem=recv_sems.at[k],
            device_id={name: partner},
            device_id_type=mesh_ids,
        )
        copy.start()
        copy.wait()
        total = source[pl.ds(mine * half, half)] + landing[...]
        if k == len(plan) - 1:
            o_ref[...] = total[0]
        else:
            target = acc.at[pl.ds(offset, half)]
            target[...] = total
            source = target
        offset += half
        count = half


def kernel_scatter(term, axes):
    sizes = [size for _, size in axes]
    groups = 1
    for size in sizes:
        groups *= size
    per_block = term.shape[0] * term.shape[1] // groups
    if any(size & (size - 1) for size in sizes) or per_block % 128:
        return halving_scatter(term, axes)
    bits = []
    for name, size in axes:
        bits += [(name, b) for b in reversed(range(size.bit_length() - 1))]
    n = len(bits)
    x = term.reshape((2,) * n + (per_block,)).transpose(tuple(reversed(range(n))) + (n,))
    x = x.reshape(groups, per_block // 128, 128)
    steps = list(reversed(bits))
    out = pl.pallas_call(
        functools.partial(halving_kernel, steps),
        out_shape=jax.ShapeDtypeStruct(x.shape[1:], x.dtype),
        in_specs=[pl.BlockSpec(memory_space=pltpu.VMEM)],
        out_specs=pl.BlockSpec(memory_space=pltpu.VMEM),
        scratch_shapes=[
            pltpu.VMEM(x.shape, x.dtype),
            pltpu.VMEM(x.shape, x.dtype),
            pltpu.SemaphoreType.DMA((n,)),
            pltpu.SemaphoreType.DMA((n,)),
        ],
        compiler_params=pltpu.CompilerParams(collective_id=0, has_side_effects=True),
    )(x)
    return out.reshape(term.shape[0] // groups, term.shape[1])


def tile_columns(extended, tile_rows, width_cells, backward_pass):
    padded = jnp.pad(extended, ((0, 0), (0, 0), (1, 1), (0, 0)))
    pieces = []
    for row_shift in range(3):
        for col_shift in range(3):
            row_start = 2 - row_shift if backward_pass else row_shift
            col_start = 2 - col_shift if backward_pass else col_shift
            pieces.append(
                padded[:, row_start : row_start + tile_rows, col_start : col_start + width_cells, :]
            )
    channels = extended.shape[3]
    return jnp.concatenate(pieces, axis=-1).reshape(-1, 9 * channels)


def temporal_taps(padded_seq, weight, frame_count, backward_pass):
    pieces = []
    for temporal_tap_index in range(9):
        first_frame_index = (
            (8 - temporal_tap_index) * TAP_DILATION
            if backward_pass
            else temporal_tap_index * TAP_DILATION
        )
        pieces.append(padded_seq[first_frame_index : first_frame_index + frame_count])
    channels = padded_seq.shape[2]
    columns = jnp.concatenate(pieces, axis=-1).reshape(-1, 9 * channels)
    return jnp.dot(columns, weight, preferred_element_type=jnp.float32)


def frame_exchange(clip_feats, out_grad, act, temporal_weight, temporal_back, temporal_reach):
    slab_frames, tile_rows, width_cells, channels = clip_feats.shape
    row_count = slab_frames * tile_rows * width_cells
    frame_devs = lax.axis_size("frame")
    per_group = tile_rows * width_cells // frame_devs
    grouped = (slab_frames, frame_devs, per_group, channels)
    act_part = lax.all_to_all(
        act.reshape(grouped), "frame", split_axis=1, concat_axis=0, tiled=True
    )
    grad_part = lax.all_to_all(out_grad, "frame", split_axis=1, concat_axis=0, tiled=True)
    feat_part = lax.all_to_all(clip_feats, "frame", split_axis=1, concat_axis=0, tiled=True)
    frame_count = act_part.shape[0]
    item_count = act_part.shape[2]
    act_pad = jnp.pad(
        act_part.reshape(frame_count, item_count, channels),
        ((temporal_reach, temporal_reach), (0, 0), (0, 0)),
    )
    grad_pad = jnp.pad(
        grad_part.reshape(frame_count, item_count, channels),
        ((temporal_reach, temporal_reach), (0, 0), (0, 0)),
    )
    mixed = temporal_taps(act_pad, temporal_weight, frame_count, False)
    out_part = (feat_part.reshape(-1, channels).astype(jnp.float32) + mixed).astype(jnp.bfloat16)
    back_part = temporal_taps(grad_pad, temporal_back, frame_count, True).astype(jnp.bfloat16)
    out_part = out_part.reshape(frame_count, 1, item_count, channels)
    back_part = back_part.reshape(frame_count, 1, item_count, channels)
    out_slab = lax.all_to_all(out_part, "frame", split_axis=0, concat_axis=1, tiled=True)
    grad_slab = lax.all_to_all(back_part, "frame", split_axis=0, concat_axis=1, tiled=True)
    act_grad = grad_slab.reshape(row_count, channels)
    return out_slab, act_grad


def per_device(clip_feats, out_grad, spatial_weight, temporal_weight):
    slab_frames, tile_rows, width_cells, channels = clip_feats.shape
    row_count = slab_frames * tile_rows * width_cells
    frame_devs = lax.axis_size("frame")
    tile_devs = lax.axis_size("tile")
    grad_scale = jnp.float32(
        1.0 / math.sqrt(slab_frames * frame_devs * tile_rows * tile_devs * width_cells)
    )
    spatial_back = (
        spatial_weight.reshape(9, channels, channels)
        .transpose(0, 2, 1)
        .reshape(9 * channels, channels)
    )
    temporal_back = (
        temporal_weight.reshape(9, channels, channels)
        .transpose(0, 2, 1)
        .reshape(9 * channels, channels)
    )
    feat_ext = padded_2(clip_feats, (("tile", 1),), 1)
    feat_columns = tile_columns(feat_ext, tile_rows, width_cells, False)
    pre = jnp.dot(feat_columns, spatial_weight, preferred_element_type=jnp.float32)
    act = jax.nn.silu(pre).astype(jnp.bfloat16)
    temporal_reach = 4 * TAP_DILATION
    if temporal_reach <= slab_frames:
        seq_shape = (slab_frames, tile_rows * width_cells, channels)
        act_ext = padded_2(act.reshape(seq_shape), (("frame", 0),), temporal_reach)
        grad_ext = padded_2(out_grad.reshape(seq_shape), (("frame", 0),), temporal_reach)
        act_grad = temporal_taps(grad_ext, temporal_back, slab_frames, True).astype(jnp.bfloat16)
        mixed = temporal_taps(act_ext, temporal_weight, slab_frames, False)
        out_slab = (clip_feats.reshape(-1, channels).astype(jnp.float32) + mixed).astype(
            jnp.bfloat16
        )
        out_slab = out_slab.reshape(clip_feats.shape)
    else:
        out_slab, act_grad = frame_exchange(
            clip_feats, out_grad, act, temporal_weight, temporal_back, temporal_reach
        )
    sig = jax.nn.sigmoid(pre)
    pre_grad = (act_grad.astype(jnp.float32) * (sig * (1.0 + pre * (1.0 - sig)))).astype(
        jnp.bfloat16
    )
    full_term = lax.dot_general(
        feat_columns, pre_grad, (((0,), (0,)), ((), ())), preferred_element_type=jnp.float32
    )
    summed = kernel_scatter(full_term, (("frame", frame_devs), ("tile", tile_devs)))
    weight_grad = summed * grad_scale
    grad_ext = padded_2(
        pre_grad.reshape(slab_frames, tile_rows, width_cells, channels), (("tile", 1),), 1
    )
    grad_columns = tile_columns(grad_ext, tile_rows, width_cells, True)
    local_back = jnp.dot(grad_columns, spatial_back, preferred_element_type=jnp.float32)
    input_grad = (out_grad.reshape(row_count, channels).astype(jnp.float32) + local_back).astype(
        jnp.bfloat16
    )
    input_grad = input_grad.reshape(slab_frames, tile_rows, width_cells, channels)
    return (out_slab, input_grad, weight_grad)


def solution(mesh):
    return jax.shard_map(
        per_device,
        mesh=mesh,
        in_specs=(
            P(("clip", "frame"), "tile", None, None),
            P(("clip", "frame"), "tile", None, None),
            P(),
            P(),
        ),
        out_specs=(
            P(("clip", "frame"), "tile", None, None),
            P(("clip", "frame"), "tile", None, None),
            P(("clip", "frame", "tile"), None),
        ),
        check_vma=False,
    )
```

```python
import functools
import math

import jax
import jax.numpy as jnp
from jax import lax
from jax.experimental import pallas as pl
from jax.experimental.pallas import tpu as pltpu
from jax.sharding import PartitionSpec as P

TAP_DILATION = 2


def padded_2(block, sides, width):
    for axis, dim in sides:
        count = lax.axis_size(axis)
        forward = [(i, i + 1) for i in range(count - 1)]
        backward = [(target, source) for source, target in forward]
        low = lax.ppermute(
            lax.slice_in_dim(block, block.shape[dim] - width, None, axis=dim), axis, forward
        )
        high = lax.ppermute(lax.slice_in_dim(block, 0, width, axis=dim), axis, backward)
        block = jnp.concatenate([low, block, high], axis=dim)
    return block


def halving_scatter(term, axes):
    sizes = [size for _, size in axes]
    if any(size & (size - 1) for size in sizes):
        return lax.psum_scatter(term, tuple(name for name, _ in axes), scatter_dimension=0, tiled=True)
    bits = []
    for name, size in axes:
        bits += [(name, size, b) for b in reversed(range(size.bit_length() - 1))]
    groups = 1
    for size in sizes:
        groups *= size
    block = term.shape[0] // groups
    x = term.reshape((2,) * len(bits) + (block,) + term.shape[1:])
    for pos in reversed(range(len(bits))):
        name, size, b = bits[pos]
        mine = (lax.axis_index(name) >> b) & 1
        keep = lax.dynamic_index_in_dim(x, mine, axis=pos, keepdims=False)
        send = lax.dynamic_index_in_dim(x, 1 - mine, axis=pos, keepdims=False)
        pairs = [(i, i ^ (1 << b)) for i in range(size)]
        x = keep + lax.ppermute(send, name, pairs)
    return x


def halving_kernel(steps, narrow, x_ref, o_ref, *scratch):
    n = len(steps)
    send_sems, recv_sems = scratch[-2], scratch[-1]
    landings = scratch[:n]
    accs = scratch[n : 2 * n - 1]
    packs = scratch[2 * n - 1 : 2 * n - 1 + narrow]
    mesh_ids = pl.DeviceIdType.MESH
    plan = []
    for name, b in steps:
        me = lax.axis_index(name)
        mine = (me // (1 << b)) % 2
        plan.append((name, me + (1 - 2 * mine) * (1 << b), mine))
    barrier = pltpu.get_barrier_semaphore()
    for name, partner, _ in plan:
        pl.semaphore_signal(barrier, inc=1, device_id={name: partner}, device_id_type=mesh_ids)
    pl.semaphore_wait(barrier, len(plan))
    source = x_ref
    count = x_ref.shape[0]
    for k, (name, partner, mine) in enumerate(plan):
        half = count // 2
        outgoing = source.at[pl.ds((1 - mine) * half, half)]
        if k < narrow:
            packs[k][...] = outgoing[...].astype(packs[k].dtype)
            outgoing = packs[k]
        copy = pltpu.make_async_remote_copy(
            src_ref=outgoing,
            dst_ref=landings[k],
            send_sem=send_sems.at[k],
            recv_sem=recv_sems.at[k],
            device_id={name: partner},
            device_id_type=mesh_ids,
        )
        copy.start()
        copy.wait()
        total = source[pl.ds(mine * half, half)] + landings[k][...].astype(jnp.float32)
        if k == n - 1:
            o_ref[...] = total[0]
        else:
            accs[k][...] = total
            source = accs[k]
        count = half


def kernel_scatter(term, axes):
    sizes = [size for _, size in axes]
    groups = 1
    for size in sizes:
        groups *= size
    per_block = term.shape[0] * term.shape[1] // groups
    if any(size & (size - 1) for size in sizes) or per_block % 128:
        return halving_scatter(term, axes)
    bits = []
    for name, size in axes:
        bits += [(name, b) for b in reversed(range(size.bit_length() - 1))]
    n = len(bits)
    x = term.reshape((2,) * n + (per_block,)).transpose(tuple(reversed(range(n))) + (n,))
    x = x.reshape(groups, per_block // 128, 128)
    steps = list(reversed(bits))
    narrow = min(3, n)
    rows = x.shape[1:]
    halves = [groups >> (k + 1) for k in range(n)]
    scratch = [
        pltpu.VMEM((halves[k],) + rows, jnp.bfloat16 if k < narrow else jnp.float32)
        for k in range(n)
    ]
    scratch += [pltpu.VMEM((halves[k],) + rows, jnp.float32) for k in range(n - 1)]
    scratch += [pltpu.VMEM((halves[k],) + rows, jnp.bfloat16) for k in range(narrow)]
    scratch += [pltpu.SemaphoreType.DMA((n,)), pltpu.SemaphoreType.DMA((n,))]
    out = pl.pallas_call(
        functools.partial(halving_kernel, steps, narrow),
        out_shape=jax.ShapeDtypeStruct(rows, x.dtype),
        in_specs=[pl.BlockSpec(memory_space=pltpu.VMEM)],
        out_specs=pl.BlockSpec(memory_space=pltpu.VMEM),
        scratch_shapes=scratch,
        compiler_params=pltpu.CompilerParams(collective_id=0, has_side_effects=True),
    )(x)
    return out.reshape(term.shape[0] // groups, term.shape[1])


def tile_columns(extended, tile_rows, width_cells, backward_pass):
    padded = jnp.pad(extended, ((0, 0), (0, 0), (1, 1), (0, 0)))
    pieces = []
    for row_shift in range(3):
        for col_shift in range(3):
            row_start = 2 - row_shift if backward_pass else row_shift
            col_start = 2 - col_shift if backward_pass else col_shift
            pieces.append(
                padded[:, row_start : row_start + tile_rows, col_start : col_start + width_cells, :]
            )
    channels = extended.shape[3]
    return jnp.concatenate(pieces, axis=-1).reshape(-1, 9 * channels)


def temporal_taps(padded_seq, weight, frame_count, backward_pass):
    pieces = []
    for temporal_tap_index in range(9):
        first_frame_index = (
            (8 - temporal_tap_index) * TAP_DILATION
            if backward_pass
            else temporal_tap_index * TAP_DILATION
        )
        pieces.append(padded_seq[first_frame_index : first_frame_index + frame_count])
    channels = padded_seq.shape[2]
    columns = jnp.concatenate(pieces, axis=-1).reshape(-1, 9 * channels)
    return jnp.dot(columns, weight, preferred_element_type=jnp.float32)


def frame_exchange(clip_feats, out_grad, act, temporal_weight, temporal_back, temporal_reach):
    slab_frames, tile_rows, width_cells, channels = clip_feats.shape
    row_count = slab_frames * tile_rows * width_cells
    frame_devs = lax.axis_size("frame")
    per_group = tile_rows * width_cells // frame_devs
    grouped = (slab_frames, frame_devs, per_group, channels)
    act_part = lax.all_to_all(
        act.reshape(grouped), "frame", split_axis=1, concat_axis=0, tiled=True
    )
    grad_part = lax.all_to_all(out_grad, "frame", split_axis=1, concat_axis=0, tiled=True)
    feat_part = lax.all_to_all(clip_feats, "frame", split_axis=1, concat_axis=0, tiled=True)
    frame_count = act_part.shape[0]
    item_count = act_part.shape[2]
    act_pad = jnp.pad(
        act_part.reshape(frame_count, item_count, channels),
        ((temporal_reach, temporal_reach), (0, 0), (0, 0)),
    )
    grad_pad = jnp.pad(
        grad_part.reshape(frame_count, item_count, channels),
        ((temporal_reach, temporal_reach), (0, 0), (0, 0)),
    )
    mixed = temporal_taps(act_pad, temporal_weight, frame_count, False)
    out_part = (feat_part.reshape(-1, channels).astype(jnp.float32) + mixed).astype(jnp.bfloat16)
    back_part = temporal_taps(grad_pad, temporal_back, frame_count, True).astype(jnp.bfloat16)
    out_part = out_part.reshape(frame_count, 1, item_count, channels)
    back_part = back_part.reshape(frame_count, 1, item_count, channels)
    out_slab = lax.all_to_all(out_part, "frame", split_axis=0, concat_axis=1, tiled=True)
    grad_slab = lax.all_to_all(back_part, "frame", split_axis=0, concat_axis=1, tiled=True)
    act_grad = grad_slab.reshape(row_count, channels)
    return out_slab, act_grad


def per_device(clip_feats, out_grad, spatial_weight, temporal_weight):
    slab_frames, tile_rows, width_cells, channels = clip_feats.shape
    row_count = slab_frames * tile_rows * width_cells
    frame_devs = lax.axis_size("frame")
    tile_devs = lax.axis_size("tile")
    grad_scale = jnp.float32(
        1.0 / math.sqrt(slab_frames * frame_devs * tile_rows * tile_devs * width_cells)
    )
    spatial_back = (
        spatial_weight.reshape(9, channels, channels)
        .transpose(0, 2, 1)
        .reshape(9 * channels, channels)
    )
    temporal_back = (
        temporal_weight.reshape(9, channels, channels)
        .transpose(0, 2, 1)
        .reshape(9 * channels, channels)
    )
    feat_ext = padded_2(clip_feats, (("tile", 1),), 1)
    feat_columns = tile_columns(feat_ext, tile_rows, width_cells, False)
    pre = jnp.dot(feat_columns, spatial_weight, preferred_element_type=jnp.float32)
    act = jax.nn.silu(pre).astype(jnp.bfloat16)
    temporal_reach = 4 * TAP_DILATION
    if temporal_reach <= slab_frames:
        seq_shape = (slab_frames, tile_rows * width_cells, channels)
        act_ext = padded_2(act.reshape(seq_shape), (("frame", 0),), temporal_reach)
        grad_ext = padded_2(out_grad.reshape(seq_shape), (("frame", 0),), temporal_reach)
        act_grad = temporal_taps(grad_ext, temporal_back, slab_frames, True).astype(jnp.bfloat16)
        mixed = temporal_taps(act_ext, temporal_weight, slab_frames, False)
        out_slab = (clip_feats.reshape(-1, channels).astype(jnp.float32) + mixed).astype(
            jnp.bfloat16
        )
        out_slab = out_slab.reshape(clip_feats.shape)
    else:
        out_slab, act_grad = frame_exchange(
            clip_feats, out_grad, act, temporal_weight, temporal_back, temporal_reach
        )
    sig = jax.nn.sigmoid(pre)
    pre_grad = (act_grad.astype(jnp.float32) * (sig * (1.0 + pre * (1.0 - sig)))).astype(
        jnp.bfloat16
    )
    full_term = lax.dot_general(
        feat_columns, pre_grad, (((0,), (0,)), ((), ())), preferred_element_type=jnp.float32
    )
    summed = kernel_scatter(full_term, (("frame", frame_devs), ("tile", tile_devs)))
    weight_grad = summed * grad_scale
    grad_ext = padded_2(
        pre_grad.reshape(slab_frames, tile_rows, width_cells, channels), (("tile", 1),), 1
    )
    grad_columns = tile_columns(grad_ext, tile_rows, width_cells, True)
    local_back = jnp.dot(grad_columns, spatial_back, preferred_element_type=jnp.float32)
    input_grad = (out_grad.reshape(row_count, channels).astype(jnp.float32) + local_back).astype(
        jnp.bfloat16
    )
    input_grad = input_grad.reshape(slab_frames, tile_rows, width_cells, channels)
    return (out_slab, input_grad, weight_grad)


def solution(mesh):
    return jax.shard_map(
        per_device,
        mesh=mesh,
        in_specs=(
            P(("clip", "frame"), "tile", None, None),
            P(("clip", "frame"), "tile", None, None),
            P(),
            P(),
        ),
        out_specs=(
            P(("clip", "frame"), "tile", None, None),
            P(("clip", "frame"), "tile", None, None),
            P(("clip", "frame", "tile"), None),
        ),
        check_vma=False,
    )
```

```python
import functools
import math

import jax
import jax.numpy as jnp
from jax import lax
from jax.experimental import pallas as pl
from jax.experimental.pallas import tpu as pltpu
from jax.sharding import PartitionSpec as P

TAP_DILATION = 2


def padded_2(block, sides, width):
    for axis, dim in sides:
        count = lax.axis_size(axis)
        forward = [(i, i + 1) for i in range(count - 1)]
        backward = [(target, source) for source, target in forward]
        low = lax.ppermute(
            lax.slice_in_dim(block, block.shape[dim] - width, None, axis=dim), axis, forward
        )
        high = lax.ppermute(lax.slice_in_dim(block, 0, width, axis=dim), axis, backward)
        block = jnp.concatenate([low, block, high], axis=dim)
    return block


def halving_scatter(term, axes):
    sizes = [size for _, size in axes]
    if any(size & (size - 1) for size in sizes):
        return lax.psum_scatter(term, tuple(name for name, _ in axes), scatter_dimension=0, tiled=True)
    bits = []
    for name, size in axes:
        bits += [(name, size, b) for b in reversed(range(size.bit_length() - 1))]
    groups = 1
    for size in sizes:
        groups *= size
    block = term.shape[0] // groups
    x = term.reshape((2,) * len(bits) + (block,) + term.shape[1:])
    for pos in reversed(range(len(bits))):
        name, size, b = bits[pos]
        mine = (lax.axis_index(name) >> b) & 1
        keep = lax.dynamic_index_in_dim(x, mine, axis=pos, keepdims=False)
        send = lax.dynamic_index_in_dim(x, 1 - mine, axis=pos, keepdims=False)
        pairs = [(i, i ^ (1 << b)) for i in range(size)]
        x = keep + lax.ppermute(send, name, pairs)
    return x


def halving_kernel(groups, narrow, x_ref, o_ref, *scratch):
    n = len(groups)
    send_sems, recv_sems = scratch[-2], scratch[-1]
    landings = scratch[:n]
    accs = scratch[n : 2 * n - 1]
    packs = scratch[2 * n - 1 : 2 * n - 1 + narrow]
    mesh_ids = pl.DeviceIdType.MESH
    plan = []
    for name, group_bits in groups:
        me = lax.axis_index(name)
        mine = [(me // (1 << b)) % 2 for b in group_bits]
        width = len(group_bits)
        own = 0
        for bit in mine:
            own = own * 2 + bit
        peers = []
        for mask in range(1, 1 << width):
            flips = [(mask >> (width - 1 - j)) % 2 for j in range(width)]
            partner = me
            chunk = 0
            for bit, flip, b in zip(mine, flips, group_bits):
                partner = partner + (1 - 2 * bit) * flip * (1 << b)
                chunk = chunk * 2 + bit + (1 - 2 * bit) * flip
            peers.append((mask, partner, chunk))
        plan.append((name, width, own, peers))
    barrier = pltpu.get_barrier_semaphore()
    contacts = 0
    for name, _, _, peers in plan:
        for _, partner, _ in peers:
            pl.semaphore_signal(barrier, inc=1, device_id={name: partner}, device_id_type=mesh_ids)
            contacts += 1
    pl.semaphore_wait(barrier, contacts)
    source = x_ref
    count = x_ref.shape[0]
    message = 0
    for k, (name, width, own, peers) in enumerate(plan):
        part = count >> width
        outbox = source
        if k < narrow:
            packs[k][...] = source[...].astype(packs[k].dtype)
            outbox = packs[k]
        copies = []
        for mask, partner, chunk in peers:
            copy = pltpu.make_async_remote_copy(
                src_ref=outbox.at[pl.ds(chunk * part, part)],
                dst_ref=landings[k].at[mask - 1],
                send_sem=send_sems.at[message],
                recv_sem=recv_sems.at[message],
                device_id={name: partner},
                device_id_type=mesh_ids,
            )
            copy.start()
            copies.append(copy)
            message += 1
        for copy in copies:
            copy.wait()
        total = source[pl.ds(own * part, part)]
        for slot in range(len(peers)):
            total = total + landings[k][slot].astype(jnp.float32)
        if k == n - 1:
            o_ref[...] = total[0]
        else:
            accs[k][...] = total
            source = accs[k]
        count = part


def kernel_scatter(term, axes):
    sizes = [size for _, size in axes]
    groups = 1
    for size in sizes:
        groups *= size
    per_block = term.shape[0] * term.shape[1] // groups
    if any(size & (size - 1) for size in sizes) or per_block % 128:
        return halving_scatter(term, axes)
    bits = []
    for name, size in axes:
        bits += [(name, b) for b in reversed(range(size.bit_length() - 1))]
    n = len(bits)
    x = term.reshape((2,) * n + (per_block,)).transpose(tuple(reversed(range(n))) + (n,))
    x = x.reshape(groups, per_block // 128, 128)
    steps = list(reversed(bits))
    plan = [(steps[0][0], [steps[0][1]])]
    for name, b in steps[1:]:
        last_name, last_bits = plan[-1]
        if len(plan) > 1 and last_name == name and len(last_bits) == 1:
            last_bits.append(b)
        else:
            plan.append((name, [b]))
    narrow = min(2, len(plan))
    rows = x.shape[1:]
    counts = [x.shape[0]]
    for _, group_bits in plan:
        counts.append(counts[-1] >> len(group_bits))
    scratch = [
        pltpu.VMEM(
            ((1 << len(g[1])) - 1, counts[k + 1]) + rows,
            jnp.bfloat16 if k < narrow else jnp.float32,
        )
        for k, g in enumerate(plan)
    ]
    scratch += [pltpu.VMEM((counts[k + 1],) + rows, jnp.float32) for k in range(len(plan) - 1)]
    scratch += [pltpu.VMEM((counts[k],) + rows, jnp.bfloat16) for k in range(narrow)]
    messages = sum((1 << len(g[1])) - 1 for g in plan)
    scratch += [pltpu.SemaphoreType.DMA((messages,)), pltpu.SemaphoreType.DMA((messages,))]
    out = pl.pallas_call(
        functools.partial(halving_kernel, plan, narrow),
        out_shape=jax.ShapeDtypeStruct(rows, x.dtype),
        in_specs=[pl.BlockSpec(memory_space=pltpu.VMEM)],
        out_specs=pl.BlockSpec(memory_space=pltpu.VMEM),
        scratch_shapes=scratch,
        compiler_params=pltpu.CompilerParams(collective_id=0, has_side_effects=True),
    )(x)
    return out.reshape(term.shape[0] // groups, term.shape[1])


def tile_columns(extended, tile_rows, width_cells, backward_pass):
    padded = jnp.pad(extended, ((0, 0), (0, 0), (1, 1), (0, 0)))
    pieces = []
    for row_shift in range(3):
        for col_shift in range(3):
            row_start = 2 - row_shift if backward_pass else row_shift
            col_start = 2 - col_shift if backward_pass else col_shift
            pieces.append(
                padded[:, row_start : row_start + tile_rows, col_start : col_start + width_cells, :]
            )
    channels = extended.shape[3]
    return jnp.concatenate(pieces, axis=-1).reshape(-1, 9 * channels)


def temporal_taps(padded_seq, weight, frame_count, backward_pass):
    pieces = []
    for temporal_tap_index in range(9):
        first_frame_index = (
            (8 - temporal_tap_index) * TAP_DILATION
            if backward_pass
            else temporal_tap_index * TAP_DILATION
        )
        pieces.append(padded_seq[first_frame_index : first_frame_index + frame_count])
    channels = padded_seq.shape[2]
    columns = jnp.concatenate(pieces, axis=-1).reshape(-1, 9 * channels)
    return jnp.dot(columns, weight, preferred_element_type=jnp.float32)


def frame_exchange(clip_feats, out_grad, act, temporal_weight, temporal_back, temporal_reach):
    slab_frames, tile_rows, width_cells, channels = clip_feats.shape
    row_count = slab_frames * tile_rows * width_cells
    frame_devs = lax.axis_size("frame")
    per_group = tile_rows * width_cells // frame_devs
    grouped = (slab_frames, frame_devs, per_group, channels)
    act_part = lax.all_to_all(
        act.reshape(grouped), "frame", split_axis=1, concat_axis=0, tiled=True
    )
    grad_part = lax.all_to_all(out_grad, "frame", split_axis=1, concat_axis=0, tiled=True)
    feat_part = lax.all_to_all(clip_feats, "frame", split_axis=1, concat_axis=0, tiled=True)
    frame_count = act_part.shape[0]
    item_count = act_part.shape[2]
    act_pad = jnp.pad(
        act_part.reshape(frame_count, item_count, channels),
        ((temporal_reach, temporal_reach), (0, 0), (0, 0)),
    )
    grad_pad = jnp.pad(
        grad_part.reshape(frame_count, item_count, channels),
        ((temporal_reach, temporal_reach), (0, 0), (0, 0)),
    )
    mixed = temporal_taps(act_pad, temporal_weight, frame_count, False)
    out_part = (feat_part.reshape(-1, channels).astype(jnp.float32) + mixed).astype(jnp.bfloat16)
    back_part = temporal_taps(grad_pad, temporal_back, frame_count, True).astype(jnp.bfloat16)
    out_part = out_part.reshape(frame_count, 1, item_count, channels)
    back_part = back_part.reshape(frame_count, 1, item_count, channels)
    out_slab = lax.all_to_all(out_part, "frame", split_axis=0, concat_axis=1, tiled=True)
    grad_slab = lax.all_to_all(back_part, "frame", split_axis=0, concat_axis=1, tiled=True)
    act_grad = grad_slab.reshape(row_count, channels)
    return out_slab, act_grad


def per_device(clip_feats, out_grad, spatial_weight, temporal_weight):
    slab_frames, tile_rows, width_cells, channels = clip_feats.shape
    row_count = slab_frames * tile_rows * width_cells
    frame_devs = lax.axis_size("frame")
    tile_devs = lax.axis_size("tile")
    grad_scale = jnp.float32(
        1.0 / math.sqrt(slab_frames * frame_devs * tile_rows * tile_devs * width_cells)
    )
    spatial_back = (
        spatial_weight.reshape(9, channels, channels)
        .transpose(0, 2, 1)
        .reshape(9 * channels, channels)
    )
    temporal_back = (
        temporal_weight.reshape(9, channels, channels)
        .transpose(0, 2, 1)
        .reshape(9 * channels, channels)
    )
    feat_ext = padded_2(clip_feats, (("tile", 1),), 1)
    feat_columns = tile_columns(feat_ext, tile_rows, width_cells, False)
    pre = jnp.dot(feat_columns, spatial_weight, preferred_element_type=jnp.float32)
    act = jax.nn.silu(pre).astype(jnp.bfloat16)
    temporal_reach = 4 * TAP_DILATION
    if temporal_reach <= slab_frames:
        seq_shape = (slab_frames, tile_rows * width_cells, channels)
        act_ext = padded_2(act.reshape(seq_shape), (("frame", 0),), temporal_reach)
        grad_ext = padded_2(out_grad.reshape(seq_shape), (("frame", 0),), temporal_reach)
        act_grad = temporal_taps(grad_ext, temporal_back, slab_frames, True).astype(jnp.bfloat16)
        mixed = temporal_taps(act_ext, temporal_weight, slab_frames, False)
        out_slab = (clip_feats.reshape(-1, channels).astype(jnp.float32) + mixed).astype(
            jnp.bfloat16
        )
        out_slab = out_slab.reshape(clip_feats.shape)
    else:
        out_slab, act_grad = frame_exchange(
            clip_feats, out_grad, act, temporal_weight, temporal_back, temporal_reach
        )
    sig = jax.nn.sigmoid(pre)
    pre_grad = (act_grad.astype(jnp.float32) * (sig * (1.0 + pre * (1.0 - sig)))).astype(
        jnp.bfloat16
    )
    full_term = lax.dot_general(
        feat_columns, pre_grad, (((0,), (0,)), ((), ())), preferred_element_type=jnp.float32
    )
    summed = kernel_scatter(full_term, (("frame", frame_devs), ("tile", tile_devs)))
    weight_grad = summed * grad_scale
    grad_ext = padded_2(
        pre_grad.reshape(slab_frames, tile_rows, width_cells, channels), (("tile", 1),), 1
    )
    grad_columns = tile_columns(grad_ext, tile_rows, width_cells, True)
    local_back = jnp.dot(grad_columns, spatial_back, preferred_element_type=jnp.float32)
    input_grad = (out_grad.reshape(row_count, channels).astype(jnp.float32) + local_back).astype(
        jnp.bfloat16
    )
    input_grad = input_grad.reshape(slab_frames, tile_rows, width_cells, channels)
    return (out_slab, input_grad, weight_grad)


def solution(mesh):
    return jax.shard_map(
        per_device,
        mesh=mesh,
        in_specs=(
            P(("clip", "frame"), "tile", None, None),
            P(("clip", "frame"), "tile", None, None),
            P(),
            P(),
        ),
        out_specs=(
            P(("clip", "frame"), "tile", None, None),
            P(("clip", "frame"), "tile", None, None),
            P(("clip", "frame", "tile"), None),
        ),
        check_vma=False,
    )
```

```python
import functools
import math

import jax
import jax.numpy as jnp
from jax import lax
from jax.experimental import pallas as pl
from jax.experimental.pallas import tpu as pltpu
from jax.sharding import PartitionSpec as P

TAP_DILATION = 2


def padded_2(block, sides, width):
    for axis, dim in sides:
        count = lax.axis_size(axis)
        forward = [(i, i + 1) for i in range(count - 1)]
        backward = [(target, source) for source, target in forward]
        low = lax.ppermute(
            lax.slice_in_dim(block, block.shape[dim] - width, None, axis=dim), axis, forward
        )
        high = lax.ppermute(lax.slice_in_dim(block, 0, width, axis=dim), axis, backward)
        block = jnp.concatenate([low, block, high], axis=dim)
    return block


def halving_scatter(term, axes):
    sizes = [size for _, size in axes]
    if any(size & (size - 1) for size in sizes):
        return lax.psum_scatter(term, tuple(name for name, _ in axes), scatter_dimension=0, tiled=True)
    bits = []
    for name, size in axes:
        bits += [(name, size, b) for b in reversed(range(size.bit_length() - 1))]
    groups = 1
    for size in sizes:
        groups *= size
    block = term.shape[0] // groups
    x = term.reshape((2,) * len(bits) + (block,) + term.shape[1:])
    for pos in reversed(range(len(bits))):
        name, size, b = bits[pos]
        mine = (lax.axis_index(name) >> b) & 1
        keep = lax.dynamic_index_in_dim(x, mine, axis=pos, keepdims=False)
        send = lax.dynamic_index_in_dim(x, 1 - mine, axis=pos, keepdims=False)
        pairs = [(i, i ^ (1 << b)) for i in range(size)]
        x = keep + lax.ppermute(send, name, pairs)
    return x


def halving_kernel(groups, narrow, x_ref, o_ref, *scratch):
    n = len(groups)
    send_sems, recv_sems = scratch[-2], scratch[-1]
    landings = scratch[:n]
    accs = scratch[n : 2 * n - 1]
    packs = scratch[2 * n - 1 : 2 * n - 1 + narrow]
    mesh_ids = pl.DeviceIdType.MESH
    plan = []
    for group_bits in groups:
        here = {name: lax.axis_index(name) for name, _ in group_bits}
        mine = [(here[name] // (1 << b)) % 2 for name, b in group_bits]
        width = len(group_bits)
        own = 0
        for bit in mine:
            own = own * 2 + bit
        peers = []
        for mask in range(1, 1 << width):
            flips = [(mask >> (width - 1 - j)) % 2 for j in range(width)]
            partner = dict(here)
            chunk = 0
            for bit, flip, (name, b) in zip(mine, flips, group_bits):
                partner[name] = partner[name] + (1 - 2 * bit) * flip * (1 << b)
                chunk = chunk * 2 + bit + (1 - 2 * bit) * flip
            peers.append((mask, partner, chunk))
        plan.append((width, own, peers))
    barrier = pltpu.get_barrier_semaphore()
    contacts = 0
    for _, _, peers in plan:
        for _, partner, _ in peers:
            pl.semaphore_signal(barrier, inc=1, device_id=partner, device_id_type=mesh_ids)
            contacts += 1
    pl.semaphore_wait(barrier, contacts)
    source = x_ref
    count = x_ref.shape[0]
    message = 0
    for k, (width, own, peers) in enumerate(plan):
        part = count >> width
        outbox = source
        if k < narrow:
            packs[k][...] = source[...].astype(packs[k].dtype)
            outbox = packs[k]
        copies = []
        for mask, partner, chunk in peers:
            copy = pltpu.make_async_remote_copy(
                src_ref=outbox.at[pl.ds(chunk * part, part)],
                dst_ref=landings[k].at[mask - 1],
                send_sem=send_sems.at[message],
                recv_sem=recv_sems.at[message],
                device_id=partner,
                device_id_type=mesh_ids,
            )
            copy.start()
            copies.append(copy)
            message += 1
        for copy in copies:
            copy.wait()
        total = source[pl.ds(own * part, part)]
        for slot in range(len(peers)):
            total = total + landings[k][slot].astype(jnp.float32)
        if k == n - 1:
            o_ref[...] = total[0]
        else:
            accs[k][...] = total
            source = accs[k]
        count = part


def kernel_scatter(term, axes):
    sizes = [size for _, size in axes]
    groups = 1
    for size in sizes:
        groups *= size
    per_block = term.shape[0] * term.shape[1] // groups
    if any(size & (size - 1) for size in sizes) or per_block % 128:
        return halving_scatter(term, axes)
    bits = []
    for name, size in axes:
        bits += [(name, b) for b in reversed(range(size.bit_length() - 1))]
    n = len(bits)
    x = term.reshape((2,) * n + (per_block,)).transpose(tuple(reversed(range(n))) + (n,))
    x = x.reshape(groups, per_block // 128, 128)
    steps = list(reversed(bits))
    plan = [steps[:1]] + [steps[i : i + 3] for i in range(1, len(steps), 3)]
    narrow = min(2, len(plan))
    rows = x.shape[1:]
    counts = [x.shape[0]]
    for group_bits in plan:
        counts.append(counts[-1] >> len(group_bits))
    scratch = [
        pltpu.VMEM(
            ((1 << len(g)) - 1, counts[k + 1]) + rows,
            jnp.bfloat16 if k < narrow else jnp.float32,
        )
        for k, g in enumerate(plan)
    ]
    scratch += [pltpu.VMEM((counts[k + 1],) + rows, jnp.float32) for k in range(len(plan) - 1)]
    scratch += [pltpu.VMEM((counts[k],) + rows, jnp.bfloat16) for k in range(narrow)]
    messages = sum((1 << len(g)) - 1 for g in plan)
    scratch += [pltpu.SemaphoreType.DMA((messages,)), pltpu.SemaphoreType.DMA((messages,))]
    out = pl.pallas_call(
        functools.partial(halving_kernel, plan, narrow),
        out_shape=jax.ShapeDtypeStruct(rows, x.dtype),
        in_specs=[pl.BlockSpec(memory_space=pltpu.VMEM)],
        out_specs=pl.BlockSpec(memory_space=pltpu.VMEM),
        scratch_shapes=scratch,
        compiler_params=pltpu.CompilerParams(collective_id=0, has_side_effects=True),
    )(x)
    return out.reshape(term.shape[0] // groups, term.shape[1])


def tile_columns(extended, tile_rows, width_cells, backward_pass):
    padded = jnp.pad(extended, ((0, 0), (0, 0), (1, 1), (0, 0)))
    pieces = []
    for row_shift in range(3):
        for col_shift in range(3):
            row_start = 2 - row_shift if backward_pass else row_shift
            col_start = 2 - col_shift if backward_pass else col_shift
            pieces.append(
                padded[:, row_start : row_start + tile_rows, col_start : col_start + width_cells, :]
            )
    channels = extended.shape[3]
    return jnp.concatenate(pieces, axis=-1).reshape(-1, 9 * channels)


def temporal_taps(padded_seq, weight, frame_count, backward_pass):
    pieces = []
    for temporal_tap_index in range(9):
        first_frame_index = (
            (8 - temporal_tap_index) * TAP_DILATION
            if backward_pass
            else temporal_tap_index * TAP_DILATION
        )
        pieces.append(padded_seq[first_frame_index : first_frame_index + frame_count])
    channels = padded_seq.shape[2]
    columns = jnp.concatenate(pieces, axis=-1).reshape(-1, 9 * channels)
    return jnp.dot(columns, weight, preferred_element_type=jnp.float32)


def frame_exchange(clip_feats, out_grad, act, temporal_weight, temporal_back, temporal_reach):
    slab_frames, tile_rows, width_cells, channels = clip_feats.shape
    row_count = slab_frames * tile_rows * width_cells
    frame_devs = lax.axis_size("frame")
    per_group = tile_rows * width_cells // frame_devs
    grouped = (slab_frames, frame_devs, per_group, channels)
    act_part = lax.all_to_all(
        act.reshape(grouped), "frame", split_axis=1, concat_axis=0, tiled=True
    )
    grad_part = lax.all_to_all(out_grad, "frame", split_axis=1, concat_axis=0, tiled=True)
    feat_part = lax.all_to_all(clip_feats, "frame", split_axis=1, concat_axis=0, tiled=True)
    frame_count = act_part.shape[0]
    item_count = act_part.shape[2]
    act_pad = jnp.pad(
        act_part.reshape(frame_count, item_count, channels),
        ((temporal_reach, temporal_reach), (0, 0), (0, 0)),
    )
    grad_pad = jnp.pad(
        grad_part.reshape(frame_count, item_count, channels),
        ((temporal_reach, temporal_reach), (0, 0), (0, 0)),
    )
    mixed = temporal_taps(act_pad, temporal_weight, frame_count, False)
    out_part = (feat_part.reshape(-1, channels).astype(jnp.float32) + mixed).astype(jnp.bfloat16)
    back_part = temporal_taps(grad_pad, temporal_back, frame_count, True).astype(jnp.bfloat16)
    out_part = out_part.reshape(frame_count, 1, item_count, channels)
    back_part = back_part.reshape(frame_count, 1, item_count, channels)
    out_slab = lax.all_to_all(out_part, "frame", split_axis=0, concat_axis=1, tiled=True)
    grad_slab = lax.all_to_all(back_part, "frame", split_axis=0, concat_axis=1, tiled=True)
    act_grad = grad_slab.reshape(row_count, channels)
    return out_slab, act_grad


def per_device(clip_feats, out_grad, spatial_weight, temporal_weight):
    slab_frames, tile_rows, width_cells, channels = clip_feats.shape
    row_count = slab_frames * tile_rows * width_cells
    frame_devs = lax.axis_size("frame")
    tile_devs = lax.axis_size("tile")
    grad_scale = jnp.float32(
        1.0 / math.sqrt(slab_frames * frame_devs * tile_rows * tile_devs * width_cells)
    )
    spatial_back = (
        spatial_weight.reshape(9, channels, channels)
        .transpose(0, 2, 1)
        .reshape(9 * channels, channels)
    )
    temporal_back = (
        temporal_weight.reshape(9, channels, channels)
        .transpose(0, 2, 1)
        .reshape(9 * channels, channels)
    )
    feat_ext = padded_2(clip_feats, (("tile", 1),), 1)
    feat_columns = tile_columns(feat_ext, tile_rows, width_cells, False)
    pre = jnp.dot(feat_columns, spatial_weight, preferred_element_type=jnp.float32)
    act = jax.nn.silu(pre).astype(jnp.bfloat16)
    temporal_reach = 4 * TAP_DILATION
    if temporal_reach <= slab_frames:
        seq_shape = (slab_frames, tile_rows * width_cells, channels)
        act_ext = padded_2(act.reshape(seq_shape), (("frame", 0),), temporal_reach)
        grad_ext = padded_2(out_grad.reshape(seq_shape), (("frame", 0),), temporal_reach)
        act_grad = temporal_taps(grad_ext, temporal_back, slab_frames, True).astype(jnp.bfloat16)
        mixed = temporal_taps(act_ext, temporal_weight, slab_frames, False)
        out_slab = (clip_feats.reshape(-1, channels).astype(jnp.float32) + mixed).astype(
            jnp.bfloat16
        )
        out_slab = out_slab.reshape(clip_feats.shape)
    else:
        out_slab, act_grad = frame_exchange(
            clip_feats, out_grad, act, temporal_weight, temporal_back, temporal_reach
        )
    sig = jax.nn.sigmoid(pre)
    pre_grad = (act_grad.astype(jnp.float32) * (sig * (1.0 + pre * (1.0 - sig)))).astype(
        jnp.bfloat16
    )
    full_term = lax.dot_general(
        feat_columns, pre_grad, (((0,), (0,)), ((), ())), preferred_element_type=jnp.float32
    )
    summed = kernel_scatter(full_term, (("frame", frame_devs), ("tile", tile_devs)))
    weight_grad = summed * grad_scale
    grad_ext = padded_2(
        pre_grad.reshape(slab_frames, tile_rows, width_cells, channels), (("tile", 1),), 1
    )
    grad_columns = tile_columns(grad_ext, tile_rows, width_cells, True)
    local_back = jnp.dot(grad_columns, spatial_back, preferred_element_type=jnp.float32)
    input_grad = (out_grad.reshape(row_count, channels).astype(jnp.float32) + local_back).astype(
        jnp.bfloat16
    )
    input_grad = input_grad.reshape(slab_frames, tile_rows, width_cells, channels)
    return (out_slab, input_grad, weight_grad)


def solution(mesh):
    return jax.shard_map(
        per_device,
        mesh=mesh,
        in_specs=(
            P(("clip", "frame"), "tile", None, None),
            P(("clip", "frame"), "tile", None, None),
            P(),
            P(),
        ),
        out_specs=(
            P(("clip", "frame"), "tile", None, None),
            P(("clip", "frame"), "tile", None, None),
            P(("clip", "frame", "tile"), None),
        ),
        check_vma=False,
    )
```

```python
import functools
import math

import jax
import jax.numpy as jnp
from jax import lax
from jax.experimental import pallas as pl
from jax.experimental.pallas import tpu as pltpu
from jax.sharding import PartitionSpec as P

TAP_DILATION = 2


def padded_2(block, sides, width):
    for axis, dim in sides:
        count = lax.axis_size(axis)
        forward = [(i, i + 1) for i in range(count - 1)]
        backward = [(target, source) for source, target in forward]
        low = lax.ppermute(
            lax.slice_in_dim(block, block.shape[dim] - width, None, axis=dim), axis, forward
        )
        high = lax.ppermute(lax.slice_in_dim(block, 0, width, axis=dim), axis, backward)
        block = jnp.concatenate([low, block, high], axis=dim)
    return block


def halving_scatter(term, axes):
    sizes = [size for _, size in axes]
    if any(size & (size - 1) for size in sizes):
        return lax.psum_scatter(term, tuple(name for name, _ in axes), scatter_dimension=0, tiled=True)
    bits = []
    for name, size in axes:
        bits += [(name, size, b) for b in reversed(range(size.bit_length() - 1))]
    groups = 1
    for size in sizes:
        groups *= size
    block = term.shape[0] // groups
    x = term.reshape((2,) * len(bits) + (block,) + term.shape[1:])
    for pos in reversed(range(len(bits))):
        name, size, b = bits[pos]
        mine = (lax.axis_index(name) >> b) & 1
        keep = lax.dynamic_index_in_dim(x, mine, axis=pos, keepdims=False)
        send = lax.dynamic_index_in_dim(x, 1 - mine, axis=pos, keepdims=False)
        pairs = [(i, i ^ (1 << b)) for i in range(size)]
        x = keep + lax.ppermute(send, name, pairs)
    return x


def halving_kernel(groups, narrow, x_ref, o_ref, *scratch):
    n = len(groups)
    send_sems, recv_sems = scratch[-2], scratch[-1]
    landings = scratch[:n]
    accs = scratch[n : 2 * n - 1]
    packs = scratch[2 * n - 1 : 2 * n - 1 + narrow]
    mesh_ids = pl.DeviceIdType.MESH
    plan = []
    for name, group_bits in groups:
        me = lax.axis_index(name)
        mine = [(me // (1 << b)) % 2 for b in group_bits]
        width = len(group_bits)
        own = 0
        for bit in mine:
            own = own * 2 + bit
        peers = []
        for mask in range(1, 1 << width):
            flips = [(mask >> (width - 1 - j)) % 2 for j in range(width)]
            partner = me
            chunk = 0
            for bit, flip, b in zip(mine, flips, group_bits):
                partner = partner + (1 - 2 * bit) * flip * (1 << b)
                chunk = chunk * 2 + bit + (1 - 2 * bit) * flip
            peers.append((mask, partner, chunk))
        plan.append((name, width, own, peers))
    barrier = pltpu.get_barrier_semaphore()
    contacts = 0
    for name, _, _, peers in plan:
        for _, partner, _ in peers:
            pl.semaphore_signal(barrier, inc=1, device_id={name: partner}, device_id_type=mesh_ids)
            contacts += 1
    pl.semaphore_wait(barrier, contacts)
    source = x_ref
    count = x_ref.shape[0]
    message = 0
    for k, (name, width, own, peers) in enumerate(plan):
        part = count >> width
        outbox = source
        if k < narrow:
            packs[k][...] = source[...].astype(packs[k].dtype)
            outbox = packs[k]
        copies = []
        for mask, partner, chunk in peers:
            copy = pltpu.make_async_remote_copy(
                src_ref=outbox.at[pl.ds(chunk * part, part)],
                dst_ref=landings[k].at[mask - 1],
                send_sem=send_sems.at[message],
                recv_sem=recv_sems.at[message],
                device_id={name: partner},
                device_id_type=mesh_ids,
            )
            copy.start()
            copies.append(copy)
            message += 1
        for copy in copies:
            copy.wait()
        total = source[pl.ds(own * part, part)]
        for slot in range(len(peers)):
            total = total + landings[k][slot].astype(jnp.float32)
        if k == n - 1:
            o_ref[...] = total[0]
        else:
            accs[k][...] = total
            source = accs[k]
        count = part


def kernel_scatter(term, axes):
    sizes = [size for _, size in axes]
    groups = 1
    for size in sizes:
        groups *= size
    per_block = term.shape[0] * term.shape[1] // groups
    if any(size & (size - 1) for size in sizes) or per_block % 128:
        return halving_scatter(term, axes)
    bits = []
    for name, size in axes:
        bits += [(name, b) for b in reversed(range(size.bit_length() - 1))]
    n = len(bits)
    x = term.reshape((2,) * n + (per_block // 128, 128))
    x = x.transpose(tuple(reversed(range(n))) + (n, n + 1)).reshape(groups, per_block // 128, 128)
    steps = list(reversed(bits))
    plan = [(steps[0][0], [steps[0][1]])]
    for name, b in steps[1:]:
        last_name, last_bits = plan[-1]
        if len(plan) > 1 and last_name == name and len(last_bits) == 1:
            last_bits.append(b)
        else:
            plan.append((name, [b]))
    narrow = min(2, len(plan))
    rows = x.shape[1:]
    counts = [x.shape[0]]
    for _, group_bits in plan:
        counts.append(counts[-1] >> len(group_bits))
    scratch = [
        pltpu.VMEM(
            ((1 << len(g[1])) - 1, counts[k + 1]) + rows,
            jnp.bfloat16 if k < narrow else jnp.float32,
        )
        for k, g in enumerate(plan)
    ]
    scratch += [pltpu.VMEM((counts[k + 1],) + rows, jnp.float32) for k in range(len(plan) - 1)]
    scratch += [pltpu.VMEM((counts[k],) + rows, jnp.bfloat16) for k in range(narrow)]
    messages = sum((1 << len(g[1])) - 1 for g in plan)
    scratch += [pltpu.SemaphoreType.DMA((messages,)), pltpu.SemaphoreType.DMA((messages,))]
    out = pl.pallas_call(
        functools.partial(halving_kernel, plan, narrow),
        out_shape=jax.ShapeDtypeStruct(rows, x.dtype),
        in_specs=[pl.BlockSpec(memory_space=pltpu.VMEM)],
        out_specs=pl.BlockSpec(memory_space=pltpu.VMEM),
        scratch_shapes=scratch,
        compiler_params=pltpu.CompilerParams(collective_id=0, has_side_effects=True),
    )(x)
    return out.reshape(term.shape[0] // groups, term.shape[1])


def tile_columns(extended, tile_rows, width_cells, backward_pass):
    padded = jnp.pad(extended, ((0, 0), (0, 0), (1, 1), (0, 0)))
    pieces = []
    for row_shift in range(3):
        for col_shift in range(3):
            row_start = 2 - row_shift if backward_pass else row_shift
            col_start = 2 - col_shift if backward_pass else col_shift
            pieces.append(
                padded[:, row_start : row_start + tile_rows, col_start : col_start + width_cells, :]
            )
    channels = extended.shape[3]
    return jnp.concatenate(pieces, axis=-1).reshape(-1, 9 * channels)


def temporal_taps(padded_seq, weight, frame_count, backward_pass):
    pieces = []
    for temporal_tap_index in range(9):
        first_frame_index = (
            (8 - temporal_tap_index) * TAP_DILATION
            if backward_pass
            else temporal_tap_index * TAP_DILATION
        )
        pieces.append(padded_seq[first_frame_index : first_frame_index + frame_count])
    channels = padded_seq.shape[2]
    columns = jnp.concatenate(pieces, axis=-1).reshape(-1, 9 * channels)
    return jnp.dot(columns, weight, preferred_element_type=jnp.float32)


def frame_exchange(clip_feats, out_grad, act, temporal_weight, temporal_back, temporal_reach):
    slab_frames, tile_rows, width_cells, channels = clip_feats.shape
    row_count = slab_frames * tile_rows * width_cells
    frame_devs = lax.axis_size("frame")
    per_group = tile_rows * width_cells // frame_devs
    grouped = (slab_frames, frame_devs, per_group, channels)
    act_part = lax.all_to_all(
        act.reshape(grouped), "frame", split_axis=1, concat_axis=0, tiled=True
    )
    grad_part = lax.all_to_all(out_grad, "frame", split_axis=1, concat_axis=0, tiled=True)
    feat_part = lax.all_to_all(clip_feats, "frame", split_axis=1, concat_axis=0, tiled=True)
    frame_count = act_part.shape[0]
    item_count = act_part.shape[2]
    act_pad = jnp.pad(
        act_part.reshape(frame_count, item_count, channels),
        ((temporal_reach, temporal_reach), (0, 0), (0, 0)),
    )
    grad_pad = jnp.pad(
        grad_part.reshape(frame_count, item_count, channels),
        ((temporal_reach, temporal_reach), (0, 0), (0, 0)),
    )
    mixed = temporal_taps(act_pad, temporal_weight, frame_count, False)
    out_part = (feat_part.reshape(-1, channels).astype(jnp.float32) + mixed).astype(jnp.bfloat16)
    back_part = temporal_taps(grad_pad, temporal_back, frame_count, True).astype(jnp.bfloat16)
    out_part = out_part.reshape(frame_count, 1, item_count, channels)
    back_part = back_part.reshape(frame_count, 1, item_count, channels)
    out_slab = lax.all_to_all(out_part, "frame", split_axis=0, concat_axis=1, tiled=True)
    grad_slab = lax.all_to_all(back_part, "frame", split_axis=0, concat_axis=1, tiled=True)
    act_grad = grad_slab.reshape(row_count, channels)
    return out_slab, act_grad


def per_device(clip_feats, out_grad, spatial_weight, temporal_weight):
    slab_frames, tile_rows, width_cells, channels = clip_feats.shape
    row_count = slab_frames * tile_rows * width_cells
    frame_devs = lax.axis_size("frame")
    tile_devs = lax.axis_size("tile")
    grad_scale = jnp.float32(
        1.0 / math.sqrt(slab_frames * frame_devs * tile_rows * tile_devs * width_cells)
    )
    spatial_back = (
        spatial_weight.reshape(9, channels, channels)
        .transpose(0, 2, 1)
        .reshape(9 * channels, channels)
    )
    temporal_back = (
        temporal_weight.reshape(9, channels, channels)
        .transpose(0, 2, 1)
        .reshape(9 * channels, channels)
    )
    feat_ext = padded_2(clip_feats, (("tile", 1),), 1)
    feat_columns = tile_columns(feat_ext, tile_rows, width_cells, False)
    pre = jnp.dot(feat_columns, spatial_weight, preferred_element_type=jnp.float32)
    act = jax.nn.silu(pre).astype(jnp.bfloat16)
    temporal_reach = 4 * TAP_DILATION
    if temporal_reach <= slab_frames:
        seq_shape = (slab_frames, tile_rows * width_cells, channels)
        act_ext = padded_2(act.reshape(seq_shape), (("frame", 0),), temporal_reach)
        grad_ext = padded_2(out_grad.reshape(seq_shape), (("frame", 0),), temporal_reach)
        act_grad = temporal_taps(grad_ext, temporal_back, slab_frames, True).astype(jnp.bfloat16)
        mixed = temporal_taps(act_ext, temporal_weight, slab_frames, False)
        out_slab = (clip_feats.reshape(-1, channels).astype(jnp.float32) + mixed).astype(
            jnp.bfloat16
        )
        out_slab = out_slab.reshape(clip_feats.shape)
    else:
        out_slab, act_grad = frame_exchange(
            clip_feats, out_grad, act, temporal_weight, temporal_back, temporal_reach
        )
    sig = jax.nn.sigmoid(pre)
    pre_grad = (act_grad.astype(jnp.float32) * (sig * (1.0 + pre * (1.0 - sig)))).astype(
        jnp.bfloat16
    )
    full_term = lax.dot_general(
        feat_columns, pre_grad, (((0,), (0,)), ((), ())), preferred_element_type=jnp.float32
    )
    summed = kernel_scatter(full_term, (("frame", frame_devs), ("tile", tile_devs)))
    weight_grad = summed * grad_scale
    grad_ext = padded_2(
        pre_grad.reshape(slab_frames, tile_rows, width_cells, channels), (("tile", 1),), 1
    )
    grad_columns = tile_columns(grad_ext, tile_rows, width_cells, True)
    local_back = jnp.dot(grad_columns, spatial_back, preferred_element_type=jnp.float32)
    input_grad = (out_grad.reshape(row_count, channels).astype(jnp.float32) + local_back).astype(
        jnp.bfloat16
    )
    input_grad = input_grad.reshape(slab_frames, tile_rows, width_cells, channels)
    return (out_slab, input_grad, weight_grad)


def solution(mesh):
    return jax.shard_map(
        per_device,
        mesh=mesh,
        in_specs=(
            P(("clip", "frame"), "tile", None, None),
            P(("clip", "frame"), "tile", None, None),
            P(),
            P(),
        ),
        out_specs=(
            P(("clip", "frame"), "tile", None, None),
            P(("clip", "frame"), "tile", None, None),
            P(("clip", "frame", "tile"), None),
        ),
        check_vma=False,
    )
```

```python
import functools
import math

import jax
import jax.numpy as jnp
from jax import lax
from jax.experimental import pallas as pl
from jax.experimental.pallas import tpu as pltpu
from jax.sharding import PartitionSpec as P

TAP_DILATION = 2


def padded_2(block, sides, width):
    for axis, dim in sides:
        count = lax.axis_size(axis)
        forward = [(i, i + 1) for i in range(count - 1)]
        backward = [(target, source) for source, target in forward]
        low = lax.ppermute(
            lax.slice_in_dim(block, block.shape[dim] - width, None, axis=dim), axis, forward
        )
        high = lax.ppermute(lax.slice_in_dim(block, 0, width, axis=dim), axis, backward)
        block = jnp.concatenate([low, block, high], axis=dim)
    return block


def halving_scatter(term, axes):
    sizes = [size for _, size in axes]
    if any(size & (size - 1) for size in sizes):
        return lax.psum_scatter(term, tuple(name for name, _ in axes), scatter_dimension=0, tiled=True)
    bits = []
    for name, size in axes:
        bits += [(name, size, b) for b in reversed(range(size.bit_length() - 1))]
    groups = 1
    for size in sizes:
        groups *= size
    block = term.shape[0] // groups
    x = term.reshape((2,) * len(bits) + (block,) + term.shape[1:])
    for pos in reversed(range(len(bits))):
        name, size, b = bits[pos]
        mine = (lax.axis_index(name) >> b) & 1
        keep = lax.dynamic_index_in_dim(x, mine, axis=pos, keepdims=False)
        send = lax.dynamic_index_in_dim(x, 1 - mine, axis=pos, keepdims=False)
        pairs = [(i, i ^ (1 << b)) for i in range(size)]
        x = keep + lax.ppermute(send, name, pairs)
    return x


def halving_kernel(groups, narrow, x_ref, cols_ref, w_ref, base_ref, o_ref, side_ref, *scratch):
    n = len(groups)
    send_sems, recv_sems = scratch[-2], scratch[-1]
    landings = scratch[:n]
    accs = scratch[n : 2 * n - 1]
    packs = scratch[2 * n - 1 : 2 * n - 1 + narrow]
    mesh_ids = pl.DeviceIdType.MESH
    plan = []
    for name, group_bits in groups:
        me = lax.axis_index(name)
        mine = [(me // (1 << b)) % 2 for b in group_bits]
        width = len(group_bits)
        own = 0
        for bit in mine:
            own = own * 2 + bit
        peers = []
        for mask in range(1, 1 << width):
            flips = [(mask >> (width - 1 - j)) % 2 for j in range(width)]
            partner = me
            chunk = 0
            for bit, flip, b in zip(mine, flips, group_bits):
                partner = partner + (1 - 2 * bit) * flip * (1 << b)
                chunk = chunk * 2 + bit + (1 - 2 * bit) * flip
            peers.append((mask, partner, chunk))
        plan.append((name, width, own, peers))
    barrier = pltpu.get_barrier_semaphore()
    contacts = 0
    for name, _, _, peers in plan:
        for _, partner, _ in peers:
            pl.semaphore_signal(barrier, inc=1, device_id={name: partner}, device_id_type=mesh_ids)
            contacts += 1
    pl.semaphore_wait(barrier, contacts)
    source = x_ref
    count = x_ref.shape[0]
    message = 0
    side_rows = cols_ref.shape[0]
    pieces = 4 if side_rows % (4 * 8) == 0 else 1
    piece = side_rows // pieces
    for k, (name, width, own, peers) in enumerate(plan):
        part = count >> width
        outbox = source
        if k < narrow:
            packs[k][...] = source[...].astype(packs[k].dtype)
            outbox = packs[k]
        copies = []
        for mask, partner, chunk in peers:
            copy = pltpu.make_async_remote_copy(
                src_ref=outbox.at[pl.ds(chunk * part, part)],
                dst_ref=landings[k].at[mask - 1],
                send_sem=send_sems.at[message],
                recv_sem=recv_sems.at[message],
                device_id={name: partner},
                device_id_type=mesh_ids,
            )
            copy.start()
            copies.append(copy)
            message += 1
        for p in range(k * pieces // n, (k + 1) * pieces // n):
            span = pl.ds(p * piece, piece)
            local = jnp.dot(cols_ref[span, :], w_ref[...], preferred_element_type=jnp.float32)
            side_ref[span, :] = (base_ref[span, :].astype(jnp.float32) + local).astype(side_ref.dtype)
        for copy in copies:
            copy.wait()
        total = source[pl.ds(own * part, part)]
        for slot in range(len(peers)):
            total = total + landings[k][slot].astype(jnp.float32)
        if k == n - 1:
            o_ref[...] = total[0]
        else:
            accs[k][...] = total
            source = accs[k]
        count = part


def side_product(columns, weight, base):
    local = jnp.dot(columns, weight, preferred_element_type=jnp.float32)
    return (base.astype(jnp.float32) + local).astype(base.dtype)


def kernel_scatter(term, axes, side):
    sizes = [size for _, size in axes]
    groups = 1
    for size in sizes:
        groups *= size
    per_block = term.shape[0] * term.shape[1] // groups
    side_rows = side[0].shape[0]
    if any(size & (size - 1) for size in sizes) or per_block % 128 or side_rows % 32:
        return halving_scatter(term, axes), side_product(*side)
    bits = []
    for name, size in axes:
        bits += [(name, b) for b in reversed(range(size.bit_length() - 1))]
    n = len(bits)
    x = term.reshape((2,) * n + (per_block // 128, 128))
    x = x.transpose(tuple(reversed(range(n))) + (n, n + 1)).reshape(groups, per_block // 128, 128)
    steps = list(reversed(bits))
    plan = [(steps[0][0], [steps[0][1]])]
    for name, b in steps[1:]:
        last_name, last_bits = plan[-1]
        if len(plan) > 1 and last_name == name and len(last_bits) == 1:
            last_bits.append(b)
        else:
            plan.append((name, [b]))
    narrow = min(2, len(plan))
    rows = x.shape[1:]
    counts = [x.shape[0]]
    for _, group_bits in plan:
        counts.append(counts[-1] >> len(group_bits))
    scratch = [
        pltpu.VMEM(
            ((1 << len(g[1])) - 1, counts[k + 1]) + rows,
            jnp.bfloat16 if k < narrow else jnp.float32,
        )
        for k, g in enumerate(plan)
    ]
    scratch += [pltpu.VMEM((counts[k + 1],) + rows, jnp.float32) for k in range(len(plan) - 1)]
    scratch += [pltpu.VMEM((counts[k],) + rows, jnp.bfloat16) for k in range(narrow)]
    messages = sum((1 << len(g[1])) - 1 for g in plan)
    scratch += [pltpu.SemaphoreType.DMA((messages,)), pltpu.SemaphoreType.DMA((messages,))]
    vmem = pl.BlockSpec(memory_space=pltpu.VMEM)
    out, side_out = pl.pallas_call(
        functools.partial(halving_kernel, plan, narrow),
        out_shape=(
            jax.ShapeDtypeStruct(rows, x.dtype),
            jax.ShapeDtypeStruct(side[2].shape, side[2].dtype),
        ),
        in_specs=[vmem] * 4,
        out_specs=(vmem, vmem),
        scratch_shapes=scratch,
        compiler_params=pltpu.CompilerParams(collective_id=0, has_side_effects=True),
    )(x, *side)
    return out.reshape(term.shape[0] // groups, term.shape[1]), side_out


def tile_columns(extended, tile_rows, width_cells, backward_pass):
    padded = jnp.pad(extended, ((0, 0), (0, 0), (1, 1), (0, 0)))
    pieces = []
    for row_shift in range(3):
        for col_shift in range(3):
            row_start = 2 - row_shift if backward_pass else row_shift
            col_start = 2 - col_shift if backward_pass else col_shift
            pieces.append(
                padded[:, row_start : row_start + tile_rows, col_start : col_start + width_cells, :]
            )
    channels = extended.shape[3]
    return jnp.concatenate(pieces, axis=-1).reshape(-1, 9 * channels)


def temporal_taps(padded_seq, weight, frame_count, backward_pass):
    pieces = []
    for temporal_tap_index in range(9):
        first_frame_index = (
            (8 - temporal_tap_index) * TAP_DILATION
            if backward_pass
            else temporal_tap_index * TAP_DILATION
        )
        pieces.append(padded_seq[first_frame_index : first_frame_index + frame_count])
    channels = padded_seq.shape[2]
    columns = jnp.concatenate(pieces, axis=-1).reshape(-1, 9 * channels)
    return jnp.dot(columns, weight, preferred_element_type=jnp.float32)


def frame_exchange(clip_feats, out_grad, act, temporal_weight, temporal_back, temporal_reach):
    slab_frames, tile_rows, width_cells, channels = clip_feats.shape
    row_count = slab_frames * tile_rows * width_cells
    frame_devs = lax.axis_size("frame")
    per_group = tile_rows * width_cells // frame_devs
    grouped = (slab_frames, frame_devs, per_group, channels)
    act_part = lax.all_to_all(
        act.reshape(grouped), "frame", split_axis=1, concat_axis=0, tiled=True
    )
    grad_part = lax.all_to_all(out_grad, "frame", split_axis=1, concat_axis=0, tiled=True)
    feat_part = lax.all_to_all(clip_feats, "frame", split_axis=1, concat_axis=0, tiled=True)
    frame_count = act_part.shape[0]
    item_count = act_part.shape[2]
    act_pad = jnp.pad(
        act_part.reshape(frame_count, item_count, channels),
        ((temporal_reach, temporal_reach), (0, 0), (0, 0)),
    )
    grad_pad = jnp.pad(
        grad_part.reshape(frame_count, item_count, channels),
        ((temporal_reach, temporal_reach), (0, 0), (0, 0)),
    )
    mixed = temporal_taps(act_pad, temporal_weight, frame_count, False)
    out_part = (feat_part.reshape(-1, channels).astype(jnp.float32) + mixed).astype(jnp.bfloat16)
    back_part = temporal_taps(grad_pad, temporal_back, frame_count, True).astype(jnp.bfloat16)
    out_part = out_part.reshape(frame_count, 1, item_count, channels)
    back_part = back_part.reshape(frame_count, 1, item_count, channels)
    out_slab = lax.all_to_all(out_part, "frame", split_axis=0, concat_axis=1, tiled=True)
    grad_slab = lax.all_to_all(back_part, "frame", split_axis=0, concat_axis=1, tiled=True)
    act_grad = grad_slab.reshape(row_count, channels)
    return out_slab, act_grad


def per_device(clip_feats, out_grad, spatial_weight, temporal_weight):
    slab_frames, tile_rows, width_cells, channels = clip_feats.shape
    row_count = slab_frames * tile_rows * width_cells
    frame_devs = lax.axis_size("frame")
    tile_devs = lax.axis_size("tile")
    grad_scale = jnp.float32(
        1.0 / math.sqrt(slab_frames * frame_devs * tile_rows * tile_devs * width_cells)
    )
    spatial_back = (
        spatial_weight.reshape(9, channels, channels)
        .transpose(0, 2, 1)
        .reshape(9 * channels, channels)
    )
    temporal_back = (
        temporal_weight.reshape(9, channels, channels)
        .transpose(0, 2, 1)
        .reshape(9 * channels, channels)
    )
    feat_ext = padded_2(clip_feats, (("tile", 1),), 1)
    feat_columns = tile_columns(feat_ext, tile_rows, width_cells, False)
    pre = jnp.dot(feat_columns, spatial_weight, preferred_element_type=jnp.float32)
    act = jax.nn.silu(pre).astype(jnp.bfloat16)
    temporal_reach = 4 * TAP_DILATION
    if temporal_reach <= slab_frames:
        seq_shape = (slab_frames, tile_rows * width_cells, channels)
        act_ext = padded_2(act.reshape(seq_shape), (("frame", 0),), temporal_reach)
        grad_ext = padded_2(out_grad.reshape(seq_shape), (("frame", 0),), temporal_reach)
        act_grad = temporal_taps(grad_ext, temporal_back, slab_frames, True).astype(jnp.bfloat16)
        mixed = temporal_taps(act_ext, temporal_weight, slab_frames, False)
        out_slab = (clip_feats.reshape(-1, channels).astype(jnp.float32) + mixed).astype(
            jnp.bfloat16
        )
        out_slab = out_slab.reshape(clip_feats.shape)
    else:
        out_slab, act_grad = frame_exchange(
            clip_feats, out_grad, act, temporal_weight, temporal_back, temporal_reach
        )
    sig = jax.nn.sigmoid(pre)
    pre_grad = (act_grad.astype(jnp.float32) * (sig * (1.0 + pre * (1.0 - sig)))).astype(
        jnp.bfloat16
    )
    full_term = lax.dot_general(
        feat_columns, pre_grad, (((0,), (0,)), ((), ())), preferred_element_type=jnp.float32
    )
    grad_ext = padded_2(
        pre_grad.reshape(slab_frames, tile_rows, width_cells, channels), (("tile", 1),), 1
    )
    grad_columns = tile_columns(grad_ext, tile_rows, width_cells, True)
    side = (grad_columns, spatial_back, out_grad.reshape(row_count, channels))
    summed, input_grad = kernel_scatter(
        full_term, (("frame", frame_devs), ("tile", tile_devs)), side
    )
    weight_grad = summed * grad_scale
    input_grad = input_grad.reshape(slab_frames, tile_rows, width_cells, channels)
    return (out_slab, input_grad, weight_grad)


def solution(mesh):
    return jax.shard_map(
        per_device,
        mesh=mesh,
        in_specs=(
            P(("clip", "frame"), "tile", None, None),
            P(("clip", "frame"), "tile", None, None),
            P(),
            P(),
        ),
        out_specs=(
            P(("clip", "frame"), "tile", None, None),
            P(("clip", "frame"), "tile", None, None),
            P(("clip", "frame", "tile"), None),
        ),
        check_vma=False,
    )
```

```python
import functools
import math

import jax
import jax.numpy as jnp
from jax import lax
from jax.experimental import pallas as pl
from jax.experimental.pallas import tpu as pltpu
from jax.sharding import PartitionSpec as P

TAP_DILATION = 2


def padded_2(block, sides, width):
    for axis, dim in sides:
        count = lax.axis_size(axis)
        forward = [(i, i + 1) for i in range(count - 1)]
        backward = [(target, source) for source, target in forward]
        low = lax.ppermute(
            lax.slice_in_dim(block, block.shape[dim] - width, None, axis=dim), axis, forward
        )
        high = lax.ppermute(lax.slice_in_dim(block, 0, width, axis=dim), axis, backward)
        block = jnp.concatenate([low, block, high], axis=dim)
    return block


def halving_scatter(term, axes):
    sizes = [size for _, size in axes]
    if any(size & (size - 1) for size in sizes):
        return lax.psum_scatter(term, tuple(name for name, _ in axes), scatter_dimension=0, tiled=True)
    bits = []
    for name, size in axes:
        bits += [(name, size, b) for b in reversed(range(size.bit_length() - 1))]
    groups = 1
    for size in sizes:
        groups *= size
    block = term.shape[0] // groups
    x = term.reshape((2,) * len(bits) + (block,) + term.shape[1:])
    for pos in reversed(range(len(bits))):
        name, size, b = bits[pos]
        mine = (lax.axis_index(name) >> b) & 1
        keep = lax.dynamic_index_in_dim(x, mine, axis=pos, keepdims=False)
        send = lax.dynamic_index_in_dim(x, 1 - mine, axis=pos, keepdims=False)
        pairs = [(i, i ^ (1 << b)) for i in range(size)]
        x = keep + lax.ppermute(send, name, pairs)
    return x


def halving_kernel(groups, narrow, x_ref, o_ref, *scratch):
    n = len(groups)
    send_sems, recv_sems = scratch[-2], scratch[-1]
    landings = scratch[:n]
    accs = scratch[n : 2 * n - 1]
    packs = scratch[2 * n - 1 : 2 * n - 1 + narrow]
    mesh_ids = pl.DeviceIdType.MESH
    plan = []
    for name, group_bits in groups:
        me = lax.axis_index(name)
        mine = [(me // (1 << b)) % 2 for b in group_bits]
        width = len(group_bits)
        own = 0
        for bit in mine:
            own = own * 2 + bit
        peers = []
        for mask in range(1, 1 << width):
            flips = [(mask >> (width - 1 - j)) % 2 for j in range(width)]
            partner = me
            chunk = 0
            for bit, flip, b in zip(mine, flips, group_bits):
                partner = partner + (1 - 2 * bit) * flip * (1 << b)
                chunk = chunk * 2 + bit + (1 - 2 * bit) * flip
            peers.append((mask, partner, chunk))
        plan.append((name, width, own, peers))
    barrier = pltpu.get_barrier_semaphore()
    contacts = 0
    for name, _, _, peers in plan:
        for _, partner, _ in peers:
            pl.semaphore_signal(barrier, inc=1, device_id={name: partner}, device_id_type=mesh_ids)
            contacts += 1
    pl.semaphore_wait(barrier, contacts)
    source = x_ref
    count = x_ref.shape[0]
    message = 0
    for k, (name, width, own, peers) in enumerate(plan):
        part = count >> width
        outbox = source
        if k < narrow:
            packs[k][...] = source[...].astype(packs[k].dtype)
            outbox = packs[k]
        copies = []
        for mask, partner, chunk in peers:
            copy = pltpu.make_async_remote_copy(
                src_ref=outbox.at[pl.ds(chunk * part, part)],
                dst_ref=landings[k].at[mask - 1],
                send_sem=send_sems.at[message],
                recv_sem=recv_sems.at[message],
                device_id={name: partner},
                device_id_type=mesh_ids,
            )
            copy.start()
            copies.append(copy)
            message += 1
        for copy in copies:
            copy.wait()
        total = source[pl.ds(own * part, part)]
        for slot in range(len(peers)):
            total = total + landings[k][slot].astype(jnp.float32)
        if k == n - 1:
            o_ref[...] = total[0]
        else:
            accs[k][...] = total
            source = accs[k]
        count = part


def kernel_scatter(term, axes):
    sizes = [size for _, size in axes]
    groups = 1
    for size in sizes:
        groups *= size
    per_block = term.shape[0] * term.shape[1] // groups
    if any(size & (size - 1) for size in sizes) or per_block % 128:
        return halving_scatter(term, axes)
    bits = []
    for name, size in axes:
        bits += [(name, b) for b in reversed(range(size.bit_length() - 1))]
    n = len(bits)
    x = term.reshape((2,) * n + (per_block // 128, 128))
    x = x.transpose(tuple(reversed(range(n))) + (n, n + 1)).reshape(groups, per_block // 128, 128)
    steps = list(reversed(bits))
    plan = [(steps[0][0], [steps[0][1]])]
    for name, b in steps[1:]:
        last_name, last_bits = plan[-1]
        if len(plan) > 1 and last_name == name and len(last_bits) == 1:
            last_bits.append(b)
        else:
            plan.append((name, [b]))
    narrow = min(2, len(plan))
    rows = x.shape[1:]
    counts = [x.shape[0]]
    for _, group_bits in plan:
        counts.append(counts[-1] >> len(group_bits))
    scratch = [
        pltpu.VMEM(
            ((1 << len(g[1])) - 1, counts[k + 1]) + rows,
            jnp.bfloat16 if k < narrow else jnp.float32,
        )
        for k, g in enumerate(plan)
    ]
    scratch += [pltpu.VMEM((counts[k + 1],) + rows, jnp.float32) for k in range(len(plan) - 1)]
    scratch += [pltpu.VMEM((counts[k],) + rows, jnp.bfloat16) for k in range(narrow)]
    messages = sum((1 << len(g[1])) - 1 for g in plan)
    scratch += [pltpu.SemaphoreType.DMA((messages,)), pltpu.SemaphoreType.DMA((messages,))]
    out = pl.pallas_call(
        functools.partial(halving_kernel, plan, narrow),
        out_shape=jax.ShapeDtypeStruct(rows, x.dtype),
        in_specs=[pl.BlockSpec(memory_space=pltpu.VMEM)],
        out_specs=pl.BlockSpec(memory_space=pltpu.VMEM),
        scratch_shapes=scratch,
        compiler_params=pltpu.CompilerParams(collective_id=0, has_side_effects=True),
    )(x)
    return out.reshape(term.shape[0] // groups, term.shape[1])


def tile_columns(extended, tile_rows, width_cells, backward_pass):
    padded = jnp.pad(extended, ((0, 0), (0, 0), (1, 1), (0, 0)))
    pieces = []
    for row_shift in range(3):
        for col_shift in range(3):
            row_start = 2 - row_shift if backward_pass else row_shift
            col_start = 2 - col_shift if backward_pass else col_shift
            pieces.append(
                padded[:, row_start : row_start + tile_rows, col_start : col_start + width_cells, :]
            )
    channels = extended.shape[3]
    return jnp.concatenate(pieces, axis=-1).reshape(-1, 9 * channels)


def temporal_taps(padded_seq, weight, frame_count, backward_pass):
    pieces = []
    for temporal_tap_index in range(9):
        first_frame_index = (
            (8 - temporal_tap_index) * TAP_DILATION
            if backward_pass
            else temporal_tap_index * TAP_DILATION
        )
        pieces.append(padded_seq[first_frame_index : first_frame_index + frame_count])
    channels = padded_seq.shape[2]
    columns = jnp.concatenate(pieces, axis=-1).reshape(-1, 9 * channels)
    return jnp.dot(columns, weight, preferred_element_type=jnp.float32)


def frame_exchange(clip_feats, out_grad, act, temporal_weight, temporal_back, temporal_reach):
    slab_frames, tile_rows, width_cells, channels = clip_feats.shape
    row_count = slab_frames * tile_rows * width_cells
    frame_devs = lax.axis_size("frame")
    per_group = tile_rows * width_cells // frame_devs
    grouped = (slab_frames, frame_devs, per_group, channels)
    act_part = lax.all_to_all(
        act.reshape(grouped), "frame", split_axis=1, concat_axis=0, tiled=True
    )
    grad_part = lax.all_to_all(out_grad, "frame", split_axis=1, concat_axis=0, tiled=True)
    feat_part = lax.all_to_all(clip_feats, "frame", split_axis=1, concat_axis=0, tiled=True)
    frame_count = act_part.shape[0]
    item_count = act_part.shape[2]
    act_pad = jnp.pad(
        act_part.reshape(frame_count, item_count, channels),
        ((temporal_reach, temporal_reach), (0, 0), (0, 0)),
    )
    grad_pad = jnp.pad(
        grad_part.reshape(frame_count, item_count, channels),
        ((temporal_reach, temporal_reach), (0, 0), (0, 0)),
    )
    mixed = temporal_taps(act_pad, temporal_weight, frame_count, False)
    out_part = (feat_part.reshape(-1, channels).astype(jnp.float32) + mixed).astype(jnp.bfloat16)
    back_part = temporal_taps(grad_pad, temporal_back, frame_count, True).astype(jnp.bfloat16)
    out_part = out_part.reshape(frame_count, 1, item_count, channels)
    back_part = back_part.reshape(frame_count, 1, item_count, channels)
    out_slab = lax.all_to_all(out_part, "frame", split_axis=0, concat_axis=1, tiled=True)
    grad_slab = lax.all_to_all(back_part, "frame", split_axis=0, concat_axis=1, tiled=True)
    act_grad = grad_slab.reshape(row_count, channels)
    return out_slab, act_grad


def per_device(clip_feats, out_grad, spatial_weight, temporal_weight):
    slab_frames, tile_rows, width_cells, channels = clip_feats.shape
    row_count = slab_frames * tile_rows * width_cells
    frame_devs = lax.axis_size("frame")
    tile_devs = lax.axis_size("tile")
    grad_scale = jnp.float32(
        1.0 / math.sqrt(slab_frames * frame_devs * tile_rows * tile_devs * width_cells)
    )
    spatial_back = (
        spatial_weight.reshape(9, channels, channels)
        .transpose(0, 2, 1)
        .reshape(9 * channels, channels)
    )
    temporal_back = (
        temporal_weight.reshape(9, channels, channels)
        .transpose(0, 2, 1)
        .reshape(9 * channels, channels)
    )
    feat_ext = padded_2(clip_feats, (("tile", 1),), 1)
    feat_columns = tile_columns(feat_ext, tile_rows, width_cells, False)
    pre = jnp.dot(feat_columns, spatial_weight, preferred_element_type=jnp.float32)
    act = jax.nn.silu(pre).astype(jnp.bfloat16)
    temporal_reach = 4 * TAP_DILATION
    if temporal_reach <= slab_frames:
        seq_shape = (slab_frames, tile_rows * width_cells, channels)
        grad_ext = padded_2(out_grad.reshape(seq_shape), (("frame", 0),), temporal_reach)
        act_grad = temporal_taps(grad_ext, temporal_back, slab_frames, True).astype(jnp.bfloat16)
        out_slab = None
    else:
        out_slab, act_grad = frame_exchange(
            clip_feats, out_grad, act, temporal_weight, temporal_back, temporal_reach
        )
    sig = jax.nn.sigmoid(pre)
    pre_grad = (act_grad.astype(jnp.float32) * (sig * (1.0 + pre * (1.0 - sig)))).astype(
        jnp.bfloat16
    )
    full_term = lax.dot_general(
        feat_columns, pre_grad, (((0,), (0,)), ((), ())), preferred_element_type=jnp.float32
    )
    summed = kernel_scatter(full_term, (("frame", frame_devs), ("tile", tile_devs)))
    weight_grad = summed * grad_scale
    act, pre_grad, summed = lax.optimization_barrier((act, pre_grad, summed))
    if out_slab is None:
        seq_shape = (slab_frames, tile_rows * width_cells, channels)
        act_ext = padded_2(act.reshape(seq_shape), (("frame", 0),), temporal_reach)
        mixed = temporal_taps(act_ext, temporal_weight, slab_frames, False)
        out_slab = (clip_feats.reshape(-1, channels).astype(jnp.float32) + mixed).astype(
            jnp.bfloat16
        )
        out_slab = out_slab.reshape(clip_feats.shape)
    grad_ext = padded_2(
        pre_grad.reshape(slab_frames, tile_rows, width_cells, channels), (("tile", 1),), 1
    )
    grad_columns = tile_columns(grad_ext, tile_rows, width_cells, True)
    local_back = jnp.dot(grad_columns, spatial_back, preferred_element_type=jnp.float32)
    input_grad = (out_grad.reshape(row_count, channels).astype(jnp.float32) + local_back).astype(
        jnp.bfloat16
    )
    input_grad = input_grad.reshape(slab_frames, tile_rows, width_cells, channels)
    return (out_slab, input_grad, weight_grad)


def solution(mesh):
    return jax.shard_map(
        per_device,
        mesh=mesh,
        in_specs=(
            P(("clip", "frame"), "tile", None, None),
            P(("clip", "frame"), "tile", None, None),
            P(),
            P(),
        ),
        out_specs=(
            P(("clip", "frame"), "tile", None, None),
            P(("clip", "frame"), "tile", None, None),
            P(("clip", "frame", "tile"), None),
        ),
        check_vma=False,
    )
```

```python
import functools
import math

import jax
import jax.numpy as jnp
from jax import lax
from jax.experimental import pallas as pl
from jax.experimental.pallas import tpu as pltpu
from jax.sharding import PartitionSpec as P

TAP_DILATION = 2


def padded_2(block, sides, width):
    for axis, dim in sides:
        count = lax.axis_size(axis)
        forward = [(i, i + 1) for i in range(count - 1)]
        backward = [(target, source) for source, target in forward]
        low = lax.ppermute(
            lax.slice_in_dim(block, block.shape[dim] - width, None, axis=dim), axis, forward
        )
        high = lax.ppermute(lax.slice_in_dim(block, 0, width, axis=dim), axis, backward)
        block = jnp.concatenate([low, block, high], axis=dim)
    return block


def halving_scatter(term, axes):
    sizes = [size for _, size in axes]
    if any(size & (size - 1) for size in sizes):
        return lax.psum_scatter(term, tuple(name for name, _ in axes), scatter_dimension=0, tiled=True)
    bits = []
    for name, size in axes:
        bits += [(name, size, b) for b in reversed(range(size.bit_length() - 1))]
    groups = 1
    for size in sizes:
        groups *= size
    block = term.shape[0] // groups
    x = term.reshape((2,) * len(bits) + (block,) + term.shape[1:])
    for pos in reversed(range(len(bits))):
        name, size, b = bits[pos]
        mine = (lax.axis_index(name) >> b) & 1
        keep = lax.dynamic_index_in_dim(x, mine, axis=pos, keepdims=False)
        send = lax.dynamic_index_in_dim(x, 1 - mine, axis=pos, keepdims=False)
        pairs = [(i, i ^ (1 << b)) for i in range(size)]
        x = keep + lax.ppermute(send, name, pairs)
    return x


def halving_kernel(groups, narrow, x_ref, o_ref, *scratch):
    n = len(groups)
    send_sems, recv_sems = scratch[-2], scratch[-1]
    landings = scratch[:n]
    accs = scratch[n : 2 * n - 1]
    packs = scratch[2 * n - 1 : 2 * n - 1 + narrow]
    mesh_ids = pl.DeviceIdType.MESH
    plan = []
    for name, group_bits in groups:
        me = lax.axis_index(name)
        mine = [(me // (1 << b)) % 2 for b in group_bits]
        width = len(group_bits)
        own = 0
        for bit in mine:
            own = own * 2 + bit
        peers = []
        for mask in range(1, 1 << width):
            flips = [(mask >> (width - 1 - j)) % 2 for j in range(width)]
            partner = me
            chunk = 0
            for bit, flip, b in zip(mine, flips, group_bits):
                partner = partner + (1 - 2 * bit) * flip * (1 << b)
                chunk = chunk * 2 + bit + (1 - 2 * bit) * flip
            peers.append((mask, partner, chunk))
        plan.append((name, width, own, peers))
    barrier = pltpu.get_barrier_semaphore()
    contacts = 0
    for name, _, _, peers in plan:
        for _, partner, _ in peers:
            pl.semaphore_signal(barrier, inc=1, device_id={name: partner}, device_id_type=mesh_ids)
            contacts += 1
    pl.semaphore_wait(barrier, contacts)
    source = x_ref
    count = x_ref.shape[0]
    message = 0
    for k, (name, width, own, peers) in enumerate(plan):
        part = count >> width
        outbox = source
        if k < narrow:
            packs[k][...] = source[...].astype(packs[k].dtype)
            outbox = packs[k]
        copies = []
        for mask, partner, chunk in peers:
            copy = pltpu.make_async_remote_copy(
                src_ref=outbox.at[pl.ds(chunk * part, part)],
                dst_ref=landings[k].at[mask - 1],
                send_sem=send_sems.at[message],
                recv_sem=recv_sems.at[message],
                device_id={name: partner},
                device_id_type=mesh_ids,
            )
            copy.start()
            copies.append(copy)
            message += 1
        for copy in copies:
            copy.wait()
        total = source[pl.ds(own * part, part)]
        for slot in range(len(peers)):
            total = total + landings[k][slot].astype(jnp.float32)
        if k == n - 1:
            o_ref[...] = total[0]
        else:
            accs[k][...] = total
            source = accs[k]
        count = part


def kernel_scatter(term, axes):
    sizes = [size for _, size in axes]
    groups = 1
    for size in sizes:
        groups *= size
    per_block = term.shape[0] * term.shape[1] // groups
    if any(size & (size - 1) for size in sizes) or per_block % 128:
        return halving_scatter(term, axes)
    bits = []
    for name, size in axes:
        bits += [(name, b) for b in reversed(range(size.bit_length() - 1))]
    n = len(bits)
    x = term.reshape((2,) * n + (per_block // 128, 128))
    x = x.transpose(tuple(reversed(range(n))) + (n, n + 1)).reshape(groups, per_block // 128, 128)
    steps = list(reversed(bits))
    plan = [(steps[0][0], [steps[0][1]])]
    for name, b in steps[1:]:
        last_name, last_bits = plan[-1]
        if len(plan) > 1 and last_name == name and len(last_bits) == 1:
            last_bits.append(b)
        else:
            plan.append((name, [b]))
    narrow = min(2, len(plan))
    rows = x.shape[1:]
    counts = [x.shape[0]]
    for _, group_bits in plan:
        counts.append(counts[-1] >> len(group_bits))
    scratch = [
        pltpu.VMEM(
            ((1 << len(g[1])) - 1, counts[k + 1]) + rows,
            jnp.bfloat16 if k < narrow else jnp.float32,
        )
        for k, g in enumerate(plan)
    ]
    scratch += [pltpu.VMEM((counts[k + 1],) + rows, jnp.float32) for k in range(len(plan) - 1)]
    scratch += [pltpu.VMEM((counts[k],) + rows, jnp.bfloat16) for k in range(narrow)]
    messages = sum((1 << len(g[1])) - 1 for g in plan)
    scratch += [pltpu.SemaphoreType.DMA((messages,)), pltpu.SemaphoreType.DMA((messages,))]
    out = pl.pallas_call(
        functools.partial(halving_kernel, plan, narrow),
        out_shape=jax.ShapeDtypeStruct(rows, x.dtype),
        in_specs=[pl.BlockSpec(memory_space=pltpu.VMEM)],
        out_specs=pl.BlockSpec(memory_space=pltpu.VMEM),
        scratch_shapes=scratch,
        compiler_params=pltpu.CompilerParams(collective_id=0, has_side_effects=True),
    )(x)
    return out.reshape(term.shape[0] // groups, term.shape[1])


def tile_columns(extended, tile_rows, width_cells, backward_pass):
    padded = jnp.pad(extended, ((0, 0), (0, 0), (1, 1), (0, 0)))
    pieces = []
    for row_shift in range(3):
        for col_shift in range(3):
            row_start = 2 - row_shift if backward_pass else row_shift
            col_start = 2 - col_shift if backward_pass else col_shift
            pieces.append(
                padded[:, row_start : row_start + tile_rows, col_start : col_start + width_cells, :]
            )
    channels = extended.shape[3]
    return jnp.concatenate(pieces, axis=-1).reshape(-1, 9 * channels)


def temporal_taps(padded_seq, weight, frame_count, backward_pass):
    pieces = []
    for temporal_tap_index in range(9):
        first_frame_index = (
            (8 - temporal_tap_index) * TAP_DILATION
            if backward_pass
            else temporal_tap_index * TAP_DILATION
        )
        pieces.append(padded_seq[first_frame_index : first_frame_index + frame_count])
    channels = padded_seq.shape[2]
    columns = jnp.concatenate(pieces, axis=-1).reshape(-1, 9 * channels)
    return jnp.dot(columns, weight, preferred_element_type=jnp.float32)


def frame_exchange(clip_feats, out_grad, act, temporal_weight, temporal_back, temporal_reach):
    slab_frames, tile_rows, width_cells, channels = clip_feats.shape
    row_count = slab_frames * tile_rows * width_cells
    frame_devs = lax.axis_size("frame")
    per_group = tile_rows * width_cells // frame_devs
    grouped = (slab_frames, frame_devs, per_group, channels)
    act_part = lax.all_to_all(
        act.reshape(grouped), "frame", split_axis=1, concat_axis=0, tiled=True
    )
    grad_part = lax.all_to_all(out_grad, "frame", split_axis=1, concat_axis=0, tiled=True)
    feat_part = lax.all_to_all(clip_feats, "frame", split_axis=1, concat_axis=0, tiled=True)
    frame_count = act_part.shape[0]
    item_count = act_part.shape[2]
    act_pad = jnp.pad(
        act_part.reshape(frame_count, item_count, channels),
        ((temporal_reach, temporal_reach), (0, 0), (0, 0)),
    )
    grad_pad = jnp.pad(
        grad_part.reshape(frame_count, item_count, channels),
        ((temporal_reach, temporal_reach), (0, 0), (0, 0)),
    )
    mixed = temporal_taps(act_pad, temporal_weight, frame_count, False)
    out_part = (feat_part.reshape(-1, channels).astype(jnp.float32) + mixed).astype(jnp.bfloat16)
    back_part = temporal_taps(grad_pad, temporal_back, frame_count, True).astype(jnp.bfloat16)
    out_part = out_part.reshape(frame_count, 1, item_count, channels)
    back_part = back_part.reshape(frame_count, 1, item_count, channels)
    out_slab = lax.all_to_all(out_part, "frame", split_axis=0, concat_axis=1, tiled=True)
    grad_slab = lax.all_to_all(back_part, "frame", split_axis=0, concat_axis=1, tiled=True)
    act_grad = grad_slab.reshape(row_count, channels)
    return out_slab, act_grad


def per_device(clip_feats, out_grad, spatial_weight, temporal_weight):
    slab_frames, tile_rows, width_cells, channels = clip_feats.shape
    row_count = slab_frames * tile_rows * width_cells
    frame_devs = lax.axis_size("frame")
    tile_devs = lax.axis_size("tile")
    grad_scale = jnp.float32(
        1.0 / math.sqrt(slab_frames * frame_devs * tile_rows * tile_devs * width_cells)
    )
    spatial_back = (
        spatial_weight.reshape(9, channels, channels)
        .transpose(0, 2, 1)
        .reshape(9 * channels, channels)
    )
    temporal_back = (
        temporal_weight.reshape(9, channels, channels)
        .transpose(0, 2, 1)
        .reshape(9 * channels, channels)
    )
    feat_ext = padded_2(clip_feats, (("tile", 1),), 1)
    feat_columns = tile_columns(feat_ext, tile_rows, width_cells, False)
    pre = jnp.dot(feat_columns, spatial_weight, preferred_element_type=jnp.float32)
    act = jax.nn.silu(pre).astype(jnp.bfloat16)
    temporal_reach = 4 * TAP_DILATION
    if temporal_reach <= slab_frames:
        seq_shape = (slab_frames, tile_rows * width_cells, channels)
        act_ext = padded_2(act.reshape(seq_shape), (("frame", 0),), temporal_reach)
        grad_ext = padded_2(out_grad.reshape(seq_shape), (("frame", 0),), temporal_reach)
        act_grad = temporal_taps(grad_ext, temporal_back, slab_frames, True).astype(jnp.bfloat16)
        mixed = temporal_taps(act_ext, temporal_weight, slab_frames, False)
        out_slab = (clip_feats.reshape(-1, channels).astype(jnp.float32) + mixed).astype(
            jnp.bfloat16
        )
        out_slab = out_slab.reshape(clip_feats.shape)
    else:
        out_slab, act_grad = frame_exchange(
            clip_feats, out_grad, act, temporal_weight, temporal_back, temporal_reach
        )
    sig = jax.nn.sigmoid(pre)
    pre_grad = (act_grad.astype(jnp.float32) * (sig * (1.0 + pre * (1.0 - sig)))).astype(
        jnp.bfloat16
    )
    full_term = lax.dot_general(
        feat_columns, pre_grad, (((0,), (0,)), ((), ())), preferred_element_type=jnp.float32
    )
    summed = kernel_scatter(full_term, (("frame", frame_devs), ("tile", tile_devs)))
    weight_grad = summed * grad_scale
    pre_grad, summed = lax.optimization_barrier((pre_grad, summed))
    grad_ext = padded_2(
        pre_grad.reshape(slab_frames, tile_rows, width_cells, channels), (("tile", 1),), 1
    )
    grad_columns = tile_columns(grad_ext, tile_rows, width_cells, True)
    local_back = jnp.dot(grad_columns, spatial_back, preferred_element_type=jnp.float32)
    input_grad = (out_grad.reshape(row_count, channels).astype(jnp.float32) + local_back).astype(
        jnp.bfloat16
    )
    input_grad = input_grad.reshape(slab_frames, tile_rows, width_cells, channels)
    return (out_slab, input_grad, weight_grad)


def solution(mesh):
    return jax.shard_map(
        per_device,
        mesh=mesh,
        in_specs=(
            P(("clip", "frame"), "tile", None, None),
            P(("clip", "frame"), "tile", None, None),
            P(),
            P(),
        ),
        out_specs=(
            P(("clip", "frame"), "tile", None, None),
            P(("clip", "frame"), "tile", None, None),
            P(("clip", "frame", "tile"), None),
        ),
        check_vma=False,
    )
```

```python
import functools
import math

import jax
import jax.numpy as jnp
from jax import lax
from jax.experimental import pallas as pl
from jax.experimental.pallas import tpu as pltpu
from jax.sharding import PartitionSpec as P

TAP_DILATION = 2


def padded_2(block, sides, width):
    for axis, dim in sides:
        count = lax.axis_size(axis)
        forward = [(i, i + 1) for i in range(count - 1)]
        backward = [(target, source) for source, target in forward]
        low = lax.ppermute(
            lax.slice_in_dim(block, block.shape[dim] - width, None, axis=dim), axis, forward
        )
        high = lax.ppermute(lax.slice_in_dim(block, 0, width, axis=dim), axis, backward)
        block = jnp.concatenate([low, block, high], axis=dim)
    return block


def halving_scatter(term, axes):
    sizes = [size for _, size in axes]
    if any(size & (size - 1) for size in sizes):
        return lax.psum_scatter(term, tuple(name for name, _ in axes), scatter_dimension=0, tiled=True)
    bits = []
    for name, size in axes:
        bits += [(name, size, b) for b in reversed(range(size.bit_length() - 1))]
    groups = 1
    for size in sizes:
        groups *= size
    block = term.shape[0] // groups
    x = term.reshape((2,) * len(bits) + (block,) + term.shape[1:])
    for pos in reversed(range(len(bits))):
        name, size, b = bits[pos]
        mine = (lax.axis_index(name) >> b) & 1
        keep = lax.dynamic_index_in_dim(x, mine, axis=pos, keepdims=False)
        send = lax.dynamic_index_in_dim(x, 1 - mine, axis=pos, keepdims=False)
        pairs = [(i, i ^ (1 << b)) for i in range(size)]
        x = keep + lax.ppermute(send, name, pairs)
    return x


def halving_kernel(groups, narrow, x_ref, o_ref, ordered, *scratch):
    n = len(groups)
    send_sems, recv_sems = scratch[-2], scratch[-1]
    landings = scratch[:n]
    accs = scratch[n : 2 * n - 1]
    packs = scratch[2 * n - 1 : 2 * n - 1 + narrow]
    mesh_ids = pl.DeviceIdType.MESH
    plan = []
    for name, group_bits in groups:
        me = lax.axis_index(name)
        mine = [(me // (1 << b)) % 2 for b in group_bits]
        width = len(group_bits)
        own = 0
        for bit in mine:
            own = own * 2 + bit
        peers = []
        for mask in range(1, 1 << width):
            flips = [(mask >> (width - 1 - j)) % 2 for j in range(width)]
            partner = me
            chunk = 0
            for bit, flip, b in zip(mine, flips, group_bits):
                partner = partner + (1 - 2 * bit) * flip * (1 << b)
                chunk = chunk * 2 + bit + (1 - 2 * bit) * flip
            peers.append((mask, partner, chunk))
        plan.append((name, width, own, peers))
    barrier = pltpu.get_barrier_semaphore()
    contacts = 0
    for name, _, _, peers in plan:
        for _, partner, _ in peers:
            pl.semaphore_signal(barrier, inc=1, device_id={name: partner}, device_id_type=mesh_ids)
            contacts += 1
    blocks = x_ref.shape[0]
    width = blocks.bit_length() - 1
    for b in range(blocks):
        turned = int(format(b, "0%db" % width)[::-1], 2)
        ordered[turned] = x_ref[b]
    pl.semaphore_wait(barrier, contacts)
    source = ordered
    count = x_ref.shape[0]
    message = 0
    for k, (name, width, own, peers) in enumerate(plan):
        part = count >> width
        outbox = source
        if k < narrow:
            packs[k][...] = source[...].astype(packs[k].dtype)
            outbox = packs[k]
        copies = []
        for mask, partner, chunk in peers:
            copy = pltpu.make_async_remote_copy(
                src_ref=outbox.at[pl.ds(chunk * part, part)],
                dst_ref=landings[k].at[mask - 1],
                send_sem=send_sems.at[message],
                recv_sem=recv_sems.at[message],
                device_id={name: partner},
                device_id_type=mesh_ids,
            )
            copy.start()
            copies.append(copy)
            message += 1
        for copy in copies:
            copy.wait()
        total = source[pl.ds(own * part, part)]
        for slot in range(len(peers)):
            total = total + landings[k][slot].astype(jnp.float32)
        if k == n - 1:
            o_ref[...] = total[0]
        else:
            accs[k][...] = total
            source = accs[k]
        count = part


def kernel_scatter(term, axes):
    sizes = [size for _, size in axes]
    groups = 1
    for size in sizes:
        groups *= size
    per_block = term.shape[0] * term.shape[1] // groups
    if any(size & (size - 1) for size in sizes) or per_block % 128:
        return halving_scatter(term, axes)
    bits = []
    for name, size in axes:
        bits += [(name, b) for b in reversed(range(size.bit_length() - 1))]
    n = len(bits)
    x = term.reshape(groups, per_block // 128, 128)
    steps = list(reversed(bits))
    plan = [(steps[0][0], [steps[0][1]])]
    for name, b in steps[1:]:
        last_name, last_bits = plan[-1]
        if len(plan) > 1 and last_name == name and len(last_bits) == 1:
            last_bits.append(b)
        else:
            plan.append((name, [b]))
    narrow = min(2, len(plan))
    rows = x.shape[1:]
    counts = [x.shape[0]]
    for _, group_bits in plan:
        counts.append(counts[-1] >> len(group_bits))
    scratch = [pltpu.VMEM(x.shape, x.dtype)]
    scratch += [
        pltpu.VMEM(
            ((1 << len(g[1])) - 1, counts[k + 1]) + rows,
            jnp.bfloat16 if k < narrow else jnp.float32,
        )
        for k, g in enumerate(plan)
    ]
    scratch += [pltpu.VMEM((counts[k + 1],) + rows, jnp.float32) for k in range(len(plan) - 1)]
    scratch += [pltpu.VMEM((counts[k],) + rows, jnp.bfloat16) for k in range(narrow)]
    messages = sum((1 << len(g[1])) - 1 for g in plan)
    scratch += [pltpu.SemaphoreType.DMA((messages,)), pltpu.SemaphoreType.DMA((messages,))]
    out = pl.pallas_call(
        functools.partial(halving_kernel, plan, narrow),
        out_shape=jax.ShapeDtypeStruct(rows, x.dtype),
        in_specs=[pl.BlockSpec(memory_space=pltpu.VMEM)],
        out_specs=pl.BlockSpec(memory_space=pltpu.VMEM),
        scratch_shapes=scratch,
        compiler_params=pltpu.CompilerParams(collective_id=0, has_side_effects=True),
    )(x)
    return out.reshape(term.shape[0] // groups, term.shape[1])


def tile_columns(extended, tile_rows, width_cells, backward_pass):
    padded = jnp.pad(extended, ((0, 0), (0, 0), (1, 1), (0, 0)))
    pieces = []
    for row_shift in range(3):
        for col_shift in range(3):
            row_start = 2 - row_shift if backward_pass else row_shift
            col_start = 2 - col_shift if backward_pass else col_shift
            pieces.append(
                padded[:, row_start : row_start + tile_rows, col_start : col_start + width_cells, :]
            )
    channels = extended.shape[3]
    return jnp.concatenate(pieces, axis=-1).reshape(-1, 9 * channels)


def temporal_taps(padded_seq, weight, frame_count, backward_pass):
    pieces = []
    for temporal_tap_index in range(9):
        first_frame_index = (
            (8 - temporal_tap_index) * TAP_DILATION
            if backward_pass
            else temporal_tap_index * TAP_DILATION
        )
        pieces.append(padded_seq[first_frame_index : first_frame_index + frame_count])
    channels = padded_seq.shape[2]
    columns = jnp.concatenate(pieces, axis=-1).reshape(-1, 9 * channels)
    return jnp.dot(columns, weight, preferred_element_type=jnp.float32)


def frame_exchange(clip_feats, out_grad, act, temporal_weight, temporal_back, temporal_reach):
    slab_frames, tile_rows, width_cells, channels = clip_feats.shape
    row_count = slab_frames * tile_rows * width_cells
    frame_devs = lax.axis_size("frame")
    per_group = tile_rows * width_cells // frame_devs
    grouped = (slab_frames, frame_devs, per_group, channels)
    act_part = lax.all_to_all(
        act.reshape(grouped), "frame", split_axis=1, concat_axis=0, tiled=True
    )
    grad_part = lax.all_to_all(out_grad, "frame", split_axis=1, concat_axis=0, tiled=True)
    feat_part = lax.all_to_all(clip_feats, "frame", split_axis=1, concat_axis=0, tiled=True)
    frame_count = act_part.shape[0]
    item_count = act_part.shape[2]
    act_pad = jnp.pad(
        act_part.reshape(frame_count, item_count, channels),
        ((temporal_reach, temporal_reach), (0, 0), (0, 0)),
    )
    grad_pad = jnp.pad(
        grad_part.reshape(frame_count, item_count, channels),
        ((temporal_reach, temporal_reach), (0, 0), (0, 0)),
    )
    mixed = temporal_taps(act_pad, temporal_weight, frame_count, False)
    out_part = (feat_part.reshape(-1, channels).astype(jnp.float32) + mixed).astype(jnp.bfloat16)
    back_part = temporal_taps(grad_pad, temporal_back, frame_count, True).astype(jnp.bfloat16)
    out_part = out_part.reshape(frame_count, 1, item_count, channels)
    back_part = back_part.reshape(frame_count, 1, item_count, channels)
    out_slab = lax.all_to_all(out_part, "frame", split_axis=0, concat_axis=1, tiled=True)
    grad_slab = lax.all_to_all(back_part, "frame", split_axis=0, concat_axis=1, tiled=True)
    act_grad = grad_slab.reshape(row_count, channels)
    return out_slab, act_grad


def per_device(clip_feats, out_grad, spatial_weight, temporal_weight):
    slab_frames, tile_rows, width_cells, channels = clip_feats.shape
    row_count = slab_frames * tile_rows * width_cells
    frame_devs = lax.axis_size("frame")
    tile_devs = lax.axis_size("tile")
    grad_scale = jnp.float32(
        1.0 / math.sqrt(slab_frames * frame_devs * tile_rows * tile_devs * width_cells)
    )
    spatial_back = (
        spatial_weight.reshape(9, channels, channels)
        .transpose(0, 2, 1)
        .reshape(9 * channels, channels)
    )
    temporal_back = (
        temporal_weight.reshape(9, channels, channels)
        .transpose(0, 2, 1)
        .reshape(9 * channels, channels)
    )
    feat_ext = padded_2(clip_feats, (("tile", 1),), 1)
    feat_columns = tile_columns(feat_ext, tile_rows, width_cells, False)
    pre = jnp.dot(feat_columns, spatial_weight, preferred_element_type=jnp.float32)
    act = jax.nn.silu(pre).astype(jnp.bfloat16)
    temporal_reach = 4 * TAP_DILATION
    if temporal_reach <= slab_frames:
        seq_shape = (slab_frames, tile_rows * width_cells, channels)
        act_ext = padded_2(act.reshape(seq_shape), (("frame", 0),), temporal_reach)
        grad_ext = padded_2(out_grad.reshape(seq_shape), (("frame", 0),), temporal_reach)
        act_grad = temporal_taps(grad_ext, temporal_back, slab_frames, True).astype(jnp.bfloat16)
        mixed = temporal_taps(act_ext, temporal_weight, slab_frames, False)
        out_slab = (clip_feats.reshape(-1, channels).astype(jnp.float32) + mixed).astype(
            jnp.bfloat16
        )
        out_slab = out_slab.reshape(clip_feats.shape)
    else:
        out_slab, act_grad = frame_exchange(
            clip_feats, out_grad, act, temporal_weight, temporal_back, temporal_reach
        )
    sig = jax.nn.sigmoid(pre)
    pre_grad = (act_grad.astype(jnp.float32) * (sig * (1.0 + pre * (1.0 - sig)))).astype(
        jnp.bfloat16
    )
    full_term = lax.dot_general(
        feat_columns, pre_grad, (((0,), (0,)), ((), ())), preferred_element_type=jnp.float32
    )
    summed = kernel_scatter(full_term, (("frame", frame_devs), ("tile", tile_devs)))
    weight_grad = summed * grad_scale
    grad_ext = padded_2(
        pre_grad.reshape(slab_frames, tile_rows, width_cells, channels), (("tile", 1),), 1
    )
    grad_columns = tile_columns(grad_ext, tile_rows, width_cells, True)
    local_back = jnp.dot(grad_columns, spatial_back, preferred_element_type=jnp.float32)
    input_grad = (out_grad.reshape(row_count, channels).astype(jnp.float32) + local_back).astype(
        jnp.bfloat16
    )
    input_grad = input_grad.reshape(slab_frames, tile_rows, width_cells, channels)
    return (out_slab, input_grad, weight_grad)


def solution(mesh):
    return jax.shard_map(
        per_device,
        mesh=mesh,
        in_specs=(
            P(("clip", "frame"), "tile", None, None),
            P(("clip", "frame"), "tile", None, None),
            P(),
            P(),
        ),
        out_specs=(
            P(("clip", "frame"), "tile", None, None),
            P(("clip", "frame"), "tile", None, None),
            P(("clip", "frame", "tile"), None),
        ),
        check_vma=False,
    )
```

```python
import functools
import math

import jax
import jax.numpy as jnp
from jax import lax
from jax.experimental import pallas as pl
from jax.experimental.pallas import tpu as pltpu
from jax.sharding import PartitionSpec as P

TAP_DILATION = 2


def padded_2(block, sides, width):
    for axis, dim in sides:
        count = lax.axis_size(axis)
        forward = [(i, i + 1) for i in range(count - 1)]
        backward = [(target, source) for source, target in forward]
        low = lax.ppermute(
            lax.slice_in_dim(block, block.shape[dim] - width, None, axis=dim), axis, forward
        )
        high = lax.ppermute(lax.slice_in_dim(block, 0, width, axis=dim), axis, backward)
        block = jnp.concatenate([low, block, high], axis=dim)
    return block


def halving_scatter(term, axes):
    sizes = [size for _, size in axes]
    if any(size & (size - 1) for size in sizes):
        return lax.psum_scatter(term, tuple(name for name, _ in axes), scatter_dimension=0, tiled=True)
    bits = []
    for name, size in axes:
        bits += [(name, size, b) for b in reversed(range(size.bit_length() - 1))]
    groups = 1
    for size in sizes:
        groups *= size
    block = term.shape[0] // groups
    x = term.reshape((2,) * len(bits) + (block,) + term.shape[1:])
    for pos in reversed(range(len(bits))):
        name, size, b = bits[pos]
        mine = (lax.axis_index(name) >> b) & 1
        keep = lax.dynamic_index_in_dim(x, mine, axis=pos, keepdims=False)
        send = lax.dynamic_index_in_dim(x, 1 - mine, axis=pos, keepdims=False)
        pairs = [(i, i ^ (1 << b)) for i in range(size)]
        x = keep + lax.ppermute(send, name, pairs)
    return x


def halving_kernel(groups, narrow, reorder, x_ref, o_ref, *scratch):
    if reorder:
        ordered, scratch = scratch[0], scratch[1:]
    n = len(groups)
    send_sems, recv_sems = scratch[-2], scratch[-1]
    landings = scratch[:n]
    accs = scratch[n : 2 * n - 1]
    packs = scratch[2 * n - 1 : 2 * n - 1 + narrow]
    mesh_ids = pl.DeviceIdType.MESH
    plan = []
    for name, group_bits in groups:
        me = lax.axis_index(name)
        mine = [(me // (1 << b)) % 2 for b in group_bits]
        width = len(group_bits)
        own = 0
        for bit in mine:
            own = own * 2 + bit
        peers = []
        for mask in range(1, 1 << width):
            flips = [(mask >> (width - 1 - j)) % 2 for j in range(width)]
            partner = me
            chunk = 0
            for bit, flip, b in zip(mine, flips, group_bits):
                partner = partner + (1 - 2 * bit) * flip * (1 << b)
                chunk = chunk * 2 + bit + (1 - 2 * bit) * flip
            peers.append((mask, partner, chunk))
        plan.append((name, width, own, peers))
    barrier = pltpu.get_barrier_semaphore()
    contacts = 0
    for name, _, _, peers in plan:
        for _, partner, _ in peers:
            pl.semaphore_signal(barrier, inc=1, device_id={name: partner}, device_id_type=mesh_ids)
            contacts += 1
    source = x_ref
    if reorder:
        blocks = x_ref.shape[0]
        width = blocks.bit_length() - 1
        for b in range(blocks):
            turned = int(format(b, "0%db" % width)[::-1], 2)
            ordered[turned] = x_ref[b]
        source = ordered
    pl.semaphore_wait(barrier, contacts)
    count = x_ref.shape[0]
    message = 0
    for k, (name, width, own, peers) in enumerate(plan):
        part = count >> width
        outbox = source
        if k < narrow:
            packs[k][...] = source[...].astype(packs[k].dtype)
            outbox = packs[k]
        copies = []
        for mask, partner, chunk in peers:
            copy = pltpu.make_async_remote_copy(
                src_ref=outbox.at[pl.ds(chunk * part, part)],
                dst_ref=landings[k].at[mask - 1],
                send_sem=send_sems.at[message],
                recv_sem=recv_sems.at[message],
                device_id={name: partner},
                device_id_type=mesh_ids,
            )
            copy.start()
            copies.append(copy)
            message += 1
        for copy in copies:
            copy.wait()
        total = source[pl.ds(own * part, part)]
        for slot in range(len(peers)):
            total = total + landings[k][slot].astype(jnp.float32)
        if k == n - 1:
            o_ref[...] = total
        else:
            accs[k][...] = total
            source = accs[k]
        count = part


def kernel_scatter(term, axes):
    sizes = [size for _, size in axes]
    groups = 1
    for size in sizes:
        groups *= size
    per_block = term.shape[0] * term.shape[1] // groups
    if any(size & (size - 1) for size in sizes) or per_block % 128:
        return halving_scatter(term, axes)
    bits = []
    for name, size in axes:
        bits += [(name, b) for b in reversed(range(size.bit_length() - 1))]
    n = len(bits)
    x = term.reshape(groups, per_block // 128, 128)
    steps = list(reversed(bits))
    plan = [(steps[0][0], [steps[0][1]])]
    for name, b in steps[1:]:
        last_name, last_bits = plan[-1]
        if len(plan) > 1 and last_name == name and len(last_bits) == 1:
            last_bits.append(b)
        else:
            plan.append((name, [b]))
    narrow = min(2, len(plan))
    rows = x.shape[1:]
    counts = [x.shape[0]]
    for _, group_bits in plan:
        counts.append(counts[-1] >> len(group_bits))
    out = x
    for k, group in enumerate(plan):
        small = jnp.bfloat16 if k < narrow else jnp.float32
        scratch = [pltpu.VMEM(x.shape, x.dtype)] if k == 0 else []
        scratch += [pltpu.VMEM(((1 << len(group[1])) - 1, counts[k + 1]) + rows, small)]
        if k < narrow:
            scratch += [pltpu.VMEM((counts[k],) + rows, jnp.bfloat16)]
        messages = (1 << len(group[1])) - 1
        scratch += [pltpu.SemaphoreType.DMA((messages,)), pltpu.SemaphoreType.DMA((messages,))]
        out = pl.pallas_call(
            functools.partial(halving_kernel, [group], 1 if k < narrow else 0, k == 0),
            out_shape=jax.ShapeDtypeStruct((counts[k + 1],) + rows, x.dtype),
            in_specs=[pl.BlockSpec(memory_space=pltpu.VMEM)],
            out_specs=pl.BlockSpec(memory_space=pltpu.VMEM),
            scratch_shapes=scratch,
            compiler_params=pltpu.CompilerParams(collective_id=k, has_side_effects=True),
        )(out)
    return out.reshape(term.shape[0] // groups, term.shape[1])


def tile_columns(extended, tile_rows, width_cells, backward_pass):
    padded = jnp.pad(extended, ((0, 0), (0, 0), (1, 1), (0, 0)))
    pieces = []
    for row_shift in range(3):
        for col_shift in range(3):
            row_start = 2 - row_shift if backward_pass else row_shift
            col_start = 2 - col_shift if backward_pass else col_shift
            pieces.append(
                padded[:, row_start : row_start + tile_rows, col_start : col_start + width_cells, :]
            )
    channels = extended.shape[3]
    return jnp.concatenate(pieces, axis=-1).reshape(-1, 9 * channels)


def temporal_taps(padded_seq, weight, frame_count, backward_pass):
    pieces = []
    for temporal_tap_index in range(9):
        first_frame_index = (
            (8 - temporal_tap_index) * TAP_DILATION
            if backward_pass
            else temporal_tap_index * TAP_DILATION
        )
        pieces.append(padded_seq[first_frame_index : first_frame_index + frame_count])
    channels = padded_seq.shape[2]
    columns = jnp.concatenate(pieces, axis=-1).reshape(-1, 9 * channels)
    return jnp.dot(columns, weight, preferred_element_type=jnp.float32)


def frame_exchange(clip_feats, out_grad, act, temporal_weight, temporal_back, temporal_reach):
    slab_frames, tile_rows, width_cells, channels = clip_feats.shape
    row_count = slab_frames * tile_rows * width_cells
    frame_devs = lax.axis_size("frame")
    per_group = tile_rows * width_cells // frame_devs
    grouped = (slab_frames, frame_devs, per_group, channels)
    act_part = lax.all_to_all(
        act.reshape(grouped), "frame", split_axis=1, concat_axis=0, tiled=True
    )
    grad_part = lax.all_to_all(out_grad, "frame", split_axis=1, concat_axis=0, tiled=True)
    feat_part = lax.all_to_all(clip_feats, "frame", split_axis=1, concat_axis=0, tiled=True)
    frame_count = act_part.shape[0]
    item_count = act_part.shape[2]
    act_pad = jnp.pad(
        act_part.reshape(frame_count, item_count, channels),
        ((temporal_reach, temporal_reach), (0, 0), (0, 0)),
    )
    grad_pad = jnp.pad(
        grad_part.reshape(frame_count, item_count, channels),
        ((temporal_reach, temporal_reach), (0, 0), (0, 0)),
    )
    mixed = temporal_taps(act_pad, temporal_weight, frame_count, False)
    out_part = (feat_part.reshape(-1, channels).astype(jnp.float32) + mixed).astype(jnp.bfloat16)
    back_part = temporal_taps(grad_pad, temporal_back, frame_count, True).astype(jnp.bfloat16)
    out_part = out_part.reshape(frame_count, 1, item_count, channels)
    back_part = back_part.reshape(frame_count, 1, item_count, channels)
    out_slab = lax.all_to_all(out_part, "frame", split_axis=0, concat_axis=1, tiled=True)
    grad_slab = lax.all_to_all(back_part, "frame", split_axis=0, concat_axis=1, tiled=True)
    act_grad = grad_slab.reshape(row_count, channels)
    return out_slab, act_grad


def per_device(clip_feats, out_grad, spatial_weight, temporal_weight):
    slab_frames, tile_rows, width_cells, channels = clip_feats.shape
    row_count = slab_frames * tile_rows * width_cells
    frame_devs = lax.axis_size("frame")
    tile_devs = lax.axis_size("tile")
    grad_scale = jnp.float32(
        1.0 / math.sqrt(slab_frames * frame_devs * tile_rows * tile_devs * width_cells)
    )
    spatial_back = (
        spatial_weight.reshape(9, channels, channels)
        .transpose(0, 2, 1)
        .reshape(9 * channels, channels)
    )
    temporal_back = (
        temporal_weight.reshape(9, channels, channels)
        .transpose(0, 2, 1)
        .reshape(9 * channels, channels)
    )
    feat_ext = padded_2(clip_feats, (("tile", 1),), 1)
    feat_columns = tile_columns(feat_ext, tile_rows, width_cells, False)
    pre = jnp.dot(feat_columns, spatial_weight, preferred_element_type=jnp.float32)
    act = jax.nn.silu(pre).astype(jnp.bfloat16)
    temporal_reach = 4 * TAP_DILATION
    if temporal_reach <= slab_frames:
        seq_shape = (slab_frames, tile_rows * width_cells, channels)
        act_ext = padded_2(act.reshape(seq_shape), (("frame", 0),), temporal_reach)
        grad_ext = padded_2(out_grad.reshape(seq_shape), (("frame", 0),), temporal_reach)
        act_grad = temporal_taps(grad_ext, temporal_back, slab_frames, True).astype(jnp.bfloat16)
        mixed = temporal_taps(act_ext, temporal_weight, slab_frames, False)
        out_slab = (clip_feats.reshape(-1, channels).astype(jnp.float32) + mixed).astype(
            jnp.bfloat16
        )
        out_slab = out_slab.reshape(clip_feats.shape)
    else:
        out_slab, act_grad = frame_exchange(
            clip_feats, out_grad, act, temporal_weight, temporal_back, temporal_reach
        )
    sig = jax.nn.sigmoid(pre)
    pre_grad = (act_grad.astype(jnp.float32) * (sig * (1.0 + pre * (1.0 - sig)))).astype(
        jnp.bfloat16
    )
    full_term = lax.dot_general(
        feat_columns, pre_grad, (((0,), (0,)), ((), ())), preferred_element_type=jnp.float32
    )
    summed = kernel_scatter(full_term, (("frame", frame_devs), ("tile", tile_devs)))
    weight_grad = summed * grad_scale
    grad_ext = padded_2(
        pre_grad.reshape(slab_frames, tile_rows, width_cells, channels), (("tile", 1),), 1
    )
    grad_columns = tile_columns(grad_ext, tile_rows, width_cells, True)
    local_back = jnp.dot(grad_columns, spatial_back, preferred_element_type=jnp.float32)
    input_grad = (out_grad.reshape(row_count, channels).astype(jnp.float32) + local_back).astype(
        jnp.bfloat16
    )
    input_grad = input_grad.reshape(slab_frames, tile_rows, width_cells, channels)
    return (out_slab, input_grad, weight_grad)


def solution(mesh):
    return jax.shard_map(
        per_device,
        mesh=mesh,
        in_specs=(
            P(("clip", "frame"), "tile", None, None),
            P(("clip", "frame"), "tile", None, None),
            P(),
            P(),
        ),
        out_specs=(
            P(("clip", "frame"), "tile", None, None),
            P(("clip", "frame"), "tile", None, None),
            P(("clip", "frame", "tile"), None),
        ),
        check_vma=False,
    )
```

```python
import functools
import math

import jax
import jax.numpy as jnp
from jax import lax
from jax.experimental import pallas as pl
from jax.experimental.pallas import tpu as pltpu
from jax.sharding import PartitionSpec as P

TAP_DILATION = 2


def padded_2(block, sides, width):
    for axis, dim in sides:
        count = lax.axis_size(axis)
        forward = [(i, i + 1) for i in range(count - 1)]
        backward = [(target, source) for source, target in forward]
        low = lax.ppermute(
            lax.slice_in_dim(block, block.shape[dim] - width, None, axis=dim), axis, forward
        )
        high = lax.ppermute(lax.slice_in_dim(block, 0, width, axis=dim), axis, backward)
        block = jnp.concatenate([low, block, high], axis=dim)
    return block


def halving_scatter(term, axes):
    sizes = [size for _, size in axes]
    if any(size & (size - 1) for size in sizes):
        return lax.psum_scatter(term, tuple(name for name, _ in axes), scatter_dimension=0, tiled=True)
    bits = []
    for name, size in axes:
        bits += [(name, size, b) for b in reversed(range(size.bit_length() - 1))]
    groups = 1
    for size in sizes:
        groups *= size
    block = term.shape[0] // groups
    x = term.reshape((2,) * len(bits) + (block,) + term.shape[1:])
    for pos in reversed(range(len(bits))):
        name, size, b = bits[pos]
        mine = (lax.axis_index(name) >> b) & 1
        keep = lax.dynamic_index_in_dim(x, mine, axis=pos, keepdims=False)
        send = lax.dynamic_index_in_dim(x, 1 - mine, axis=pos, keepdims=False)
        pairs = [(i, i ^ (1 << b)) for i in range(size)]
        x = keep + lax.ppermute(send, name, pairs)
    return x


def halving_kernel(groups, narrow, scale, x_ref, o_ref, ordered, *scratch):
    n = len(groups)
    send_sems, recv_sems = scratch[-2], scratch[-1]
    landings = scratch[:n]
    accs = scratch[n : 2 * n - 1]
    packs = scratch[2 * n - 1 : 2 * n - 1 + narrow]
    mesh_ids = pl.DeviceIdType.MESH
    plan = []
    for name, group_bits in groups:
        me = lax.axis_index(name)
        mine = [(me // (1 << b)) % 2 for b in group_bits]
        width = len(group_bits)
        own = 0
        for bit in mine:
            own = own * 2 + bit
        peers = []
        for mask in range(1, 1 << width):
            flips = [(mask >> (width - 1 - j)) % 2 for j in range(width)]
            partner = me
            chunk = 0
            for bit, flip, b in zip(mine, flips, group_bits):
                partner = partner + (1 - 2 * bit) * flip * (1 << b)
                chunk = chunk * 2 + bit + (1 - 2 * bit) * flip
            peers.append((mask, partner, chunk))
        plan.append((name, width, own, peers))
    barrier = pltpu.get_barrier_semaphore()
    contacts = 0
    for name, _, _, peers in plan:
        for _, partner, _ in peers:
            pl.semaphore_signal(barrier, inc=1, device_id={name: partner}, device_id_type=mesh_ids)
            contacts += 1
    blocks = x_ref.shape[0]
    width = blocks.bit_length() - 1
    for b in range(blocks):
        turned = int(format(b, "0%db" % width)[::-1], 2)
        ordered[turned] = x_ref[b]
    pl.semaphore_wait(barrier, contacts)
    source = ordered
    count = x_ref.shape[0]
    message = 0
    for k, (name, width, own, peers) in enumerate(plan):
        part = count >> width
        outbox = source
        if k < narrow:
            packs[k][...] = source[...].astype(packs[k].dtype)
            outbox = packs[k]
        copies = []
        for mask, partner, chunk in peers:
            copy = pltpu.make_async_remote_copy(
                src_ref=outbox.at[pl.ds(chunk * part, part)],
                dst_ref=landings[k].at[mask - 1],
                send_sem=send_sems.at[message],
                recv_sem=recv_sems.at[message],
                device_id={name: partner},
                device_id_type=mesh_ids,
            )
            copy.start()
            copies.append(copy)
            message += 1
        for copy in copies:
            copy.wait()
        total = source[pl.ds(own * part, part)]
        for slot in range(len(peers)):
            total = total + landings[k][slot].astype(jnp.float32)
        if k == n - 1:
            o_ref[...] = total[0] * scale
        else:
            accs[k][...] = total
            source = accs[k]
        count = part


def kernel_scatter(term, axes, scale):
    sizes = [size for _, size in axes]
    groups = 1
    for size in sizes:
        groups *= size
    per_block = term.shape[0] * term.shape[1] // groups
    if any(size & (size - 1) for size in sizes) or per_block % 128:
        return halving_scatter(term, axes) * jnp.float32(scale)
    bits = []
    for name, size in axes:
        bits += [(name, b) for b in reversed(range(size.bit_length() - 1))]
    n = len(bits)
    x = term.reshape(groups, per_block // 128, 128)
    steps = list(reversed(bits))
    plan = [(steps[0][0], [steps[0][1]])]
    for name, b in steps[1:]:
        last_name, last_bits = plan[-1]
        if len(plan) > 1 and last_name == name and len(last_bits) == 1:
            last_bits.append(b)
        else:
            plan.append((name, [b]))
    narrow = min(2, len(plan))
    rows = x.shape[1:]
    counts = [x.shape[0]]
    for _, group_bits in plan:
        counts.append(counts[-1] >> len(group_bits))
    scratch = [pltpu.VMEM(x.shape, x.dtype)]
    scratch += [
        pltpu.VMEM(
            ((1 << len(g[1])) - 1, counts[k + 1]) + rows,
            jnp.bfloat16 if k < narrow else jnp.float32,
        )
        for k, g in enumerate(plan)
    ]
    scratch += [pltpu.VMEM((counts[k + 1],) + rows, jnp.float32) for k in range(len(plan) - 1)]
    scratch += [pltpu.VMEM((counts[k],) + rows, jnp.bfloat16) for k in range(narrow)]
    messages = sum((1 << len(g[1])) - 1 for g in plan)
    scratch += [pltpu.SemaphoreType.DMA((messages,)), pltpu.SemaphoreType.DMA((messages,))]
    out = pl.pallas_call(
        functools.partial(halving_kernel, plan, narrow, scale),
        out_shape=jax.ShapeDtypeStruct(rows, x.dtype),
        in_specs=[pl.BlockSpec(memory_space=pltpu.VMEM)],
        out_specs=pl.BlockSpec(memory_space=pltpu.VMEM),
        scratch_shapes=scratch,
        compiler_params=pltpu.CompilerParams(collective_id=0, has_side_effects=True),
    )(x)
    return out.reshape(term.shape[0] // groups, term.shape[1])


def tile_columns(extended, tile_rows, width_cells, backward_pass):
    padded = jnp.pad(extended, ((0, 0), (0, 0), (1, 1), (0, 0)))
    pieces = []
    for row_shift in range(3):
        for col_shift in range(3):
            row_start = 2 - row_shift if backward_pass else row_shift
            col_start = 2 - col_shift if backward_pass else col_shift
            pieces.append(
                padded[:, row_start : row_start + tile_rows, col_start : col_start + width_cells, :]
            )
    channels = extended.shape[3]
    return jnp.concatenate(pieces, axis=-1).reshape(-1, 9 * channels)


def temporal_taps(padded_seq, weight, frame_count, backward_pass):
    pieces = []
    for temporal_tap_index in range(9):
        first_frame_index = (
            (8 - temporal_tap_index) * TAP_DILATION
            if backward_pass
            else temporal_tap_index * TAP_DILATION
        )
        pieces.append(padded_seq[first_frame_index : first_frame_index + frame_count])
    channels = padded_seq.shape[2]
    columns = jnp.concatenate(pieces, axis=-1).reshape(-1, 9 * channels)
    return jnp.dot(columns, weight, preferred_element_type=jnp.float32)


def frame_exchange(clip_feats, out_grad, act, temporal_weight, temporal_back, temporal_reach):
    slab_frames, tile_rows, width_cells, channels = clip_feats.shape
    row_count = slab_frames * tile_rows * width_cells
    frame_devs = lax.axis_size("frame")
    per_group = tile_rows * width_cells // frame_devs
    grouped = (slab_frames, frame_devs, per_group, channels)
    act_part = lax.all_to_all(
        act.reshape(grouped), "frame", split_axis=1, concat_axis=0, tiled=True
    )
    grad_part = lax.all_to_all(out_grad, "frame", split_axis=1, concat_axis=0, tiled=True)
    feat_part = lax.all_to_all(clip_feats, "frame", split_axis=1, concat_axis=0, tiled=True)
    frame_count = act_part.shape[0]
    item_count = act_part.shape[2]
    act_pad = jnp.pad(
        act_part.reshape(frame_count, item_count, channels),
        ((temporal_reach, temporal_reach), (0, 0), (0, 0)),
    )
    grad_pad = jnp.pad(
        grad_part.reshape(frame_count, item_count, channels),
        ((temporal_reach, temporal_reach), (0, 0), (0, 0)),
    )
    mixed = temporal_taps(act_pad, temporal_weight, frame_count, False)
    out_part = (feat_part.reshape(-1, channels).astype(jnp.float32) + mixed).astype(jnp.bfloat16)
    back_part = temporal_taps(grad_pad, temporal_back, frame_count, True).astype(jnp.bfloat16)
    out_part = out_part.reshape(frame_count, 1, item_count, channels)
    back_part = back_part.reshape(frame_count, 1, item_count, channels)
    out_slab = lax.all_to_all(out_part, "frame", split_axis=0, concat_axis=1, tiled=True)
    grad_slab = lax.all_to_all(back_part, "frame", split_axis=0, concat_axis=1, tiled=True)
    act_grad = grad_slab.reshape(row_count, channels)
    return out_slab, act_grad


def per_device(clip_feats, out_grad, spatial_weight, temporal_weight):
    slab_frames, tile_rows, width_cells, channels = clip_feats.shape
    row_count = slab_frames * tile_rows * width_cells
    frame_devs = lax.axis_size("frame")
    tile_devs = lax.axis_size("tile")
    grad_scale = 1.0 / math.sqrt(slab_frames * frame_devs * tile_rows * tile_devs * width_cells)
    spatial_back = (
        spatial_weight.reshape(9, channels, channels)
        .transpose(0, 2, 1)
        .reshape(9 * channels, channels)
    )
    temporal_back = (
        temporal_weight.reshape(9, channels, channels)
        .transpose(0, 2, 1)
        .reshape(9 * channels, channels)
    )
    feat_ext = padded_2(clip_feats, (("tile", 1),), 1)
    feat_columns = tile_columns(feat_ext, tile_rows, width_cells, False)
    pre = jnp.dot(feat_columns, spatial_weight, preferred_element_type=jnp.float32)
    act = jax.nn.silu(pre).astype(jnp.bfloat16)
    temporal_reach = 4 * TAP_DILATION
    if temporal_reach <= slab_frames:
        seq_shape = (slab_frames, tile_rows * width_cells, channels)
        act_ext = padded_2(act.reshape(seq_shape), (("frame", 0),), temporal_reach)
        grad_ext = padded_2(out_grad.reshape(seq_shape), (("frame", 0),), temporal_reach)
        act_grad = temporal_taps(grad_ext, temporal_back, slab_frames, True).astype(jnp.bfloat16)
        mixed = temporal_taps(act_ext, temporal_weight, slab_frames, False)
        out_slab = (clip_feats.reshape(-1, channels).astype(jnp.float32) + mixed).astype(
            jnp.bfloat16
        )
        out_slab = out_slab.reshape(clip_feats.shape)
    else:
        out_slab, act_grad = frame_exchange(
            clip_feats, out_grad, act, temporal_weight, temporal_back, temporal_reach
        )
    sig = jax.nn.sigmoid(pre)
    pre_grad = (act_grad.astype(jnp.float32) * (sig * (1.0 + pre * (1.0 - sig)))).astype(
        jnp.bfloat16
    )
    full_term = lax.dot_general(
        feat_columns, pre_grad, (((0,), (0,)), ((), ())), preferred_element_type=jnp.float32
    )
    weight_grad = kernel_scatter(
        full_term,
        (("frame", frame_devs), ("tile", tile_devs)),
        grad_scale,
    )
    grad_ext = padded_2(
        pre_grad.reshape(slab_frames, tile_rows, width_cells, channels), (("tile", 1),), 1
    )
    grad_columns = tile_columns(grad_ext, tile_rows, width_cells, True)
    local_back = jnp.dot(grad_columns, spatial_back, preferred_element_type=jnp.float32)
    input_grad = (out_grad.reshape(row_count, channels).astype(jnp.float32) + local_back).astype(
        jnp.bfloat16
    )
    input_grad = input_grad.reshape(slab_frames, tile_rows, width_cells, channels)
    return (out_slab, input_grad, weight_grad)


def solution(mesh):
    return jax.shard_map(
        per_device,
        mesh=mesh,
        in_specs=(
            P(("clip", "frame"), "tile", None, None),
            P(("clip", "frame"), "tile", None, None),
            P(),
            P(),
        ),
        out_specs=(
            P(("clip", "frame"), "tile", None, None),
            P(("clip", "frame"), "tile", None, None),
            P(("clip", "frame", "tile"), None),
        ),
        check_vma=False,
    )
```

```python
import functools
import math

import jax
import jax.numpy as jnp
from jax import lax
from jax.experimental import pallas as pl
from jax.experimental.pallas import tpu as pltpu
from jax.sharding import PartitionSpec as P

TAP_DILATION = 2


def padded_2(block, sides, width):
    for axis, dim in sides:
        count = lax.axis_size(axis)
        forward = [(i, i + 1) for i in range(count - 1)]
        backward = [(target, source) for source, target in forward]
        low = lax.ppermute(
            lax.slice_in_dim(block, block.shape[dim] - width, None, axis=dim), axis, forward
        )
        high = lax.ppermute(lax.slice_in_dim(block, 0, width, axis=dim), axis, backward)
        block = jnp.concatenate([low, block, high], axis=dim)
    return block


def halving_scatter(term, axes):
    sizes = [size for _, size in axes]
    if any(size & (size - 1) for size in sizes):
        return lax.psum_scatter(term, tuple(name for name, _ in axes), scatter_dimension=0, tiled=True)
    bits = []
    for name, size in axes:
        bits += [(name, size, b) for b in reversed(range(size.bit_length() - 1))]
    groups = 1
    for size in sizes:
        groups *= size
    block = term.shape[0] // groups
    x = term.reshape((2,) * len(bits) + (block,) + term.shape[1:])
    for pos in reversed(range(len(bits))):
        name, size, b = bits[pos]
        mine = (lax.axis_index(name) >> b) & 1
        keep = lax.dynamic_index_in_dim(x, mine, axis=pos, keepdims=False)
        send = lax.dynamic_index_in_dim(x, 1 - mine, axis=pos, keepdims=False)
        pairs = [(i, i ^ (1 << b)) for i in range(size)]
        x = keep + lax.ppermute(send, name, pairs)
    return x


def halving_kernel(
    groups, narrow, scale, dilation, x_ref, lo_ref, mid_ref, hi_ref, tw_ref, feat_ref,
    o_ref, bo_ref, ordered, acc_out, *scratch
):
    n = len(groups)
    slab, items, channels = mid_ref.shape
    slabs = (lo_ref, mid_ref, hi_ref)
    taps = tw_ref.shape[0] // channels
    acc_out[...] = jnp.zeros_like(acc_out)
    send_sems, recv_sems = scratch[-2], scratch[-1]
    landings = scratch[:n]
    accs = scratch[n : 2 * n - 1]
    packs = scratch[2 * n - 1 : 2 * n - 1 + narrow]
    mesh_ids = pl.DeviceIdType.MESH
    plan = []
    for name, group_bits in groups:
        me = lax.axis_index(name)
        mine = [(me // (1 << b)) % 2 for b in group_bits]
        width = len(group_bits)
        own = 0
        for bit in mine:
            own = own * 2 + bit
        peers = []
        for mask in range(1, 1 << width):
            flips = [(mask >> (width - 1 - j)) % 2 for j in range(width)]
            partner = me
            chunk = 0
            for bit, flip, b in zip(mine, flips, group_bits):
                partner = partner + (1 - 2 * bit) * flip * (1 << b)
                chunk = chunk * 2 + bit + (1 - 2 * bit) * flip
            peers.append((mask, partner, chunk))
        plan.append((name, width, own, peers))
    barrier = pltpu.get_barrier_semaphore()
    contacts = 0
    for name, _, _, peers in plan:
        for _, partner, _ in peers:
            pl.semaphore_signal(barrier, inc=1, device_id={name: partner}, device_id_type=mesh_ids)
            contacts += 1
    blocks = x_ref.shape[0]
    width = blocks.bit_length() - 1
    for b in range(blocks):
        turned = int(format(b, "0%db" % width)[::-1], 2)
        ordered[turned] = x_ref[b]
    pl.semaphore_wait(barrier, contacts)
    source = ordered
    count = x_ref.shape[0]
    message = 0
    for k, (name, width, own, peers) in enumerate(plan):
        part = count >> width
        outbox = source
        if k < narrow:
            packs[k][...] = source[...].astype(packs[k].dtype)
            outbox = packs[k]
        copies = []
        for mask, partner, chunk in peers:
            copy = pltpu.make_async_remote_copy(
                src_ref=outbox.at[pl.ds(chunk * part, part)],
                dst_ref=landings[k].at[mask - 1],
                send_sem=send_sems.at[message],
                recv_sem=recv_sems.at[message],
                device_id={name: partner},
                device_id_type=mesh_ids,
            )
            copy.start()
            copies.append(copy)
            message += 1
        for tap in range(k * taps // n, (k + 1) * taps // n):
            weight = tw_ref[pl.ds(tap * channels, channels), :]
            which, off = divmod(tap * dilation, slab)
            first = (slab - off) * items
            head = slabs[which][off:slab].reshape(first, channels)
            acc_out[0:first, :] += jnp.dot(head, weight, preferred_element_type=jnp.float32)
            if off:
                tail = slabs[which + 1][0:off].reshape(off * items, channels)
                acc_out[first:, :] += jnp.dot(tail, weight, preferred_element_type=jnp.float32)
        for copy in copies:
            copy.wait()
        total = source[pl.ds(own * part, part)]
        for slot in range(len(peers)):
            total = total + landings[k][slot].astype(jnp.float32)
        if k == n - 1:
            o_ref[...] = total[0] * scale
            bo_ref[...] = (feat_ref[...].astype(jnp.float32) + acc_out[...]).astype(bo_ref.dtype)
        else:
            accs[k][...] = total
            source = accs[k]
        count = part


def forward_taps(lo, mid, hi, weight, feat):
    mixed = temporal_taps(jnp.concatenate([lo, mid, hi], axis=0), weight, mid.shape[0], False)
    return (feat.astype(jnp.float32) + mixed).astype(feat.dtype)


def kernel_scatter(term, axes, scale, forward):
    sizes = [size for _, size in axes]
    groups = 1
    for size in sizes:
        groups *= size
    per_block = term.shape[0] * term.shape[1] // groups
    if any(size & (size - 1) for size in sizes) or per_block % 128:
        return halving_scatter(term, axes) * jnp.float32(scale), forward_taps(*forward)
    bits = []
    for name, size in axes:
        bits += [(name, b) for b in reversed(range(size.bit_length() - 1))]
    n = len(bits)
    x = term.reshape(groups, per_block // 128, 128)
    steps = list(reversed(bits))
    plan = [(steps[0][0], [steps[0][1]])]
    for name, b in steps[1:]:
        last_name, last_bits = plan[-1]
        if len(plan) > 1 and last_name == name and len(last_bits) == 1:
            last_bits.append(b)
        else:
            plan.append((name, [b]))
    narrow = min(2, len(plan))
    rows = x.shape[1:]
    counts = [x.shape[0]]
    for _, group_bits in plan:
        counts.append(counts[-1] >> len(group_bits))
    scratch = [pltpu.VMEM(x.shape, x.dtype), pltpu.VMEM(forward[4].shape, jnp.float32)]
    scratch += [
        pltpu.VMEM(
            ((1 << len(g[1])) - 1, counts[k + 1]) + rows,
            jnp.bfloat16 if k < narrow else jnp.float32,
        )
        for k, g in enumerate(plan)
    ]
    scratch += [pltpu.VMEM((counts[k + 1],) + rows, jnp.float32) for k in range(len(plan) - 1)]
    scratch += [pltpu.VMEM((counts[k],) + rows, jnp.bfloat16) for k in range(narrow)]
    messages = sum((1 << len(g[1])) - 1 for g in plan)
    scratch += [pltpu.SemaphoreType.DMA((messages,)), pltpu.SemaphoreType.DMA((messages,))]
    out, block_out = pl.pallas_call(
        functools.partial(halving_kernel, plan, narrow, scale, TAP_DILATION),
        out_shape=(
            jax.ShapeDtypeStruct(rows, x.dtype),
            jax.ShapeDtypeStruct(forward[4].shape, forward[4].dtype),
        ),
        in_specs=[pl.BlockSpec(memory_space=pltpu.VMEM)] * 6,
        out_specs=(pl.BlockSpec(memory_space=pltpu.VMEM),) * 2,
        scratch_shapes=scratch,
        compiler_params=pltpu.CompilerParams(collective_id=0, has_side_effects=True),
    )(x, *forward)
    return out.reshape(term.shape[0] // groups, term.shape[1]), block_out


def tile_columns(extended, tile_rows, width_cells, backward_pass):
    padded = jnp.pad(extended, ((0, 0), (0, 0), (1, 1), (0, 0)))
    pieces = []
    for row_shift in range(3):
        for col_shift in range(3):
            row_start = 2 - row_shift if backward_pass else row_shift
            col_start = 2 - col_shift if backward_pass else col_shift
            pieces.append(
                padded[:, row_start : row_start + tile_rows, col_start : col_start + width_cells, :]
            )
    channels = extended.shape[3]
    return jnp.concatenate(pieces, axis=-1).reshape(-1, 9 * channels)


def temporal_taps(padded_seq, weight, frame_count, backward_pass):
    pieces = []
    for temporal_tap_index in range(9):
        first_frame_index = (
            (8 - temporal_tap_index) * TAP_DILATION
            if backward_pass
            else temporal_tap_index * TAP_DILATION
        )
        pieces.append(padded_seq[first_frame_index : first_frame_index + frame_count])
    channels = padded_seq.shape[2]
    columns = jnp.concatenate(pieces, axis=-1).reshape(-1, 9 * channels)
    return jnp.dot(columns, weight, preferred_element_type=jnp.float32)


def frame_exchange(clip_feats, out_grad, act, temporal_weight, temporal_back, temporal_reach):
    slab_frames, tile_rows, width_cells, channels = clip_feats.shape
    row_count = slab_frames * tile_rows * width_cells
    frame_devs = lax.axis_size("frame")
    per_group = tile_rows * width_cells // frame_devs
    grouped = (slab_frames, frame_devs, per_group, channels)
    act_part = lax.all_to_all(
        act.reshape(grouped), "frame", split_axis=1, concat_axis=0, tiled=True
    )
    grad_part = lax.all_to_all(out_grad, "frame", split_axis=1, concat_axis=0, tiled=True)
    feat_part = lax.all_to_all(clip_feats, "frame", split_axis=1, concat_axis=0, tiled=True)
    frame_count = act_part.shape[0]
    item_count = act_part.shape[2]
    act_pad = jnp.pad(
        act_part.reshape(frame_count, item_count, channels),
        ((temporal_reach, temporal_reach), (0, 0), (0, 0)),
    )
    grad_pad = jnp.pad(
        grad_part.reshape(frame_count, item_count, channels),
        ((temporal_reach, temporal_reach), (0, 0), (0, 0)),
    )
    mixed = temporal_taps(act_pad, temporal_weight, frame_count, False)
    out_part = (feat_part.reshape(-1, channels).astype(jnp.float32) + mixed).astype(jnp.bfloat16)
    back_part = temporal_taps(grad_pad, temporal_back, frame_count, True).astype(jnp.bfloat16)
    out_part = out_part.reshape(frame_count, 1, item_count, channels)
    back_part = back_part.reshape(frame_count, 1, item_count, channels)
    out_slab = lax.all_to_all(out_part, "frame", split_axis=0, concat_axis=1, tiled=True)
    grad_slab = lax.all_to_all(back_part, "frame", split_axis=0, concat_axis=1, tiled=True)
    act_grad = grad_slab.reshape(row_count, channels)
    return out_slab, act_grad


def per_device(clip_feats, out_grad, spatial_weight, temporal_weight):
    slab_frames, tile_rows, width_cells, channels = clip_feats.shape
    row_count = slab_frames * tile_rows * width_cells
    frame_devs = lax.axis_size("frame")
    tile_devs = lax.axis_size("tile")
    grad_scale = 1.0 / math.sqrt(slab_frames * frame_devs * tile_rows * tile_devs * width_cells)
    spatial_back = (
        spatial_weight.reshape(9, channels, channels)
        .transpose(0, 2, 1)
        .reshape(9 * channels, channels)
    )
    temporal_back = (
        temporal_weight.reshape(9, channels, channels)
        .transpose(0, 2, 1)
        .reshape(9 * channels, channels)
    )
    feat_ext = padded_2(clip_feats, (("tile", 1),), 1)
    feat_columns = tile_columns(feat_ext, tile_rows, width_cells, False)
    pre = jnp.dot(feat_columns, spatial_weight, preferred_element_type=jnp.float32)
    act = jax.nn.silu(pre).astype(jnp.bfloat16)
    temporal_reach = 4 * TAP_DILATION
    if temporal_reach <= slab_frames:
        seq_shape = (slab_frames, tile_rows * width_cells, channels)
        act_ext = padded_2(act.reshape(seq_shape), (("frame", 0),), temporal_reach)
        grad_ext = padded_2(out_grad.reshape(seq_shape), (("frame", 0),), temporal_reach)
        act_grad = temporal_taps(grad_ext, temporal_back, slab_frames, True).astype(jnp.bfloat16)
        forward = (
            act_ext[:slab_frames],
            act_ext[slab_frames : 2 * slab_frames],
            act_ext[2 * slab_frames :],
            temporal_weight,
            clip_feats.reshape(-1, channels),
        )
        out_slab = None
    else:
        out_slab, act_grad = frame_exchange(
            clip_feats, out_grad, act, temporal_weight, temporal_back, temporal_reach
        )
    sig = jax.nn.sigmoid(pre)
    pre_grad = (act_grad.astype(jnp.float32) * (sig * (1.0 + pre * (1.0 - sig)))).astype(
        jnp.bfloat16
    )
    full_term = lax.dot_general(
        feat_columns, pre_grad, (((0,), (0,)), ((), ())), preferred_element_type=jnp.float32
    )
    mesh_axes = (("frame", frame_devs), ("tile", tile_devs))
    if out_slab is None and temporal_reach == slab_frames:
        weight_grad, out_slab = kernel_scatter(full_term, mesh_axes, grad_scale, forward)
        out_slab = out_slab.reshape(clip_feats.shape)
    else:
        if out_slab is None:
            out_slab = forward_taps(*forward).reshape(clip_feats.shape)
        weight_grad = halving_scatter(full_term, mesh_axes) * jnp.float32(grad_scale)
    grad_ext = padded_2(
        pre_grad.reshape(slab_frames, tile_rows, width_cells, channels), (("tile", 1),), 1
    )
    grad_columns = tile_columns(grad_ext, tile_rows, width_cells, True)
    local_back = jnp.dot(grad_columns, spatial_back, preferred_element_type=jnp.float32)
    input_grad = (out_grad.reshape(row_count, channels).astype(jnp.float32) + local_back).astype(
        jnp.bfloat16
    )
    input_grad = input_grad.reshape(slab_frames, tile_rows, width_cells, channels)
    return (out_slab, input_grad, weight_grad)


def solution(mesh):
    return jax.shard_map(
        per_device,
        mesh=mesh,
        in_specs=(
            P(("clip", "frame"), "tile", None, None),
            P(("clip", "frame"), "tile", None, None),
            P(),
            P(),
        ),
        out_specs=(
            P(("clip", "frame"), "tile", None, None),
            P(("clip", "frame"), "tile", None, None),
            P(("clip", "frame", "tile"), None),
        ),
        check_vma=False,
    )
```

```python
import functools
import math

import jax
import jax.numpy as jnp
from jax import lax
from jax.experimental import pallas as pl
from jax.experimental.pallas import tpu as pltpu
from jax.sharding import PartitionSpec as P

TAP_DILATION = 2


def padded_2(block, sides, width):
    for axis, dim in sides:
        count = lax.axis_size(axis)
        forward = [(i, i + 1) for i in range(count - 1)]
        backward = [(target, source) for source, target in forward]
        low = lax.ppermute(
            lax.slice_in_dim(block, block.shape[dim] - width, None, axis=dim), axis, forward
        )
        high = lax.ppermute(lax.slice_in_dim(block, 0, width, axis=dim), axis, backward)
        block = jnp.concatenate([low, block, high], axis=dim)
    return block


def halving_scatter(term, axes):
    sizes = [size for _, size in axes]
    if any(size & (size - 1) for size in sizes):
        return lax.psum_scatter(term, tuple(name for name, _ in axes), scatter_dimension=0, tiled=True)
    bits = []
    for name, size in axes:
        bits += [(name, size, b) for b in reversed(range(size.bit_length() - 1))]
    groups = 1
    for size in sizes:
        groups *= size
    block = term.shape[0] // groups
    x = term.reshape((2,) * len(bits) + (block,) + term.shape[1:])
    for pos in reversed(range(len(bits))):
        name, size, b = bits[pos]
        mine = (lax.axis_index(name) >> b) & 1
        keep = lax.dynamic_index_in_dim(x, mine, axis=pos, keepdims=False)
        send = lax.dynamic_index_in_dim(x, 1 - mine, axis=pos, keepdims=False)
        pairs = [(i, i ^ (1 << b)) for i in range(size)]
        x = keep + lax.ppermute(send, name, pairs)
    return x


def halving_kernel(groups, narrow, scale, x_ref, o_ref, ordered, *scratch):
    n = len(groups)
    send_sems, recv_sems = scratch[-2], scratch[-1]
    landings = scratch[:n]
    accs = scratch[n : 2 * n - 1]
    packs = scratch[2 * n - 1 : 2 * n - 1 + narrow]
    mesh_ids = pl.DeviceIdType.MESH
    plan = []
    for name, group_bits in groups:
        me = lax.axis_index(name)
        mine = [(me // (1 << b)) % 2 for b in group_bits]
        width = len(group_bits)
        own = 0
        for bit in mine:
            own = own * 2 + bit
        peers = []
        for mask in range(1, 1 << width):
            flips = [(mask >> (width - 1 - j)) % 2 for j in range(width)]
            partner = me
            chunk = 0
            for bit, flip, b in zip(mine, flips, group_bits):
                partner = partner + (1 - 2 * bit) * flip * (1 << b)
                chunk = chunk * 2 + bit + (1 - 2 * bit) * flip
            peers.append((mask, partner, chunk))
        plan.append((name, width, own, peers))
    barrier = pltpu.get_barrier_semaphore()
    contacts = 0
    for name, _, _, peers in plan:
        for _, partner, _ in peers:
            pl.semaphore_signal(barrier, inc=1, device_id={name: partner}, device_id_type=mesh_ids)
            contacts += 1
    blocks = ordered.shape[0]
    rows_in = x_ref.shape[0] // blocks
    width = blocks.bit_length() - 1
    for b in range(blocks):
        turned = int(format(b, "0%db" % width)[::-1], 2)
        ordered[turned] = x_ref[b * rows_in : (b + 1) * rows_in, :].reshape(ordered.shape[1:])
    pl.semaphore_wait(barrier, contacts)
    source = ordered
    count = ordered.shape[0]
    message = 0
    for k, (name, width, own, peers) in enumerate(plan):
        part = count >> width
        outbox = source
        if k < narrow:
            packs[k][...] = source[...].astype(packs[k].dtype)
            outbox = packs[k]
        copies = []
        for mask, partner, chunk in peers:
            copy = pltpu.make_async_remote_copy(
                src_ref=outbox.at[pl.ds(chunk * part, part)],
                dst_ref=landings[k].at[mask - 1],
                send_sem=send_sems.at[message],
                recv_sem=recv_sems.at[message],
                device_id={name: partner},
                device_id_type=mesh_ids,
            )
            copy.start()
            copies.append(copy)
            message += 1
        for copy in copies:
            copy.wait()
        total = source[pl.ds(own * part, part)]
        for slot in range(len(peers)):
            total = total + landings[k][slot].astype(jnp.float32)
        if k == n - 1:
            o_ref[...] = total[0] * scale
        else:
            accs[k][...] = total
            source = accs[k]
        count = part


def kernel_scatter(term, axes, scale):
    sizes = [size for _, size in axes]
    groups = 1
    for size in sizes:
        groups *= size
    per_block = term.shape[0] * term.shape[1] // groups
    if any(size & (size - 1) for size in sizes) or per_block % 128:
        return halving_scatter(term, axes) * jnp.float32(scale)
    bits = []
    for name, size in axes:
        bits += [(name, b) for b in reversed(range(size.bit_length() - 1))]
    n = len(bits)
    x = term
    block_rows = term.shape[0] // groups
    steps = list(reversed(bits))
    plan = [(steps[0][0], [steps[0][1]])]
    for name, b in steps[1:]:
        last_name, last_bits = plan[-1]
        if len(plan) > 1 and last_name == name and len(last_bits) == 1:
            last_bits.append(b)
        else:
            plan.append((name, [b]))
    narrow = min(2, len(plan))
    rows = (per_block // 128, 128)
    staged = (groups,) + rows
    counts = [groups]
    for _, group_bits in plan:
        counts.append(counts[-1] >> len(group_bits))
    scratch = [pltpu.VMEM(staged, x.dtype)]
    scratch += [
        pltpu.VMEM(
            ((1 << len(g[1])) - 1, counts[k + 1]) + rows,
            jnp.bfloat16 if k < narrow else jnp.float32,
        )
        for k, g in enumerate(plan)
    ]
    scratch += [pltpu.VMEM((counts[k + 1],) + rows, jnp.float32) for k in range(len(plan) - 1)]
    scratch += [pltpu.VMEM((counts[k],) + rows, jnp.bfloat16) for k in range(narrow)]
    messages = sum((1 << len(g[1])) - 1 for g in plan)
    scratch += [pltpu.SemaphoreType.DMA((messages,)), pltpu.SemaphoreType.DMA((messages,))]
    out = pl.pallas_call(
        functools.partial(halving_kernel, plan, narrow, scale),
        out_shape=jax.ShapeDtypeStruct(rows, x.dtype),
        in_specs=[pl.BlockSpec(memory_space=pltpu.VMEM)],
        out_specs=pl.BlockSpec(memory_space=pltpu.VMEM),
        scratch_shapes=scratch,
        compiler_params=pltpu.CompilerParams(collective_id=0, has_side_effects=True),
    )(x)
    return out.reshape(term.shape[0] // groups, term.shape[1])


def tile_columns(extended, tile_rows, width_cells, backward_pass):
    padded = jnp.pad(extended, ((0, 0), (0, 0), (1, 1), (0, 0)))
    pieces = []
    for row_shift in range(3):
        for col_shift in range(3):
            row_start = 2 - row_shift if backward_pass else row_shift
            col_start = 2 - col_shift if backward_pass else col_shift
            pieces.append(
                padded[:, row_start : row_start + tile_rows, col_start : col_start + width_cells, :]
            )
    channels = extended.shape[3]
    return jnp.concatenate(pieces, axis=-1).reshape(-1, 9 * channels)


def temporal_taps(padded_seq, weight, frame_count, backward_pass):
    pieces = []
    for temporal_tap_index in range(9):
        first_frame_index = (
            (8 - temporal_tap_index) * TAP_DILATION
            if backward_pass
            else temporal_tap_index * TAP_DILATION
        )
        pieces.append(padded_seq[first_frame_index : first_frame_index + frame_count])
    channels = padded_seq.shape[2]
    columns = jnp.concatenate(pieces, axis=-1).reshape(-1, 9 * channels)
    return jnp.dot(columns, weight, preferred_element_type=jnp.float32)


def frame_exchange(clip_feats, out_grad, act, temporal_weight, temporal_back, temporal_reach):
    slab_frames, tile_rows, width_cells, channels = clip_feats.shape
    row_count = slab_frames * tile_rows * width_cells
    frame_devs = lax.axis_size("frame")
    per_group = tile_rows * width_cells // frame_devs
    grouped = (slab_frames, frame_devs, per_group, channels)
    act_part = lax.all_to_all(
        act.reshape(grouped), "frame", split_axis=1, concat_axis=0, tiled=True
    )
    grad_part = lax.all_to_all(out_grad, "frame", split_axis=1, concat_axis=0, tiled=True)
    feat_part = lax.all_to_all(clip_feats, "frame", split_axis=1, concat_axis=0, tiled=True)
    frame_count = act_part.shape[0]
    item_count = act_part.shape[2]
    act_pad = jnp.pad(
        act_part.reshape(frame_count, item_count, channels),
        ((temporal_reach, temporal_reach), (0, 0), (0, 0)),
    )
    grad_pad = jnp.pad(
        grad_part.reshape(frame_count, item_count, channels),
        ((temporal_reach, temporal_reach), (0, 0), (0, 0)),
    )
    mixed = temporal_taps(act_pad, temporal_weight, frame_count, False)
    out_part = (feat_part.reshape(-1, channels).astype(jnp.float32) + mixed).astype(jnp.bfloat16)
    back_part = temporal_taps(grad_pad, temporal_back, frame_count, True).astype(jnp.bfloat16)
    out_part = out_part.reshape(frame_count, 1, item_count, channels)
    back_part = back_part.reshape(frame_count, 1, item_count, channels)
    out_slab = lax.all_to_all(out_part, "frame", split_axis=0, concat_axis=1, tiled=True)
    grad_slab = lax.all_to_all(back_part, "frame", split_axis=0, concat_axis=1, tiled=True)
    act_grad = grad_slab.reshape(row_count, channels)
    return out_slab, act_grad


def per_device(clip_feats, out_grad, spatial_weight, temporal_weight):
    slab_frames, tile_rows, width_cells, channels = clip_feats.shape
    row_count = slab_frames * tile_rows * width_cells
    frame_devs = lax.axis_size("frame")
    tile_devs = lax.axis_size("tile")
    grad_scale = 1.0 / math.sqrt(slab_frames * frame_devs * tile_rows * tile_devs * width_cells)
    spatial_back = (
        spatial_weight.reshape(9, channels, channels)
        .transpose(0, 2, 1)
        .reshape(9 * channels, channels)
    )
    temporal_back = (
        temporal_weight.reshape(9, channels, channels)
        .transpose(0, 2, 1)
        .reshape(9 * channels, channels)
    )
    feat_ext = padded_2(clip_feats, (("tile", 1),), 1)
    feat_columns = tile_columns(feat_ext, tile_rows, width_cells, False)
    pre = jnp.dot(feat_columns, spatial_weight, preferred_element_type=jnp.float32)
    act = jax.nn.silu(pre).astype(jnp.bfloat16)
    temporal_reach = 4 * TAP_DILATION
    if temporal_reach <= slab_frames:
        seq_shape = (slab_frames, tile_rows * width_cells, channels)
        act_ext = padded_2(act.reshape(seq_shape), (("frame", 0),), temporal_reach)
        grad_ext = padded_2(out_grad.reshape(seq_shape), (("frame", 0),), temporal_reach)
        act_grad = temporal_taps(grad_ext, temporal_back, slab_frames, True).astype(jnp.bfloat16)
        mixed = temporal_taps(act_ext, temporal_weight, slab_frames, False)
        out_slab = (clip_feats.reshape(-1, channels).astype(jnp.float32) + mixed).astype(
            jnp.bfloat16
        )
        out_slab = out_slab.reshape(clip_feats.shape)
    else:
        out_slab, act_grad = frame_exchange(
            clip_feats, out_grad, act, temporal_weight, temporal_back, temporal_reach
        )
    sig = jax.nn.sigmoid(pre)
    pre_grad = (act_grad.astype(jnp.float32) * (sig * (1.0 + pre * (1.0 - sig)))).astype(
        jnp.bfloat16
    )
    full_term = lax.dot_general(
        feat_columns, pre_grad, (((0,), (0,)), ((), ())), preferred_element_type=jnp.float32
    )
    weight_grad = kernel_scatter(
        full_term,
        (("frame", frame_devs), ("tile", tile_devs)),
        grad_scale,
    )
    grad_ext = padded_2(
        pre_grad.reshape(slab_frames, tile_rows, width_cells, channels), (("tile", 1),), 1
    )
    grad_columns = tile_columns(grad_ext, tile_rows, width_cells, True)
    local_back = jnp.dot(grad_columns, spatial_back, preferred_element_type=jnp.float32)
    input_grad = (out_grad.reshape(row_count, channels).astype(jnp.float32) + local_back).astype(
        jnp.bfloat16
    )
    input_grad = input_grad.reshape(slab_frames, tile_rows, width_cells, channels)
    return (out_slab, input_grad, weight_grad)


def solution(mesh):
    return jax.shard_map(
        per_device,
        mesh=mesh,
        in_specs=(
            P(("clip", "frame"), "tile", None, None),
            P(("clip", "frame"), "tile", None, None),
            P(),
            P(),
        ),
        out_specs=(
            P(("clip", "frame"), "tile", None, None),
            P(("clip", "frame"), "tile", None, None),
            P(("clip", "frame", "tile"), None),
        ),
        check_vma=False,
    )
```

```python
import functools
import math

import jax
import jax.numpy as jnp
from jax import lax
from jax.experimental import pallas as pl
from jax.experimental.pallas import tpu as pltpu
from jax.sharding import PartitionSpec as P

TAP_DILATION = 2


def padded_2(block, sides, width):
    for axis, dim in sides:
        count = lax.axis_size(axis)
        forward = [(i, i + 1) for i in range(count - 1)]
        backward = [(target, source) for source, target in forward]
        low = lax.ppermute(
            lax.slice_in_dim(block, block.shape[dim] - width, None, axis=dim), axis, forward
        )
        high = lax.ppermute(lax.slice_in_dim(block, 0, width, axis=dim), axis, backward)
        block = jnp.concatenate([low, block, high], axis=dim)
    return block


def halving_scatter(term, axes):
    sizes = [size for _, size in axes]
    if any(size & (size - 1) for size in sizes):
        return lax.psum_scatter(term, tuple(name for name, _ in axes), scatter_dimension=0, tiled=True)
    bits = []
    for name, size in axes:
        bits += [(name, size, b) for b in reversed(range(size.bit_length() - 1))]
    groups = 1
    for size in sizes:
        groups *= size
    block = term.shape[0] // groups
    x = term.reshape((2,) * len(bits) + (block,) + term.shape[1:])
    for pos in reversed(range(len(bits))):
        name, size, b = bits[pos]
        mine = (lax.axis_index(name) >> b) & 1
        keep = lax.dynamic_index_in_dim(x, mine, axis=pos, keepdims=False)
        send = lax.dynamic_index_in_dim(x, 1 - mine, axis=pos, keepdims=False)
        pairs = [(i, i ^ (1 << b)) for i in range(size)]
        x = keep + lax.ppermute(send, name, pairs)
    return x


def halving_kernel(groups, narrow, scale, x_ref, o_ref, ordered, *scratch):
    n = len(groups)
    send_sems, recv_sems = scratch[-2], scratch[-1]
    landings = scratch[:n]
    accs = scratch[n : 2 * n - 1]
    packs = scratch[2 * n - 1 : 2 * n - 1 + narrow]
    mesh_ids = pl.DeviceIdType.MESH
    plan = []
    for name, group_bits in groups:
        me = lax.axis_index(name)
        mine = [(me // (1 << b)) % 2 for b in group_bits]
        width = len(group_bits)
        own = 0
        for bit in mine:
            own = own * 2 + bit
        peers = []
        for mask in range(1, 1 << width):
            flips = [(mask >> (width - 1 - j)) % 2 for j in range(width)]
            partner = me
            chunk = 0
            for bit, flip, b in zip(mine, flips, group_bits):
                partner = partner + (1 - 2 * bit) * flip * (1 << b)
                chunk = chunk * 2 + bit + (1 - 2 * bit) * flip
            peers.append((mask, partner, chunk))
        plan.append((name, width, own, peers))
    barrier = pltpu.get_barrier_semaphore()
    contacts = 0
    for name, _, _, peers in plan:
        for _, partner, _ in peers:
            pl.semaphore_signal(barrier, inc=1, device_id={name: partner}, device_id_type=mesh_ids)
            contacts += 1
    blocks = x_ref.shape[0]
    width = blocks.bit_length() - 1
    for b in range(blocks):
        turned = int(format(b, "0%db" % width)[::-1], 2)
        ordered[turned] = x_ref[b]
    pl.semaphore_wait(barrier, contacts)
    source = ordered
    count = x_ref.shape[0]
    message = 0
    for k, (name, width, own, peers) in enumerate(plan):
        part = count >> width
        copies = []
        for mask, partner, chunk in peers:
            outgoing = source.at[pl.ds(chunk * part, part)]
            if k < narrow:
                packs[k][mask - 1] = outgoing[...].astype(packs[k].dtype)
                outgoing = packs[k].at[mask - 1]
            copy = pltpu.make_async_remote_copy(
                src_ref=outgoing,
                dst_ref=landings[k].at[mask - 1],
                send_sem=send_sems.at[message],
                recv_sem=recv_sems.at[message],
                device_id={name: partner},
                device_id_type=mesh_ids,
            )
            copy.start()
            copies.append(copy)
            message += 1
        total = source[pl.ds(own * part, part)]
        for slot, copy in enumerate(copies):
            copy.wait()
            total = total + landings[k][slot].astype(jnp.float32)
        if k == n - 1:
            o_ref[...] = total[0] * scale
        else:
            accs[k][...] = total
            source = accs[k]
        count = part


def kernel_scatter(term, axes, scale):
    sizes = [size for _, size in axes]
    groups = 1
    for size in sizes:
        groups *= size
    per_block = term.shape[0] * term.shape[1] // groups
    if any(size & (size - 1) for size in sizes) or per_block % 128:
        return halving_scatter(term, axes) * jnp.float32(scale)
    bits = []
    for name, size in axes:
        bits += [(name, b) for b in reversed(range(size.bit_length() - 1))]
    n = len(bits)
    x = term.reshape(groups, per_block // 128, 128)
    steps = list(reversed(bits))
    plan = [(steps[0][0], [steps[0][1]])]
    for name, b in steps[1:]:
        last_name, last_bits = plan[-1]
        if len(plan) > 1 and last_name == name and len(last_bits) == 1:
            last_bits.append(b)
        else:
            plan.append((name, [b]))
    narrow = min(2, len(plan))
    rows = x.shape[1:]
    counts = [x.shape[0]]
    for _, group_bits in plan:
        counts.append(counts[-1] >> len(group_bits))
    scratch = [pltpu.VMEM(x.shape, x.dtype)]
    scratch += [
        pltpu.VMEM(
            ((1 << len(g[1])) - 1, counts[k + 1]) + rows,
            jnp.bfloat16 if k < narrow else jnp.float32,
        )
        for k, g in enumerate(plan)
    ]
    scratch += [pltpu.VMEM((counts[k + 1],) + rows, jnp.float32) for k in range(len(plan) - 1)]
    scratch += [
        pltpu.VMEM(((1 << len(plan[k][1])) - 1, counts[k + 1]) + rows, jnp.bfloat16)
        for k in range(narrow)
    ]
    messages = sum((1 << len(g[1])) - 1 for g in plan)
    scratch += [pltpu.SemaphoreType.DMA((messages,)), pltpu.SemaphoreType.DMA((messages,))]
    out = pl.pallas_call(
        functools.partial(halving_kernel, plan, narrow, scale),
        out_shape=jax.ShapeDtypeStruct(rows, x.dtype),
        in_specs=[pl.BlockSpec(memory_space=pltpu.VMEM)],
        out_specs=pl.BlockSpec(memory_space=pltpu.VMEM),
        scratch_shapes=scratch,
        compiler_params=pltpu.CompilerParams(collective_id=0, has_side_effects=True),
    )(x)
    return out.reshape(term.shape[0] // groups, term.shape[1])


def tile_columns(extended, tile_rows, width_cells, backward_pass):
    padded = jnp.pad(extended, ((0, 0), (0, 0), (1, 1), (0, 0)))
    pieces = []
    for row_shift in range(3):
        for col_shift in range(3):
            row_start = 2 - row_shift if backward_pass else row_shift
            col_start = 2 - col_shift if backward_pass else col_shift
            pieces.append(
                padded[:, row_start : row_start + tile_rows, col_start : col_start + width_cells, :]
            )
    channels = extended.shape[3]
    return jnp.concatenate(pieces, axis=-1).reshape(-1, 9 * channels)


def temporal_taps(padded_seq, weight, frame_count, backward_pass):
    pieces = []
    for temporal_tap_index in range(9):
        first_frame_index = (
            (8 - temporal_tap_index) * TAP_DILATION
            if backward_pass
            else temporal_tap_index * TAP_DILATION
        )
        pieces.append(padded_seq[first_frame_index : first_frame_index + frame_count])
    channels = padded_seq.shape[2]
    columns = jnp.concatenate(pieces, axis=-1).reshape(-1, 9 * channels)
    return jnp.dot(columns, weight, preferred_element_type=jnp.float32)


def frame_exchange(clip_feats, out_grad, act, temporal_weight, temporal_back, temporal_reach):
    slab_frames, tile_rows, width_cells, channels = clip_feats.shape
    row_count = slab_frames * tile_rows * width_cells
    frame_devs = lax.axis_size("frame")
    per_group = tile_rows * width_cells // frame_devs
    grouped = (slab_frames, frame_devs, per_group, channels)
    act_part = lax.all_to_all(
        act.reshape(grouped), "frame", split_axis=1, concat_axis=0, tiled=True
    )
    grad_part = lax.all_to_all(out_grad, "frame", split_axis=1, concat_axis=0, tiled=True)
    feat_part = lax.all_to_all(clip_feats, "frame", split_axis=1, concat_axis=0, tiled=True)
    frame_count = act_part.shape[0]
    item_count = act_part.shape[2]
    act_pad = jnp.pad(
        act_part.reshape(frame_count, item_count, channels),
        ((temporal_reach, temporal_reach), (0, 0), (0, 0)),
    )
    grad_pad = jnp.pad(
        grad_part.reshape(frame_count, item_count, channels),
        ((temporal_reach, temporal_reach), (0, 0), (0, 0)),
    )
    mixed = temporal_taps(act_pad, temporal_weight, frame_count, False)
    out_part = (feat_part.reshape(-1, channels).astype(jnp.float32) + mixed).astype(jnp.bfloat16)
    back_part = temporal_taps(grad_pad, temporal_back, frame_count, True).astype(jnp.bfloat16)
    out_part = out_part.reshape(frame_count, 1, item_count, channels)
    back_part = back_part.reshape(frame_count, 1, item_count, channels)
    out_slab = lax.all_to_all(out_part, "frame", split_axis=0, concat_axis=1, tiled=True)
    grad_slab = lax.all_to_all(back_part, "frame", split_axis=0, concat_axis=1, tiled=True)
    act_grad = grad_slab.reshape(row_count, channels)
    return out_slab, act_grad


def per_device(clip_feats, out_grad, spatial_weight, temporal_weight):
    slab_frames, tile_rows, width_cells, channels = clip_feats.shape
    row_count = slab_frames * tile_rows * width_cells
    frame_devs = lax.axis_size("frame")
    tile_devs = lax.axis_size("tile")
    grad_scale = 1.0 / math.sqrt(slab_frames * frame_devs * tile_rows * tile_devs * width_cells)
    spatial_back = (
        spatial_weight.reshape(9, channels, channels)
        .transpose(0, 2, 1)
        .reshape(9 * channels, channels)
    )
    temporal_back = (
        temporal_weight.reshape(9, channels, channels)
        .transpose(0, 2, 1)
        .reshape(9 * channels, channels)
    )
    feat_ext = padded_2(clip_feats, (("tile", 1),), 1)
    feat_columns = tile_columns(feat_ext, tile_rows, width_cells, False)
    pre = jnp.dot(feat_columns, spatial_weight, preferred_element_type=jnp.float32)
    act = jax.nn.silu(pre).astype(jnp.bfloat16)
    temporal_reach = 4 * TAP_DILATION
    if temporal_reach <= slab_frames:
        seq_shape = (slab_frames, tile_rows * width_cells, channels)
        act_ext = padded_2(act.reshape(seq_shape), (("frame", 0),), temporal_reach)
        grad_ext = padded_2(out_grad.reshape(seq_shape), (("frame", 0),), temporal_reach)
        act_grad = temporal_taps(grad_ext, temporal_back, slab_frames, True).astype(jnp.bfloat16)
        mixed = temporal_taps(act_ext, temporal_weight, slab_frames, False)
        out_slab = (clip_feats.reshape(-1, channels).astype(jnp.float32) + mixed).astype(
            jnp.bfloat16
        )
        out_slab = out_slab.reshape(clip_feats.shape)
    else:
        out_slab, act_grad = frame_exchange(
            clip_feats, out_grad, act, temporal_weight, temporal_back, temporal_reach
        )
    sig = jax.nn.sigmoid(pre)
    pre_grad = (act_grad.astype(jnp.float32) * (sig * (1.0 + pre * (1.0 - sig)))).astype(
        jnp.bfloat16
    )
    full_term = lax.dot_general(
        feat_columns, pre_grad, (((0,), (0,)), ((), ())), preferred_element_type=jnp.float32
    )
    weight_grad = kernel_scatter(
        full_term,
        (("frame", frame_devs), ("tile", tile_devs)),
        grad_scale,
    )
    grad_ext = padded_2(
        pre_grad.reshape(slab_frames, tile_rows, width_cells, channels), (("tile", 1),), 1
    )
    grad_columns = tile_columns(grad_ext, tile_rows, width_cells, True)
    local_back = jnp.dot(grad_columns, spatial_back, preferred_element_type=jnp.float32)
    input_grad = (out_grad.reshape(row_count, channels).astype(jnp.float32) + local_back).astype(
        jnp.bfloat16
    )
    input_grad = input_grad.reshape(slab_frames, tile_rows, width_cells, channels)
    return (out_slab, input_grad, weight_grad)


def solution(mesh):
    return jax.shard_map(
        per_device,
        mesh=mesh,
        in_specs=(
            P(("clip", "frame"), "tile", None, None),
            P(("clip", "frame"), "tile", None, None),
            P(),
            P(),
        ),
        out_specs=(
            P(("clip", "frame"), "tile", None, None),
            P(("clip", "frame"), "tile", None, None),
            P(("clip", "frame", "tile"), None),
        ),
        check_vma=False,
    )
```

```python
import functools
import math

import jax
import jax.numpy as jnp
from jax import lax
from jax.experimental import pallas as pl
from jax.experimental.pallas import tpu as pltpu
from jax.sharding import PartitionSpec as P

TAP_DILATION = 2


def padded_2(block, sides, width):
    for axis, dim in sides:
        count = lax.axis_size(axis)
        forward = [(i, i + 1) for i in range(count - 1)]
        backward = [(target, source) for source, target in forward]
        low = lax.ppermute(
            lax.slice_in_dim(block, block.shape[dim] - width, None, axis=dim), axis, forward
        )
        high = lax.ppermute(lax.slice_in_dim(block, 0, width, axis=dim), axis, backward)
        block = jnp.concatenate([low, block, high], axis=dim)
    return block


def halving_scatter(term, axes):
    sizes = [size for _, size in axes]
    if any(size & (size - 1) for size in sizes):
        return lax.psum_scatter(term, tuple(name for name, _ in axes), scatter_dimension=0, tiled=True)
    bits = []
    for name, size in axes:
        bits += [(name, size, b) for b in reversed(range(size.bit_length() - 1))]
    groups = 1
    for size in sizes:
        groups *= size
    block = term.shape[0] // groups
    x = term.reshape((2,) * len(bits) + (block,) + term.shape[1:])
    for pos in reversed(range(len(bits))):
        name, size, b = bits[pos]
        mine = (lax.axis_index(name) >> b) & 1
        keep = lax.dynamic_index_in_dim(x, mine, axis=pos, keepdims=False)
        send = lax.dynamic_index_in_dim(x, 1 - mine, axis=pos, keepdims=False)
        pairs = [(i, i ^ (1 << b)) for i in range(size)]
        x = keep + lax.ppermute(send, name, pairs)
    return x


def halving_kernel(groups, narrow, scale, x_ref, o_ref, ordered, *scratch):
    n = len(groups)
    send_sems, recv_sems = scratch[-2], scratch[-1]
    landings = scratch[:n]
    accs = scratch[n : 2 * n - 1]
    packs = scratch[2 * n - 1 : 2 * n - 1 + narrow]
    mesh_ids = pl.DeviceIdType.MESH
    plan = []
    for name, group_bits in groups:
        me = lax.axis_index(name)
        mine = [(me // (1 << b)) % 2 for b in group_bits]
        width = len(group_bits)
        own = 0
        for bit in mine:
            own = own * 2 + bit
        peers = []
        for mask in range(1, 1 << width):
            flips = [(mask >> (width - 1 - j)) % 2 for j in range(width)]
            partner = me
            chunk = 0
            for bit, flip, b in zip(mine, flips, group_bits):
                partner = partner + (1 - 2 * bit) * flip * (1 << b)
                chunk = chunk * 2 + bit + (1 - 2 * bit) * flip
            peers.append((mask, partner, chunk))
        plan.append((name, width, own, peers))
    barrier = pltpu.get_barrier_semaphore()
    contacts = 0
    for name, _, _, peers in plan:
        for _, partner, _ in peers:
            pl.semaphore_signal(barrier, inc=1, device_id={name: partner}, device_id_type=mesh_ids)
            contacts += 1
    blocks = ordered.shape[0]
    rows_in = x_ref.shape[0] // blocks
    width = blocks.bit_length() - 1
    for b in range(blocks):
        turned = int(format(b, "0%db" % width)[::-1], 2)
        ordered[turned] = x_ref[b * rows_in : (b + 1) * rows_in, :].reshape(ordered.shape[1:])
    pl.semaphore_wait(barrier, contacts)
    source = ordered
    count = ordered.shape[0]
    message = 0
    for k, (name, width, own, peers) in enumerate(plan):
        part = count >> width
        copies = []
        for mask, partner, chunk in peers:
            outgoing = source.at[pl.ds(chunk * part, part)]
            if k < narrow:
                packs[k][mask - 1] = outgoing[...].astype(packs[k].dtype)
                outgoing = packs[k].at[mask - 1]
            copy = pltpu.make_async_remote_copy(
                src_ref=outgoing,
                dst_ref=landings[k].at[mask - 1],
                send_sem=send_sems.at[message],
                recv_sem=recv_sems.at[message],
                device_id={name: partner},
                device_id_type=mesh_ids,
            )
            copy.start()
            copies.append(copy)
            message += 1
        total = source[pl.ds(own * part, part)]
        for slot, copy in enumerate(copies):
            copy.wait()
            total = total + landings[k][slot].astype(jnp.float32)
        if k == n - 1:
            o_ref[...] = total[0] * scale
        else:
            accs[k][...] = total
            source = accs[k]
        count = part


def kernel_scatter(term, axes, scale):
    sizes = [size for _, size in axes]
    groups = 1
    for size in sizes:
        groups *= size
    per_block = term.shape[0] * term.shape[1] // groups
    if any(size & (size - 1) for size in sizes) or per_block % 128:
        return halving_scatter(term, axes) * jnp.float32(scale)
    bits = []
    for name, size in axes:
        bits += [(name, b) for b in reversed(range(size.bit_length() - 1))]
    n = len(bits)
    x = term
    steps = list(reversed(bits))
    plan = [(steps[0][0], [steps[0][1]])]
    for name, b in steps[1:]:
        last_name, last_bits = plan[-1]
        if len(plan) > 1 and last_name == name and len(last_bits) == 1:
            last_bits.append(b)
        else:
            plan.append((name, [b]))
    narrow = min(2, len(plan))
    rows = (per_block // 128, 128)
    staged = (groups,) + rows
    counts = [groups]
    for _, group_bits in plan:
        counts.append(counts[-1] >> len(group_bits))
    scratch = [pltpu.VMEM(staged, x.dtype)]
    scratch += [
        pltpu.VMEM(
            ((1 << len(g[1])) - 1, counts[k + 1]) + rows,
            jnp.bfloat16 if k < narrow else jnp.float32,
        )
        for k, g in enumerate(plan)
    ]
    scratch += [pltpu.VMEM((counts[k + 1],) + rows, jnp.float32) for k in range(len(plan) - 1)]
    scratch += [
        pltpu.VMEM(((1 << len(plan[k][1])) - 1, counts[k + 1]) + rows, jnp.bfloat16)
        for k in range(narrow)
    ]
    messages = sum((1 << len(g[1])) - 1 for g in plan)
    scratch += [pltpu.SemaphoreType.DMA((messages,)), pltpu.SemaphoreType.DMA((messages,))]
    out = pl.pallas_call(
        functools.partial(halving_kernel, plan, narrow, scale),
        out_shape=jax.ShapeDtypeStruct(rows, x.dtype),
        in_specs=[pl.BlockSpec(memory_space=pltpu.VMEM)],
        out_specs=pl.BlockSpec(memory_space=pltpu.VMEM),
        scratch_shapes=scratch,
        compiler_params=pltpu.CompilerParams(collective_id=0, has_side_effects=True),
    )(x)
    return out.reshape(term.shape[0] // groups, term.shape[1])


def tile_columns(extended, tile_rows, width_cells, backward_pass):
    padded = jnp.pad(extended, ((0, 0), (0, 0), (1, 1), (0, 0)))
    pieces = []
    for row_shift in range(3):
        for col_shift in range(3):
            row_start = 2 - row_shift if backward_pass else row_shift
            col_start = 2 - col_shift if backward_pass else col_shift
            pieces.append(
                padded[:, row_start : row_start + tile_rows, col_start : col_start + width_cells, :]
            )
    channels = extended.shape[3]
    return jnp.concatenate(pieces, axis=-1).reshape(-1, 9 * channels)


def temporal_taps(padded_seq, weight, frame_count, backward_pass):
    pieces = []
    for temporal_tap_index in range(9):
        first_frame_index = (
            (8 - temporal_tap_index) * TAP_DILATION
            if backward_pass
            else temporal_tap_index * TAP_DILATION
        )
        pieces.append(padded_seq[first_frame_index : first_frame_index + frame_count])
    channels = padded_seq.shape[2]
    columns = jnp.concatenate(pieces, axis=-1).reshape(-1, 9 * channels)
    return jnp.dot(columns, weight, preferred_element_type=jnp.float32)


def frame_exchange(clip_feats, out_grad, act, temporal_weight, temporal_back, temporal_reach):
    slab_frames, tile_rows, width_cells, channels = clip_feats.shape
    row_count = slab_frames * tile_rows * width_cells
    frame_devs = lax.axis_size("frame")
    per_group = tile_rows * width_cells // frame_devs
    grouped = (slab_frames, frame_devs, per_group, channels)
    act_part = lax.all_to_all(
        act.reshape(grouped), "frame", split_axis=1, concat_axis=0, tiled=True
    )
    grad_part = lax.all_to_all(out_grad, "frame", split_axis=1, concat_axis=0, tiled=True)
    feat_part = lax.all_to_all(clip_feats, "frame", split_axis=1, concat_axis=0, tiled=True)
    frame_count = act_part.shape[0]
    item_count = act_part.shape[2]
    act_pad = jnp.pad(
        act_part.reshape(frame_count, item_count, channels),
        ((temporal_reach, temporal_reach), (0, 0), (0, 0)),
    )
    grad_pad = jnp.pad(
        grad_part.reshape(frame_count, item_count, channels),
        ((temporal_reach, temporal_reach), (0, 0), (0, 0)),
    )
    mixed = temporal_taps(act_pad, temporal_weight, frame_count, False)
    out_part = (feat_part.reshape(-1, channels).astype(jnp.float32) + mixed).astype(jnp.bfloat16)
    back_part = temporal_taps(grad_pad, temporal_back, frame_count, True).astype(jnp.bfloat16)
    out_part = out_part.reshape(frame_count, 1, item_count, channels)
    back_part = back_part.reshape(frame_count, 1, item_count, channels)
    out_slab = lax.all_to_all(out_part, "frame", split_axis=0, concat_axis=1, tiled=True)
    grad_slab = lax.all_to_all(back_part, "frame", split_axis=0, concat_axis=1, tiled=True)
    act_grad = grad_slab.reshape(row_count, channels)
    return out_slab, act_grad


def per_device(clip_feats, out_grad, spatial_weight, temporal_weight):
    slab_frames, tile_rows, width_cells, channels = clip_feats.shape
    row_count = slab_frames * tile_rows * width_cells
    frame_devs = lax.axis_size("frame")
    tile_devs = lax.axis_size("tile")
    grad_scale = 1.0 / math.sqrt(slab_frames * frame_devs * tile_rows * tile_devs * width_cells)
    spatial_back = (
        spatial_weight.reshape(9, channels, channels)
        .transpose(0, 2, 1)
        .reshape(9 * channels, channels)
    )
    temporal_back = (
        temporal_weight.reshape(9, channels, channels)
        .transpose(0, 2, 1)
        .reshape(9 * channels, channels)
    )
    feat_ext = padded_2(clip_feats, (("tile", 1),), 1)
    feat_columns = tile_columns(feat_ext, tile_rows, width_cells, False)
    pre = jnp.dot(feat_columns, spatial_weight, preferred_element_type=jnp.float32)
    act = jax.nn.silu(pre).astype(jnp.bfloat16)
    temporal_reach = 4 * TAP_DILATION
    if temporal_reach <= slab_frames:
        seq_shape = (slab_frames, tile_rows * width_cells, channels)
        act_ext = padded_2(act.reshape(seq_shape), (("frame", 0),), temporal_reach)
        grad_ext = padded_2(out_grad.reshape(seq_shape), (("frame", 0),), temporal_reach)
        act_grad = temporal_taps(grad_ext, temporal_back, slab_frames, True).astype(jnp.bfloat16)
        mixed = temporal_taps(act_ext, temporal_weight, slab_frames, False)
        out_slab = (clip_feats.reshape(-1, channels).astype(jnp.float32) + mixed).astype(
            jnp.bfloat16
        )
        out_slab = out_slab.reshape(clip_feats.shape)
    else:
        out_slab, act_grad = frame_exchange(
            clip_feats, out_grad, act, temporal_weight, temporal_back, temporal_reach
        )
    sig = jax.nn.sigmoid(pre)
    pre_grad = (act_grad.astype(jnp.float32) * (sig * (1.0 + pre * (1.0 - sig)))).astype(
        jnp.bfloat16
    )
    full_term = lax.dot_general(
        feat_columns, pre_grad, (((0,), (0,)), ((), ())), preferred_element_type=jnp.float32
    )
    weight_grad = kernel_scatter(
        full_term,
        (("frame", frame_devs), ("tile", tile_devs)),
        grad_scale,
    )
    grad_ext = padded_2(
        pre_grad.reshape(slab_frames, tile_rows, width_cells, channels), (("tile", 1),), 1
    )
    grad_columns = tile_columns(grad_ext, tile_rows, width_cells, True)
    local_back = jnp.dot(grad_columns, spatial_back, preferred_element_type=jnp.float32)
    input_grad = (out_grad.reshape(row_count, channels).astype(jnp.float32) + local_back).astype(
        jnp.bfloat16
    )
    input_grad = input_grad.reshape(slab_frames, tile_rows, width_cells, channels)
    return (out_slab, input_grad, weight_grad)


def solution(mesh):
    return jax.shard_map(
        per_device,
        mesh=mesh,
        in_specs=(
            P(("clip", "frame"), "tile", None, None),
            P(("clip", "frame"), "tile", None, None),
            P(),
            P(),
        ),
        out_specs=(
            P(("clip", "frame"), "tile", None, None),
            P(("clip", "frame"), "tile", None, None),
            P(("clip", "frame", "tile"), None),
        ),
        check_vma=False,
    )
```
